128 devices in a mesh: req: 32 (over z, y, x_lo), exp: 4 (over x_hi, core).
Axes of the slice: x: 4 (x_hi: 2, x_lo: 2; x = x_hi * 2 + x_lo), y: 4, z: 4, core: 2. Of those that a mesh axis runs over, the one named last changes fastest.
Arguments:
- hidden_in: bfloat16 [8192, 2048], P(('req', 'exp')), may hold values from -6 to 6
- query_in: bfloat16 [8192, 2048], P('req', 'exp'), may hold values from -6 to 6
- key_in: bfloat16 [8192, 2048], P('req', 'exp'), may hold values from -6 to 6
- value_in: bfloat16 [8192, 2048], P('req', 'exp'), may hold values from -24 to 24
- query_gain: float32 [128], replicated, may hold values from 0.5 to 2.5
- key_gain: float32 [128], replicated, may hold values from 0.5 to 2.5
- cache_keys: bfloat16 [64, 32, 2048], P('req', None, 'exp'), may hold values from -400 to 400
- cache_values: bfloat16 [64, 32, 2048], P('req', None, 'exp'), may hold values from -24 to 24
- cache_block: int32 [128], replicated, may hold values from -1 to 63, as said below
- request_lengths: int32 [32, 4], P('req'), may hold values from 1 to 128, 256 in all within a row
- out_proj: bfloat16 [2048, 2048], P('exp'), may hold values from -0.125 to 0.125
- norm_gain: float32 [2048], replicated, may hold values from 0.25 to 1.75
- expert_ids: int32 [8192, 8], P(('req', 'exp')), may hold values from 0 to 63, all different within a row; in each aligned block of 64 rows (0 to 63, 64 to 127, ...) at most 10 rows name the same one
- gate_values: float32 [8192, 8], P(('req', 'exp')), may hold values from 0.4 to 1.6
- old_slots: int32 [64], replicated, may hold values from 0 to 63, each once
- new_replicas: int32 [32], replicated, may hold values from 0 to 63
- slot_weights: bfloat16 [64, 3, 2048, 1024], P('req', None, None, 'exp'), may hold values from -0.125 to 0.125
Outputs:
- layer_out: bfloat16 [8192, 2048], P(('req', 'exp'))
- replica_weights: bfloat16 [32, 3, 2048, 1024], P('req', None, None, 'exp')
The draws below stay inside these ranges and needn't reach their ends.
Inputs may be any that keep to these rules, and one draw needn't show every extreme that they name: `cache_block`: each index of req has exactly 2 of its 4 requests with a block; every block serves exactly one request. `expert_ids`: in each aligned block of 64 rows (the rows of one device) no expert is named by more than 10 rows, a bound that some block reaches; the 8 experts of a row differ. `old_slots`: every expert is in exactly one slot. `request_lengths`: the lengths of each index of req sum to 256.
All inputs are finite; a program needn't handle non-finite values.
Results may differ from the reference program's by a relative error of at most 0.025.
Values may be sent and summed in bfloat16 or wider, within the bound.
A program may use at most 128 MiB of HBM per device.

```python
import math
import jax
import jax.numpy as jnp
import numpy as np
from jax import lax

D = 2048
HEADS = 16
HEAD_DIM = 128
FF = 1024
TOPK = 8
REQ_GRP = 4
CACHE_DEV = 2
PRE = 32
TOK_DEV = 64
TOK_GRP = 256
TOKENS = 8192
EXPERTS = 64
MOST = 10
N_REQ = 32
N_EXP = 4


def draw_cache_block(key, part):
    first_key, second_key = jax.random.split(jax.random.fold_in(key, 17))
    orders = jax.vmap(lambda one_key: jax.random.permutation(one_key, REQ_GRP))(jax.random.split(first_key, N_REQ))
    cached = (orders < CACHE_DEV).reshape(-1)
    rank = jnp.cumsum(cached.astype(jnp.int32)) - 1
    blocks = jax.random.permutation(second_key, N_REQ * CACHE_DEV).astype(jnp.int32)
    chosen = jnp.take(blocks, jnp.maximum(rank, 0))
    return jnp.where(cached, chosen, -1).astype(jnp.int32)


def draw_cache_keys(key, part):
    first_key, second_key, third_key, fourth_key = jax.random.split(jax.random.fold_in(key, 29), 4)
    block_count = N_REQ * CACHE_DEV
    block_shape = (block_count, PRE, HEADS * HEAD_DIM)
    background = 1.5 * jax.random.truncated_normal(first_key, -6.0, 6.0, block_shape, jnp.float32)
    strength = jnp.exp(jax.random.uniform(second_key, (block_count, 1, 1), jnp.float32, math.log(20.0), math.log(60.0)))
    leading = strength * jax.random.truncated_normal(third_key, -4.0, 4.0, (block_count, 1, HEADS * HEAD_DIM), jnp.float32)
    nudging = 1.5 * jax.random.truncated_normal(fourth_key, -4.0, 4.0, (block_count, 1, HEADS * HEAD_DIM), jnp.float32)
    row_index = jnp.arange(PRE, dtype=jnp.int32)[None, :, None]
    planted = jnp.where(row_index == 0, leading, jnp.where(row_index == 1, leading + nudging, background))
    return jnp.clip(planted, -400.0, 400.0).astype(jnp.bfloat16)


def with_ends(drawn, rng, least, high):
    dims = drawn.shape
    spot = [jax.random.randint(jax.random.fold_in(rng, axis), (), 0, dims[axis]) for axis in range(len(dims))]
    drawn = drawn.at[tuple(spot)].set(least)
    longest = dims.index(max(dims))
    spot[longest] = (spot[longest] + 1) % dims[longest]
    return drawn.at[tuple(spot)].set(high)


def shard_levels(key, shape, cuts, low, largest):
    loudness = 1.0
    for dim, blocks in cuts:
        heights = jax.random.uniform(jax.random.fold_in(jax.random.fold_in(key, 6), dim), (blocks,), jnp.float32, low / len(cuts), largest / len(cuts))
        loudness = loudness * jnp.repeat(jnp.exp(heights), shape[dim] // blocks).reshape((-1,) + (1,) * (len(shape) - 1 - dim))
    return loudness


def profile(number_of, total, bound, slope):
    loads = [(1 << 20) // math.isqrt(standing ** slope) + 1 for standing in range(2, number_of + 1)]
    surplus, given = total - bound - (number_of - 1), [1] * (number_of - 1)
    while surplus > 0:
        candidates = [i for i in range(number_of - 1) if given[i] < bound]
        mass, budget = sum([loads[i] for i in candidates]), surplus
        for i in candidates:
            more = min(bound - given[i], max(1, budget * loads[i] // mass), surplus)
            given[i] = given[i] + more
            surplus = surplus - more
    return np.array([bound] + given)


def ragged_sizes(rng, amount, total, limit, skew):
    if amount == 2:
        one = jax.random.randint(rng, (), max(1, total - limit), min(limit, total - 1) + 1)
        return jnp.stack([one, total - one])
    sizes = jnp.asarray(profile(amount, total, limit, skew), jnp.int32)
    couples = (amount - 1) // 2
    giver, receiver = sizes[1:1 + 2 * couples:2], sizes[2:2 + 2 * couples:2]
    margin = jnp.minimum(giver - 1, limit - receiver)
    moved = jax.random.randint(jax.random.fold_in(rng, 1), (couples,), 0, 1 << 20) % (margin + 1)
    sizes = sizes.at[1:1 + 2 * couples:2].set(giver - moved).at[2:2 + 2 * couples:2].set(receiver + moved)
    return sizes[jax.random.permutation(jax.random.fold_in(rng, 2), amount)]


def assign_block(key, own, number, rows, amount, top, limit, slope):
    ranking = jax.random.permutation(key, amount)
    heavy_load, usual = load_shares(amount, rows * top, limit, slope, True), load_shares(amount, rows * top, limit, slope, False)
    places = jnp.arange(amount)

    def named(sizes, offset_by):
        used = int((sizes > 0).sum())
        fixed = max(1, used // 4)
        moved = fixed + (places - fixed + offset_by * (used - fixed)) % max(1, amount - fixed)
        return jnp.zeros((amount,), jnp.int32).at[ranking[jnp.where(places < fixed, places, moved)]].set(jnp.asarray(sizes, jnp.int32))

    sizes = jnp.where(number % 4 == 0, named(heavy_load, number // 4), named(usual, number - number // 4 - 1))
    mixed = jax.random.permutation(jax.random.fold_in(own, 3), amount)
    giver, receiver = mixed[0:amount // 2 * 2:2], mixed[1:amount // 2 * 2:2]
    room = jnp.minimum(sizes[giver] - 1, limit - sizes[receiver]) // 2
    room = jnp.where((giver == ranking[0]) | (receiver == ranking[0]) | (sizes[receiver] == 0), 0, jnp.maximum(room, 0))
    moved = jax.random.randint(jax.random.fold_in(own, 4), (amount // 2,), 0, 1 << 20) % (room + 1)
    sizes = sizes.at[giver].add(-moved).at[receiver].add(moved)
    members = jnp.searchsorted(jnp.cumsum(sizes), jnp.arange(rows * top), side="right").astype(jnp.int32)
    listing = members.reshape(top, rows).T
    listing = listing[jax.random.permutation(jax.random.fold_in(own, 1), rows)]
    offset_by = jax.random.randint(jax.random.fold_in(own, 2), (rows, 1), 0, top)
    return jnp.take_along_axis(listing, (jnp.arange(top)[None, :] + offset_by) % top, axis=1)


def load_shares(amount, total, most, lean, full):
    portions = [(1 << 20) // math.isqrt(grade ** lean) + 1 for grade in range(1, amount + 1)]
    largest = most if full else min(most, max(-(-total // amount), total * portions[0] // sum(portions)))
    least = 1 if total - largest >= amount - 1 else 0
    given, spare = [largest] + [least] * (amount - 1), total - largest - least * (amount - 1)
    while spare > 0:
        movable = [i for i in range(1, amount) if given[i] < largest] or [i for i in range(1, amount) if given[i] < most]
        mass, left = sum([portions[i] for i in movable]), spare
        for i in movable:
            extra = min(most - given[i], max(1, left * portions[i] // mass), spare)
            given[i] = given[i] + extra
            spare = spare - extra
    return np.array(given)


def gaussian(rng, extent, scale, bound, shards=(), kind=jnp.bfloat16):
    result = scale * jax.random.normal(rng, extent, jnp.float32)
    if shards:
        result = result * shard_levels(rng, extent, shards, -0.22, 0.18)
    return jnp.clip(result, -bound, bound).astype(kind)


def setup_inputs(seed: int = 0) -> dict:
    key_of = jax.random.split(jax.random.key(seed), 18)
    hidden_in = gaussian(key_of[0], (TOKENS, D), 1.0, 6.0, ((0, 128),))
    query_in = gaussian(key_of[1], (TOKENS, HEADS * HEAD_DIM), 1.0, 6.0, ((0, 32), (1, 4)))
    key_in = gaussian(key_of[2], (TOKENS, HEADS * HEAD_DIM), 1.0, 6.0, ((0, 32), (1, 4)))
    value_in = gaussian(key_of[3], (TOKENS, HEADS * HEAD_DIM), 4.0, 24.0, ((0, 32), (1, 4)))
    query_gain = jnp.clip(jnp.exp(jax.random.uniform(key_of[4], (HEAD_DIM,), jnp.float32, math.log(0.5), math.log(2.5))), 0.5, 2.5)
    key_gain = jnp.clip(jnp.exp(jax.random.uniform(key_of[5], (HEAD_DIM,), jnp.float32, math.log(0.5), math.log(2.5))), 0.5, 2.5)
    cache_keys = draw_cache_keys(jax.random.fold_in(key_of[17], 71), 0)
    cache_values = gaussian(key_of[7], (N_REQ * CACHE_DEV, PRE, HEADS * HEAD_DIM), 4.0, 24.0, ((0, 32), (2, 4)))
    cache_block = draw_cache_block(jax.random.fold_in(key_of[17], 71), 0)
    request_lengths = jax.vmap(lambda own: ragged_sizes(own, REQ_GRP, TOK_GRP, TOK_GRP // 2, 2))(jax.random.split(key_of[9], N_REQ)).reshape((N_REQ, REQ_GRP)).astype(jnp.int32)
    out_proj = gaussian(key_of[10], (HEADS * HEAD_DIM, D), (HEADS * HEAD_DIM) ** -0.5, 0.125, ((0, 4),))
    norm_gain = jnp.clip(1.0 + 0.15 * jax.random.normal(key_of[11], (D,), jnp.float32), 0.25, 1.75)
    expert_ids_keys = jax.random.split(jax.random.fold_in(key_of[12], 1), TOKENS // TOK_DEV)
    expert_ids_turns = jax.random.permutation(jax.random.fold_in(key_of[12], 3), TOKENS // TOK_DEV)
    expert_ids = jax.vmap(lambda own, number: assign_block(jax.random.fold_in(key_of[12], 2), own, number, TOK_DEV, EXPERTS, TOPK, MOST, 1))(expert_ids_keys, expert_ids_turns).reshape((TOKENS, TOPK))
    gate_values = jnp.clip(0.4 + 1.2 * jax.random.uniform(key_of[13], (TOKENS, TOPK), jnp.float32) ** shard_levels(key_of[13], (TOKENS, TOPK), ((0, 128),), -0.2, 0.2), 0.4, 1.6)
    old_slots = jax.random.permutation(key_of[14], EXPERTS).astype(jnp.int32)
    new_replicas = with_ends(jax.random.randint(key_of[15], (N_REQ,), 0, EXPERTS), jax.random.fold_in(key_of[15], 1), 0, EXPERTS - 1).astype(jnp.int32)
    slot_weights = gaussian(key_of[16], (EXPERTS, 3, D, FF), D ** -0.5, 0.125, ((0, 32), (3, 4)))
    return dict(hidden_in=hidden_in, query_in=query_in, key_in=key_in, value_in=value_in, query_gain=query_gain, key_gain=key_gain, cache_keys=cache_keys, cache_values=cache_values, cache_block=cache_block, request_lengths=request_lengths, out_proj=out_proj, norm_gain=norm_gain, expert_ids=expert_ids, gate_values=gate_values, old_slots=old_slots, new_replicas=new_replicas, slot_weights=slot_weights)


def prepare(values, gain, position):
    vector = values.astype(jnp.float32)
    scaled = vector * lax.rsqrt(lax.optimization_barrier(jnp.mean(vector * vector, axis=-1, keepdims=True)) + 1e-06) * gain
    half_size = scaled.shape[-1] // 2
    frequency = 10000.0 ** (-(jnp.arange(half_size, dtype=jnp.float32) * 2.0 / scaled.shape[-1]))
    angles = position[:, None] * frequency[None, :]
    cosine = jnp.cos(angles)[:, None, :]
    sine_part = jnp.sin(angles)[:, None, :]
    lower_half = scaled[..., :half_size]
    upper_half = scaled[..., half_size:]
    rotated = jnp.concatenate([lower_half * cosine - upper_half * sine_part, upper_half * cosine + lower_half * sine_part], axis=-1)
    return rotated.astype(jnp.bfloat16)

def run_expert(in_rows, weights):
    gate_act = jnp.dot(in_rows, weights[0], preferred_element_type=jnp.float32)
    up_act = jnp.dot(in_rows, weights[1], preferred_element_type=jnp.float32)
    hidden = (jax.nn.silu(gate_act) * up_act).astype(jnp.bfloat16)
    row_count = in_rows.shape[0]
    quarter = FF // N_EXP
    blocks = hidden.reshape(row_count, N_EXP, quarter).astype(jnp.float32)
    down_rows = weights[2].reshape(D, N_EXP, quarter).astype(jnp.float32)
    parts = jnp.einsum('cqf,dqf->qcd', blocks, down_rows)
    return lax.optimization_barrier(jnp.sum(parts.astype(jnp.bfloat16).astype(jnp.float32), axis=0))

def reference(hidden_in, query_in, key_in, value_in, query_gain, key_gain, cache_keys, cache_values, cache_block, request_lengths, out_proj, norm_gain, expert_ids, gate_values, old_slots, new_replicas, slot_weights):
    scale = 1.0 / math.sqrt(HEAD_DIM)
    query_groups = query_in.reshape(N_REQ, TOK_GRP, HEADS, HEAD_DIM)
    key_groups = key_in.reshape(N_REQ, TOK_GRP, HEADS, HEAD_DIM)
    value_groups = value_in.reshape(N_REQ, TOK_GRP, HEADS, HEAD_DIM)
    block_groups = cache_block.reshape(N_REQ, REQ_GRP)

    def attend_group(inputs):
        query_here, key_here, value_here, lengths, blocks = inputs
        req_ends = jnp.cumsum(lengths).astype(jnp.int32)
        starts = (req_ends - lengths).astype(jnp.int32)
        places = jnp.arange(TOK_GRP, dtype=jnp.int32)
        member = (places[:, None] >= starts[None, :]) & (places[:, None] < req_ends[None, :])
        request_idx = jnp.arange(REQ_GRP, dtype=jnp.int32)
        segment = lax.optimization_barrier(jnp.sum(jnp.where(member, request_idx[None, :], 0), axis=1)).astype(jnp.int32)
        offset = places - lax.optimization_barrier(jnp.sum(jnp.where(member, starts[None, :], 0), axis=1)).astype(jnp.int32)
        has_cache = blocks >= 0
        token_cached = lax.optimization_barrier(jnp.sum(jnp.where(member & has_cache[None, :], 1, 0), axis=1)) > 0
        position = (offset + jnp.where(token_cached, PRE, 0)).astype(jnp.float32)
        query_n = prepare(query_here, query_gain, position)
        key_n = prepare(key_here, key_gain, position)
        safe_blocks = jnp.maximum(blocks, 0).astype(jnp.int32)
        far_keys = jnp.take(cache_keys, safe_blocks, axis=0).reshape(REQ_GRP * PRE, HEADS, HEAD_DIM)
        far_values = jnp.take(cache_values, safe_blocks, axis=0).reshape(REQ_GRP * PRE, HEADS, HEAD_DIM)
        keyset = jnp.concatenate([key_n, far_keys], axis=0)
        valueset = jnp.concatenate([value_here, far_values], axis=0)
        key_request = jnp.concatenate([segment, jnp.repeat(request_idx, PRE)])
        key_live = jnp.concatenate([jnp.ones((TOK_GRP,), dtype=bool), jnp.repeat(has_cache, PRE)])
        allowed = (segment[:, None] == key_request[None, :]) & key_live[None, :]
        scores = jnp.einsum('qhd,khd->hqk', query_n.astype(jnp.float32), keyset.astype(jnp.float32)) * scale
        scores = jnp.where(allowed[None], scores, -1e+30)
        peak = lax.optimization_barrier(jnp.max(scores, axis=-1, keepdims=True))
        expos = jnp.exp(scores - peak)
        weights = (expos / lax.optimization_barrier(jnp.sum(expos, axis=-1, keepdims=True))).astype(jnp.bfloat16)
        attended = jnp.einsum('hqk,khd->qhd', weights.astype(jnp.float32), valueset.astype(jnp.float32))
        return attended.astype(jnp.bfloat16).reshape(TOK_GRP, HEADS * HEAD_DIM)
    attended = lax.map(attend_group, (query_groups, key_groups, value_groups, request_lengths, block_groups))
    attended = attended.reshape(TOKENS, HEADS * HEAD_DIM)
    attn_out = jnp.dot(attended, out_proj, preferred_element_type=jnp.float32)
    residual = hidden_in.astype(jnp.float32) + attn_out
    normed = (residual * lax.rsqrt(lax.optimization_barrier(jnp.mean(residual * residual, axis=-1, keepdims=True)) + 1e-06) * norm_gain).astype(jnp.bfloat16)
    flat_ids = expert_ids.reshape(-1).astype(jnp.int32)
    order = jnp.argsort(flat_ids, stable=True).astype(jnp.int32)
    expert_range = jnp.arange(EXPERTS, dtype=jnp.int32)
    counts = lax.optimization_barrier(jnp.sum((flat_ids[None, :] == expert_range[:, None]).astype(jnp.int32), axis=1)).astype(jnp.int32)
    firsts = (jnp.cumsum(counts) - counts).astype(jnp.int32)
    capacity_all = TOKENS // TOK_DEV * MOST
    token_sorted = jnp.concatenate([(order // TOPK).astype(jnp.int32), jnp.zeros((capacity_all,), jnp.int32)])
    gate_sorted = jnp.concatenate([jnp.take(gate_values.reshape(-1), order), jnp.zeros((capacity_all,), gate_values.dtype)])
    slot_of = jnp.argsort(old_slots).astype(jnp.int32)

    def expert_step(total, expert):
        begin = firsts[expert]
        picked = lax.dynamic_slice_in_dim(token_sorted, begin, capacity_all)
        gates_here = lax.dynamic_slice_in_dim(gate_sorted, begin, capacity_all)
        live = jnp.arange(capacity_all, dtype=jnp.int32) < counts[expert]
        weights = lax.dynamic_index_in_dim(slot_weights, slot_of[expert], 0, keepdims=False)
        output = run_expert(jnp.take(normed, picked, axis=0), weights)
        factor = jnp.where(live, gates_here, 0.0)
        return (total.at[picked].add(output * factor[:, None]), None)
    mixture, _ = lax.scan(expert_step, jnp.zeros((TOKENS, D), jnp.float32), expert_range)
    layer_out = (residual + mixture).astype(jnp.bfloat16)
    replica_weights = jnp.take(slot_weights, jnp.take(slot_of, new_replicas), axis=0)
    return (layer_out, replica_weights)
```

```python
import math

import jax
import jax.numpy as jnp
from jax import lax
from jax.sharding import PartitionSpec as P


def prepare(values, gain, position):
    vector = values.astype(jnp.float32)
    scaled = vector * lax.rsqrt(jnp.mean(vector * vector, axis=-1, keepdims=True) + 1e-06) * gain
    half_size = scaled.shape[-1] // 2
    frequency = 10000.0 ** (-(jnp.arange(half_size, dtype=jnp.float32) * 2.0 / scaled.shape[-1]))
    angles = position[:, None] * frequency[None, :]
    cosine = jnp.cos(angles)[:, None, :]
    sine_part = jnp.sin(angles)[:, None, :]
    lower_half = scaled[..., :half_size]
    upper_half = scaled[..., half_size:]
    rotated = jnp.concatenate(
        [
            lower_half * cosine - upper_half * sine_part,
            upper_half * cosine + lower_half * sine_part,
        ],
        axis=-1,
    )
    return rotated.astype(jnp.bfloat16)


def compact(block_rows, slots_wanted):
    live = block_rows >= 0
    ranks = jnp.cumsum(live.astype(jnp.int32), axis=1) - 1
    request_idx = jnp.arange(block_rows.shape[1], dtype=jnp.int32)[None, :]
    chosen_blocks = []
    chosen_requests = []
    for slot_num in range(slots_wanted):
        picked = live & (ranks == slot_num)
        chosen_blocks.append(jnp.sum(jnp.where(picked, block_rows, 0), axis=1))
        chosen_requests.append(jnp.sum(jnp.where(picked, request_idx, 0), axis=1))
    return (jnp.stack(chosen_blocks, axis=1), jnp.stack(chosen_requests, axis=1))


def run_slots(inbox, slot_weights, capacity):
    sources = inbox.shape[0]
    model_width = inbox.shape[2]
    slot_count = slot_weights.shape[0]
    grouped = inbox.reshape(sources, slot_count, capacity, model_width)
    results = []
    for slot_num in range(slot_count):
        in_rows = grouped[:, slot_num].reshape(sources * capacity, model_width)
        gate_act = jnp.dot(in_rows, slot_weights[slot_num, 0], preferred_element_type=jnp.float32)
        up_act = jnp.dot(in_rows, slot_weights[slot_num, 1], preferred_element_type=jnp.float32)
        hidden = (jax.nn.silu(gate_act) * up_act).astype(jnp.bfloat16)
        partial_value = lax.dot_general(
            hidden,
            slot_weights[slot_num, 2],
            (((1,), (1,)), ((), ())),
            preferred_element_type=jnp.float32,
        )
        results.append(partial_value.reshape(sources, capacity, model_width))
    return jnp.stack(results, axis=1).reshape(sources, slot_count * capacity, model_width)


def body(
    hidden_in,
    query_in,
    key_in,
    value_in,
    query_gain,
    key_gain,
    cache_keys,
    cache_values,
    cache_block,
    request_lengths,
    out_proj,
    norm_gain,
    expert_ids,
    gate_values,
    old_slots,
    new_replicas,
    slot_weights,
):
    req_count = lax.axis_size("req")
    exp_count = lax.axis_size("exp")
    group_idx = lax.axis_index("req")
    tok_grp, width_q = query_in.shape
    tok_dev, model_width = hidden_in.shape
    head_size = query_gain.shape[0]
    head_count = width_q // head_size
    cache_dev = cache_keys.shape[0]
    pre_len = cache_keys.shape[1]
    req_grp = request_lengths.shape[1]
    lengths = request_lengths[0]
    req_ends = jnp.cumsum(lengths)
    starts = req_ends - lengths
    places = jnp.arange(tok_grp, dtype=jnp.int32)
    member = (places[:, None] >= starts[None, :]) & (places[:, None] < req_ends[None, :])
    request_idx = jnp.arange(req_grp, dtype=jnp.int32)
    segment = jnp.sum(jnp.where(member, request_idx[None, :], 0), axis=1)
    offset = places - jnp.sum(jnp.where(member, starts[None, :], 0), axis=1)
    block_rows = cache_block.reshape(req_count, req_grp)
    my_blocks = lax.dynamic_index_in_dim(block_rows, group_idx, 0, keepdims=False)
    has_cache = my_blocks >= 0
    token_cached = jnp.sum(jnp.where(member & has_cache[None, :], 1, 0), axis=1) > 0
    position = (offset + jnp.where(token_cached, pre_len, 0)).astype(jnp.float32)
    need_blocks, need_requests = compact(block_rows, cache_dev)
    my_requests = lax.dynamic_index_in_dim(need_requests, group_idx, 0, keepdims=False)
    key_width = cache_keys.shape[2]
    rows_per = pre_len // req_count
    both = jnp.concatenate([cache_keys, cache_values], axis=-1)
    both = both.reshape(cache_dev, req_count, rows_per, 2 * key_width).transpose(1, 0, 2, 3)
    spread = lax.all_to_all(both, "req", split_axis=0, concat_axis=0, tiled=True)
    spread = spread.reshape(req_count * cache_dev, rows_per, 2 * key_width)
    picked = jnp.take(spread, need_blocks.reshape(-1), axis=0)
    picked = picked.reshape(req_count, cache_dev, rows_per, 2 * key_width)
    gathered = lax.all_to_all(picked, "req", split_axis=0, concat_axis=0, tiled=True)
    gathered = gathered.transpose(1, 0, 2, 3).reshape(cache_dev, pre_len, 2 * key_width)
    far_keys = gathered[..., :key_width]
    far_values = gathered[..., key_width:]
    query_n = prepare(query_in.reshape(tok_grp, head_count, head_size), query_gain, position)
    key_n = prepare(key_in.reshape(tok_grp, head_count, head_size), key_gain, position)
    keyset = jnp.concatenate(
        [key_n, far_keys.reshape(cache_dev * pre_len, head_count, head_size)], axis=0
    )
    valueset = jnp.concatenate(
        [
            value_in.reshape(tok_grp, head_count, head_size),
            far_values.reshape(cache_dev * pre_len, head_count, head_size),
        ],
        axis=0,
    )
    key_request = jnp.concatenate([segment, jnp.repeat(my_requests, pre_len)])
    allowed = segment[:, None] == key_request[None, :]
    scores = jnp.einsum("qhd,khd->hqk", query_n, keyset, preferred_element_type=jnp.float32) * (
        1.0 / math.sqrt(head_size)
    )
    scores = jnp.where(allowed[None], scores, -1e30)
    peak = jnp.max(scores, axis=-1, keepdims=True)
    expos = jnp.exp(scores - peak)
    weights = (expos / jnp.sum(expos, axis=-1, keepdims=True)).astype(jnp.bfloat16)
    attended = jnp.einsum("hqk,khd->qhd", weights, valueset, preferred_element_type=jnp.float32)
    attended = attended.astype(jnp.bfloat16).reshape(tok_grp, width_q)
    attn_out = lax.psum_scatter(
        jnp.dot(attended, out_proj, preferred_element_type=jnp.float32),
        "exp",
        scatter_dimension=0,
        tiled=True,
    )
    residual = hidden_in.astype(jnp.float32) + attn_out
    normed = (
        residual
        * lax.rsqrt(jnp.mean(residual * residual, axis=-1, keepdims=True) + 1e-06)
        * norm_gain
    ).astype(jnp.bfloat16)
    topk_count = expert_ids.shape[1]
    slot_total = old_slots.shape[0]
    slots_here = slot_weights.shape[0]
    capacity = max(2, tok_dev * topk_count * 5 // (4 * slot_total))
    slot_range = jnp.arange(slot_total, dtype=jnp.int32)
    slot_of = jnp.sum(
        jnp.where(old_slots[None, :] == slot_range[:, None], slot_range[None, :], 0), axis=1
    )
    flat_ids = expert_ids.reshape(-1)
    onehot = flat_ids[:, None] == slot_range[None, :]
    row_slot = jnp.sum(jnp.where(onehot, slot_of[None, :], 0), axis=1)
    before = jnp.cumsum(onehot.astype(jnp.int32), axis=0) - onehot.astype(jnp.int32)
    row_rank = jnp.sum(jnp.where(onehot, before, 0), axis=1)
    target = row_slot * capacity + row_rank
    send_rows = jnp.repeat(normed, topk_count, axis=0)
    outbox = jnp.zeros((slot_total * capacity, model_width), jnp.bfloat16).at[target].set(send_rows)
    outbox = outbox.reshape(req_count, slots_here * capacity, model_width)
    copies = jnp.broadcast_to(
        outbox[:, None], (req_count, exp_count, slots_here * capacity, model_width)
    )
    copies = copies.reshape(req_count * exp_count, slots_here * capacity, model_width)
    inbox = lax.all_to_all(copies, ("req", "exp"), split_axis=0, concat_axis=0, tiled=True)
    partial_value = run_slots(inbox, slot_weights, capacity).astype(jnp.bfloat16)
    returned = lax.all_to_all(
        partial_value, ("req", "exp"), split_axis=0, concat_axis=0, tiled=True
    )
    result = jnp.sum(
        returned.astype(jnp.float32).reshape(
            req_count, exp_count, slots_here * capacity, model_width
        ),
        axis=1,
    )
    result_rows = jnp.take(result.reshape(slot_total * capacity, model_width), target, axis=0)
    mixture = jnp.sum(
        result_rows.reshape(tok_dev, topk_count, model_width) * gate_values[:, :, None], axis=1
    )
    layer_out = (residual + mixture).astype(jnp.bfloat16)
    spread_slots = lax.all_to_all(slot_weights, "req", split_axis=2, concat_axis=0, tiled=True)
    replica_onehot = new_replicas[:, None] == slot_range[None, :]
    source_slot = jnp.sum(jnp.where(replica_onehot, slot_of[None, :], 0), axis=1)
    chosen_pieces = jnp.take(spread_slots, source_slot, axis=0)
    replica_weights = lax.all_to_all(chosen_pieces, "req", split_axis=0, concat_axis=2, tiled=True)
    return (layer_out, replica_weights)


def solution(mesh):
    in_specs = (
        P(("req", "exp"), None),
        P("req", "exp"),
        P("req", "exp"),
        P("req", "exp"),
        P(),
        P(),
        P("req", None, "exp"),
        P("req", None, "exp"),
        P(),
        P("req", None),
        P("exp", None),
        P(),
        P(("req", "exp"), None),
        P(("req", "exp"), None),
        P(),
        P(),
        P("req", None, None, "exp"),
    )
    out_specs = (P(("req", "exp"), None), P("req", None, None, "exp"))
    return jax.shard_map(body, mesh=mesh, in_specs=in_specs, out_specs=out_specs, check_vma=False)
```

```python
import math

import jax
import jax.numpy as jnp
from jax import lax
from jax.sharding import PartitionSpec as P


def prepare(values, gain, position):
    vector = values.astype(jnp.float32)
    scaled = vector * lax.rsqrt(jnp.mean(vector * vector, axis=-1, keepdims=True) + 1e-06) * gain
    half_size = scaled.shape[-1] // 2
    frequency = 10000.0 ** (-(jnp.arange(half_size, dtype=jnp.float32) * 2.0 / scaled.shape[-1]))
    angles = position[:, None] * frequency[None, :]
    cosine = jnp.cos(angles)[:, None, :]
    sine_part = jnp.sin(angles)[:, None, :]
    lower_half = scaled[..., :half_size]
    upper_half = scaled[..., half_size:]
    rotated = jnp.concatenate(
        [
            lower_half * cosine - upper_half * sine_part,
            upper_half * cosine + lower_half * sine_part,
        ],
        axis=-1,
    )
    return rotated.astype(jnp.bfloat16)


def compact(block_rows, slots_wanted):
    live = block_rows >= 0
    ranks = jnp.cumsum(live.astype(jnp.int32), axis=1) - 1
    request_idx = jnp.arange(block_rows.shape[1], dtype=jnp.int32)[None, :]
    chosen_blocks = []
    chosen_requests = []
    for slot_num in range(slots_wanted):
        picked = live & (ranks == slot_num)
        chosen_blocks.append(jnp.sum(jnp.where(picked, block_rows, 0), axis=1))
        chosen_requests.append(jnp.sum(jnp.where(picked, request_idx, 0), axis=1))
    return (jnp.stack(chosen_blocks, axis=1), jnp.stack(chosen_requests, axis=1))


def body(
    hidden_in,
    query_in,
    key_in,
    value_in,
    query_gain,
    key_gain,
    cache_keys,
    cache_values,
    cache_block,
    request_lengths,
    out_proj,
    norm_gain,
    expert_ids,
    gate_values,
    old_slots,
    new_replicas,
    slot_weights,
):
    req_count = lax.axis_size("req")
    exp_count = lax.axis_size("exp")
    group_idx = lax.axis_index("req")
    tok_grp, width_q = query_in.shape
    tok_dev, model_width = hidden_in.shape
    head_size = query_gain.shape[0]
    head_count = width_q // head_size
    cache_dev = cache_keys.shape[0]
    pre_len = cache_keys.shape[1]
    req_grp = request_lengths.shape[1]
    lengths = request_lengths[0]
    req_ends = jnp.cumsum(lengths)
    starts = req_ends - lengths
    places = jnp.arange(tok_grp, dtype=jnp.int32)
    member = (places[:, None] >= starts[None, :]) & (places[:, None] < req_ends[None, :])
    request_idx = jnp.arange(req_grp, dtype=jnp.int32)
    segment = jnp.sum(jnp.where(member, request_idx[None, :], 0), axis=1)
    offset = places - jnp.sum(jnp.where(member, starts[None, :], 0), axis=1)
    block_rows = cache_block.reshape(req_count, req_grp)
    my_blocks = lax.dynamic_index_in_dim(block_rows, group_idx, 0, keepdims=False)
    has_cache = my_blocks >= 0
    token_cached = jnp.sum(jnp.where(member & has_cache[None, :], 1, 0), axis=1) > 0
    position = (offset + jnp.where(token_cached, pre_len, 0)).astype(jnp.float32)
    need_blocks, need_requests = compact(block_rows, cache_dev)
    my_requests = lax.dynamic_index_in_dim(need_requests, group_idx, 0, keepdims=False)
    key_width = cache_keys.shape[2]
    rows_per = pre_len // req_count
    both = jnp.concatenate([cache_keys, cache_values], axis=-1)
    both = both.reshape(cache_dev, req_count, rows_per, 2 * key_width).transpose(1, 0, 2, 3)
    spread = lax.all_to_all(both, "req", split_axis=0, concat_axis=0, tiled=True)
    spread = spread.reshape(req_count * cache_dev, rows_per, 2 * key_width)
    picked = jnp.take(spread, need_blocks.reshape(-1), axis=0)
    picked = picked.reshape(req_count, cache_dev, rows_per, 2 * key_width)
    gathered = lax.all_to_all(picked, "req", split_axis=0, concat_axis=0, tiled=True)
    gathered = gathered.transpose(1, 0, 2, 3).reshape(cache_dev, pre_len, 2 * key_width)
    far_keys = gathered[..., :key_width]
    far_values = gathered[..., key_width:]
    query_n = prepare(query_in.reshape(tok_grp, head_count, head_size), query_gain, position)
    key_n = prepare(key_in.reshape(tok_grp, head_count, head_size), key_gain, position)
    keyset = jnp.concatenate(
        [key_n, far_keys.reshape(cache_dev * pre_len, head_count, head_size)], axis=0
    )
    valueset = jnp.concatenate(
        [
            value_in.reshape(tok_grp, head_count, head_size),
            far_values.reshape(cache_dev * pre_len, head_count, head_size),
        ],
        axis=0,
    )
    key_request = jnp.concatenate([segment, jnp.repeat(my_requests, pre_len)])
    allowed = segment[:, None] == key_request[None, :]
    scores = jnp.einsum("qhd,khd->hqk", query_n, keyset, preferred_element_type=jnp.float32) * (
        1.0 / math.sqrt(head_size)
    )
    scores = jnp.where(allowed[None], scores, -1e30)
    peak = jnp.max(scores, axis=-1, keepdims=True)
    expos = jnp.exp(scores - peak)
    weights = (expos / jnp.sum(expos, axis=-1, keepdims=True)).astype(jnp.bfloat16)
    attended = jnp.einsum("hqk,khd->qhd", weights, valueset, preferred_element_type=jnp.float32)
    attended = attended.astype(jnp.bfloat16).reshape(tok_grp, width_q)
    attn_out = lax.psum_scatter(
        jnp.dot(attended, out_proj, preferred_element_type=jnp.float32),
        "exp",
        scatter_dimension=0,
        tiled=True,
    )
    residual = hidden_in.astype(jnp.float32) + attn_out
    normed = (
        residual
        * lax.rsqrt(jnp.mean(residual * residual, axis=-1, keepdims=True) + 1e-06)
        * norm_gain
    ).astype(jnp.bfloat16)
    topk_count = expert_ids.shape[1]
    slot_total = old_slots.shape[0]
    slots_here = slot_weights.shape[0]
    capacity = max(2, tok_dev * topk_count * 5 // (4 * slot_total))
    slot_range = jnp.arange(slot_total, dtype=jnp.int32)
    slot_of = jnp.sum(
        jnp.where(old_slots[None, :] == slot_range[:, None], slot_range[None, :], 0), axis=1
    )
    flat_ids = expert_ids.reshape(-1)
    onehot = flat_ids[:, None] == slot_range[None, :]
    row_slot = jnp.sum(jnp.where(onehot, slot_of[None, :], 0), axis=1)
    before = jnp.cumsum(onehot.astype(jnp.int32), axis=0) - onehot.astype(jnp.int32)
    row_rank = jnp.sum(jnp.where(onehot, before, 0), axis=1)
    target = row_slot * capacity + row_rank
    exp_idx = lax.axis_index("exp")
    pair_bit = exp_idx % 2
    pair_count = exp_count // 2
    own_part = lax.dynamic_index_in_dim(slot_weights, pair_bit, 0, keepdims=False)
    give_part = lax.dynamic_index_in_dim(slot_weights, 1 - pair_bit, 0, keepdims=False)
    swap = [(e, e ^ 1) for e in range(exp_count)]
    got_part = lax.ppermute(give_part, "exp", perm=swap)
    send_rows = jnp.repeat(normed, topk_count, axis=0)
    outbox = jnp.zeros((slot_total * capacity, model_width), jnp.bfloat16).at[target].set(send_rows)
    outbox = outbox.reshape(req_count, 1, slots_here, capacity, model_width)
    copies = jnp.broadcast_to(
        outbox, (req_count, pair_count, slots_here, capacity, model_width)
    )
    copies = copies.reshape(req_count * exp_count, capacity, model_width)
    inbox = lax.all_to_all(copies, ("req", "exp"), split_axis=0, concat_axis=0, tiled=True)
    in_rows = inbox.reshape(req_count * exp_count * capacity, model_width)
    halves = []
    for part in (own_part, got_part):
        gate_act = jnp.dot(in_rows, part[0], preferred_element_type=jnp.float32)
        up_act = jnp.dot(in_rows, part[1], preferred_element_type=jnp.float32)
        hidden = (jax.nn.silu(gate_act) * up_act).astype(jnp.bfloat16)
        piece = lax.dot_general(
            hidden, part[2], (((1,), (1,)), ((), ())), preferred_element_type=jnp.float32
        )
        halves.append(piece.astype(jnp.bfloat16).astype(jnp.float32))
    partial_value = (halves[0] + halves[1]).astype(jnp.bfloat16)
    partial_value = partial_value.reshape(req_count * exp_count, capacity, model_width)
    returned = lax.all_to_all(
        partial_value, ("req", "exp"), split_axis=0, concat_axis=0, tiled=True
    )
    result = jnp.sum(
        returned.astype(jnp.float32).reshape(
            req_count, pair_count, slots_here * capacity, model_width
        ),
        axis=1,
    )
    result_rows = jnp.take(result.reshape(slot_total * capacity, model_width), target, axis=0)
    mixture = jnp.sum(
        result_rows.reshape(tok_dev, topk_count, model_width) * gate_values[:, :, None], axis=1
    )
    layer_out = (residual + mixture).astype(jnp.bfloat16)
    spread_slots = lax.all_to_all(slot_weights, "req", split_axis=2, concat_axis=0, tiled=True)
    replica_onehot = new_replicas[:, None] == slot_range[None, :]
    source_slot = jnp.sum(jnp.where(replica_onehot, slot_of[None, :], 0), axis=1)
    chosen_pieces = jnp.take(spread_slots, source_slot, axis=0)
    replica_weights = lax.all_to_all(chosen_pieces, "req", split_axis=0, concat_axis=2, tiled=True)
    return (layer_out, replica_weights)


def solution(mesh):
    in_specs = (
        P(("req", "exp"), None),
        P("req", "exp"),
        P("req", "exp"),
        P("req", "exp"),
        P(),
        P(),
        P("req", None, "exp"),
        P("req", None, "exp"),
        P(),
        P("req", None),
        P("exp", None),
        P(),
        P(("req", "exp"), None),
        P(("req", "exp"), None),
        P(),
        P(),
        P("req", None, None, "exp"),
    )
    out_specs = (P(("req", "exp"), None), P("req", None, None, "exp"))
    return jax.shard_map(body, mesh=mesh, in_specs=in_specs, out_specs=out_specs, check_vma=False)
```

```python
import math

import jax
import jax.numpy as jnp
from jax import lax
from jax.sharding import PartitionSpec as P


def prepare(values, gain, position):
    vector = values.astype(jnp.float32)
    scaled = vector * lax.rsqrt(jnp.mean(vector * vector, axis=-1, keepdims=True) + 1e-06) * gain
    half_size = scaled.shape[-1] // 2
    frequency = 10000.0 ** (-(jnp.arange(half_size, dtype=jnp.float32) * 2.0 / scaled.shape[-1]))
    angles = position[:, None] * frequency[None, :]
    cosine = jnp.cos(angles)[:, None, :]
    sine_part = jnp.sin(angles)[:, None, :]
    lower_half = scaled[..., :half_size]
    upper_half = scaled[..., half_size:]
    rotated = jnp.concatenate(
        [
            lower_half * cosine - upper_half * sine_part,
            upper_half * cosine + lower_half * sine_part,
        ],
        axis=-1,
    )
    return rotated.astype(jnp.bfloat16)


def compact(block_rows, slots_wanted):
    live = block_rows >= 0
    ranks = jnp.cumsum(live.astype(jnp.int32), axis=1) - 1
    request_idx = jnp.arange(block_rows.shape[1], dtype=jnp.int32)[None, :]
    chosen_blocks = []
    chosen_requests = []
    for slot_num in range(slots_wanted):
        picked = live & (ranks == slot_num)
        chosen_blocks.append(jnp.sum(jnp.where(picked, block_rows, 0), axis=1))
        chosen_requests.append(jnp.sum(jnp.where(picked, request_idx, 0), axis=1))
    return (jnp.stack(chosen_blocks, axis=1), jnp.stack(chosen_requests, axis=1))


def body(
    hidden_in,
    query_in,
    key_in,
    value_in,
    query_gain,
    key_gain,
    cache_keys,
    cache_values,
    cache_block,
    request_lengths,
    out_proj,
    norm_gain,
    expert_ids,
    gate_values,
    old_slots,
    new_replicas,
    slot_weights,
):
    req_count = lax.axis_size("req")
    exp_count = lax.axis_size("exp")
    group_idx = lax.axis_index("req")
    tok_grp, width_q = query_in.shape
    tok_dev, model_width = hidden_in.shape
    head_size = query_gain.shape[0]
    head_count = width_q // head_size
    cache_dev = cache_keys.shape[0]
    pre_len = cache_keys.shape[1]
    req_grp = request_lengths.shape[1]
    lengths = request_lengths[0]
    req_ends = jnp.cumsum(lengths)
    starts = req_ends - lengths
    places = jnp.arange(tok_grp, dtype=jnp.int32)
    member = (places[:, None] >= starts[None, :]) & (places[:, None] < req_ends[None, :])
    request_idx = jnp.arange(req_grp, dtype=jnp.int32)
    segment = jnp.sum(jnp.where(member, request_idx[None, :], 0), axis=1)
    offset = places - jnp.sum(jnp.where(member, starts[None, :], 0), axis=1)
    block_rows = cache_block.reshape(req_count, req_grp)
    my_blocks = lax.dynamic_index_in_dim(block_rows, group_idx, 0, keepdims=False)
    has_cache = my_blocks >= 0
    token_cached = jnp.sum(jnp.where(member & has_cache[None, :], 1, 0), axis=1) > 0
    position = (offset + jnp.where(token_cached, pre_len, 0)).astype(jnp.float32)
    need_blocks, need_requests = compact(block_rows, cache_dev)
    my_requests = lax.dynamic_index_in_dim(need_requests, group_idx, 0, keepdims=False)
    key_width = cache_keys.shape[2]
    rows_per = pre_len // req_count
    both = jnp.concatenate([cache_keys, cache_values], axis=-1)
    both = both.reshape(cache_dev, req_count, rows_per, 2 * key_width).transpose(1, 0, 2, 3)
    spread = lax.all_to_all(both, "req", split_axis=0, concat_axis=0, tiled=True)
    spread = spread.reshape(req_count * cache_dev, rows_per, 2 * key_width)
    picked = jnp.take(spread, need_blocks.reshape(-1), axis=0)
    picked = picked.reshape(req_count, cache_dev, rows_per, 2 * key_width)
    gathered = lax.all_to_all(picked, "req", split_axis=0, concat_axis=0, tiled=True)
    gathered = gathered.transpose(1, 0, 2, 3).reshape(cache_dev, pre_len, 2 * key_width)
    far_keys = gathered[..., :key_width]
    far_values = gathered[..., key_width:]
    query_n = prepare(query_in.reshape(tok_grp, head_count, head_size), query_gain, position)
    key_n = prepare(key_in.reshape(tok_grp, head_count, head_size), key_gain, position)
    keyset = jnp.concatenate(
        [key_n, far_keys.reshape(cache_dev * pre_len, head_count, head_size)], axis=0
    )
    valueset = jnp.concatenate(
        [
            value_in.reshape(tok_grp, head_count, head_size),
            far_values.reshape(cache_dev * pre_len, head_count, head_size),
        ],
        axis=0,
    )
    key_request = jnp.concatenate([segment, jnp.repeat(my_requests, pre_len)])
    allowed = segment[:, None] == key_request[None, :]
    scores = jnp.einsum("qhd,khd->hqk", query_n, keyset, preferred_element_type=jnp.float32) * (
        1.0 / math.sqrt(head_size)
    )
    scores = jnp.where(allowed[None], scores, -1e30)
    peak = jnp.max(scores, axis=-1, keepdims=True)
    expos = jnp.exp(scores - peak)
    weights = (expos / jnp.sum(expos, axis=-1, keepdims=True)).astype(jnp.bfloat16)
    attended = jnp.einsum("hqk,khd->qhd", weights, valueset, preferred_element_type=jnp.float32)
    attended = attended.astype(jnp.bfloat16).reshape(tok_grp, width_q)
    attn_out = lax.psum_scatter(
        jnp.dot(attended, out_proj, preferred_element_type=jnp.float32),
        "exp",
        scatter_dimension=0,
        tiled=True,
    )
    residual = hidden_in.astype(jnp.float32) + attn_out
    normed = (
        residual
        * lax.rsqrt(jnp.mean(residual * residual, axis=-1, keepdims=True) + 1e-06)
        * norm_gain
    ).astype(jnp.bfloat16)
    topk_count = expert_ids.shape[1]
    slot_total = old_slots.shape[0]
    slots_here = slot_weights.shape[0]
    capacity = max(2, tok_dev * topk_count * 5 // (4 * slot_total))
    slot_range = jnp.arange(slot_total, dtype=jnp.int32)
    slot_of = jnp.sum(
        jnp.where(old_slots[None, :] == slot_range[:, None], slot_range[None, :], 0), axis=1
    )
    flat_ids = expert_ids.reshape(-1)
    onehot = flat_ids[:, None] == slot_range[None, :]
    row_slot = jnp.sum(jnp.where(onehot, slot_of[None, :], 0), axis=1)
    before = jnp.cumsum(onehot.astype(jnp.int32), axis=0) - onehot.astype(jnp.int32)
    row_rank = jnp.sum(jnp.where(onehot, before, 0), axis=1)
    target = row_slot * capacity + row_rank
    exp_idx = lax.axis_index("exp")
    pair_bit = exp_idx % 2
    pair_count = exp_count // 2
    own_part = lax.dynamic_index_in_dim(slot_weights, pair_bit, 0, keepdims=False)
    give_part = lax.dynamic_index_in_dim(slot_weights, 1 - pair_bit, 0, keepdims=False)
    swap = [(e, e ^ 1) for e in range(exp_count)]
    got_part = lax.ppermute(give_part, "exp", perm=swap)
    lanes = 128
    tile_rows = capacity * model_width // lanes

    def as_tiles(rows):
        return rows.reshape(req_count * exp_count, tile_rows, lanes)

    def as_rows(tiles):
        return tiles.reshape(req_count * exp_count * capacity, model_width)

    send_rows = jnp.repeat(normed, topk_count, axis=0)
    outbox = jnp.zeros((slot_total * capacity, model_width), jnp.bfloat16).at[target].set(send_rows)
    outbox = outbox.reshape(req_count, 1, slots_here * capacity * model_width)
    copies = jnp.broadcast_to(
        outbox, (req_count, pair_count, slots_here * capacity * model_width)
    )
    copies = as_tiles(copies)
    inbox = lax.all_to_all(copies, ("req", "exp"), split_axis=0, concat_axis=0, tiled=True)
    in_rows = as_rows(inbox)
    halves = []
    for part in (own_part, got_part):
        gate_act = jnp.dot(in_rows, part[0], preferred_element_type=jnp.float32)
        up_act = jnp.dot(in_rows, part[1], preferred_element_type=jnp.float32)
        hidden = (jax.nn.silu(gate_act) * up_act).astype(jnp.bfloat16)
        piece = lax.dot_general(
            hidden, part[2], (((1,), (1,)), ((), ())), preferred_element_type=jnp.float32
        )
        halves.append(piece.astype(jnp.bfloat16).astype(jnp.float32))
    partial_value = as_tiles((halves[0] + halves[1]).astype(jnp.bfloat16))
    returned = as_rows(
        lax.all_to_all(partial_value, ("req", "exp"), split_axis=0, concat_axis=0, tiled=True)
    )
    dest_req = row_slot // slots_here
    dest_pos = row_slot % slots_here
    result_rows = None
    for pair_num in range(pair_count):
        where_from = (dest_req * exp_count + pair_num * slots_here + dest_pos) * capacity + row_rank
        one = jnp.take(returned, where_from, axis=0).astype(jnp.float32)
        result_rows = one if result_rows is None else result_rows + one
    mixture = jnp.sum(
        result_rows.reshape(tok_dev, topk_count, model_width) * gate_values[:, :, None], axis=1
    )
    layer_out = (residual + mixture).astype(jnp.bfloat16)
    spread_slots = lax.all_to_all(slot_weights, "req", split_axis=2, concat_axis=0, tiled=True)
    replica_onehot = new_replicas[:, None] == slot_range[None, :]
    source_slot = jnp.sum(jnp.where(replica_onehot, slot_of[None, :], 0), axis=1)
    chosen_pieces = jnp.take(spread_slots, source_slot, axis=0)
    replica_weights = lax.all_to_all(chosen_pieces, "req", split_axis=0, concat_axis=2, tiled=True)
    return (layer_out, replica_weights)


def solution(mesh):
    in_specs = (
        P(("req", "exp"), None),
        P("req", "exp"),
        P("req", "exp"),
        P("req", "exp"),
        P(),
        P(),
        P("req", None, "exp"),
        P("req", None, "exp"),
        P(),
        P("req", None),
        P("exp", None),
        P(),
        P(("req", "exp"), None),
        P(("req", "exp"), None),
        P(),
        P(),
        P("req", None, None, "exp"),
    )
    out_specs = (P(("req", "exp"), None), P("req", None, None, "exp"))
    return jax.shard_map(body, mesh=mesh, in_specs=in_specs, out_specs=out_specs, check_vma=False)
```

```python
import functools
import math

import jax
import jax.numpy as jnp
from jax import lax
from jax.experimental import pallas as pl
from jax.experimental.pallas import tpu as pltpu
from jax.sharding import PartitionSpec as P

MESH = pl.DeviceIdType.MESH


def cache_kernel(n, need_ref, both_ref, out_ref, stage, send_buf, land, sems):
    me = lax.axis_index("req")
    ex = lax.axis_index("exp")
    barrier = pltpu.get_barrier_semaphore()

    def greet(k, carry):
        peer = lax.rem(me + k, n)
        pl.semaphore_signal(barrier, inc=1, device_id=(peer, ex), device_id_type=MESH)
        return carry

    lax.fori_loop(1, n, greet, 0)
    pl.semaphore_wait(barrier, n - 1)

    def first_copy(k, peer):
        return pltpu.make_async_remote_copy(
            src_ref=both_ref.at[peer],
            dst_ref=stage.at[me],
            send_sem=sems.at[0, k],
            recv_sem=sems.at[1, k],
            device_id=(peer, ex),
            device_id_type=MESH,
        )

    def second_copy(k, peer):
        return pltpu.make_async_remote_copy(
            src_ref=send_buf.at[k],
            dst_ref=land.at[me],
            send_sem=sems.at[2, k],
            recv_sem=sems.at[3, k],
            device_id=(peer, ex),
            device_id_type=MESH,
        )

    def send_first(k, carry):
        first_copy(k, lax.rem(me + k, n)).start()
        return carry

    lax.fori_loop(1, n, send_first, 0)
    stage[me] = both_ref[me]

    def wait_first(k, carry):
        source = lax.rem(me + n - k, n)
        pltpu.make_async_remote_copy(
            src_ref=both_ref.at[me],
            dst_ref=stage.at[source],
            send_sem=sems.at[0, k],
            recv_sem=sems.at[1, k],
            device_id=(source, ex),
            device_id_type=MESH,
        ).wait_recv()
        return carry

    lax.fori_loop(1, n, wait_first, 0)
    rows = lax.broadcasted_iota(jnp.int32, both_ref.shape[1:], 0)

    def pieces_for(dest):
        picked = []
        for c in range(2):
            block = need_ref[dest * 2 + c]
            slab = stage[block // 2].astype(jnp.float32)
            one = jnp.where(block % 2 == 0, slab[0:1], slab[1:2])
            picked.append(jnp.broadcast_to(one, slab.shape))
        return jnp.where(rows == 0, picked[0], picked[1]).astype(land.dtype)

    def send_second(k, carry):
        dest = lax.rem(me + k, n)
        send_buf[k] = pieces_for(dest)
        second_copy(k, dest).start()
        return carry

    lax.fori_loop(1, n, send_second, 0)
    land[me] = pieces_for(me)

    def wait_second(k, carry):
        source = lax.rem(me + n - k, n)
        pltpu.make_async_remote_copy(
            src_ref=send_buf.at[k],
            dst_ref=land.at[source],
            send_sem=sems.at[2, k],
            recv_sem=sems.at[3, k],
            device_id=(source, ex),
            device_id_type=MESH,
        ).wait_recv()
        first_copy(k, lax.rem(me + k, n)).wait_send()
        second_copy(k, lax.rem(me + k, n)).wait_send()
        return carry

    lax.fori_loop(1, n, wait_second, 0)
    out_ref[...] = land[...]


def exchange_cache(both_t, need_flat, n):
    shape = both_t.shape
    return pl.pallas_call(
        functools.partial(cache_kernel, n),
        out_shape=jax.ShapeDtypeStruct(shape, both_t.dtype),
        in_specs=[
            pl.BlockSpec(memory_space=pltpu.SMEM),
            pl.BlockSpec(memory_space=pltpu.VMEM),
        ],
        out_specs=pl.BlockSpec(memory_space=pltpu.VMEM),
        scratch_shapes=[
            pltpu.VMEM(shape, both_t.dtype),
            pltpu.VMEM(shape, both_t.dtype),
            pltpu.VMEM(shape, both_t.dtype),
            pltpu.SemaphoreType.DMA((4, n)),
        ],
        compiler_params=pltpu.CompilerParams(collective_id=0, has_side_effects=True),
    )(need_flat, both_t)


def prepare(values, gain, position):
    vector = values.astype(jnp.float32)
    scaled = vector * lax.rsqrt(jnp.mean(vector * vector, axis=-1, keepdims=True) + 1e-06) * gain
    half_size = scaled.shape[-1] // 2
    frequency = 10000.0 ** (-(jnp.arange(half_size, dtype=jnp.float32) * 2.0 / scaled.shape[-1]))
    angles = position[:, None] * frequency[None, :]
    cosine = jnp.cos(angles)[:, None, :]
    sine_part = jnp.sin(angles)[:, None, :]
    lower_half = scaled[..., :half_size]
    upper_half = scaled[..., half_size:]
    rotated = jnp.concatenate(
        [
            lower_half * cosine - upper_half * sine_part,
            upper_half * cosine + lower_half * sine_part,
        ],
        axis=-1,
    )
    return rotated.astype(jnp.bfloat16)


def compact(block_rows, slots_wanted):
    live = block_rows >= 0
    ranks = jnp.cumsum(live.astype(jnp.int32), axis=1) - 1
    request_idx = jnp.arange(block_rows.shape[1], dtype=jnp.int32)[None, :]
    chosen_blocks = []
    chosen_requests = []
    for slot_num in range(slots_wanted):
        picked = live & (ranks == slot_num)
        chosen_blocks.append(jnp.sum(jnp.where(picked, block_rows, 0), axis=1))
        chosen_requests.append(jnp.sum(jnp.where(picked, request_idx, 0), axis=1))
    return (jnp.stack(chosen_blocks, axis=1), jnp.stack(chosen_requests, axis=1))


def body(
    hidden_in,
    query_in,
    key_in,
    value_in,
    query_gain,
    key_gain,
    cache_keys,
    cache_values,
    cache_block,
    request_lengths,
    out_proj,
    norm_gain,
    expert_ids,
    gate_values,
    old_slots,
    new_replicas,
    slot_weights,
):
    req_count = lax.axis_size("req")
    exp_count = lax.axis_size("exp")
    group_idx = lax.axis_index("req")
    tok_grp, width_q = query_in.shape
    tok_dev, model_width = hidden_in.shape
    head_size = query_gain.shape[0]
    head_count = width_q // head_size
    cache_dev = cache_keys.shape[0]
    pre_len = cache_keys.shape[1]
    req_grp = request_lengths.shape[1]
    lengths = request_lengths[0]
    req_ends = jnp.cumsum(lengths)
    starts = req_ends - lengths
    places = jnp.arange(tok_grp, dtype=jnp.int32)
    member = (places[:, None] >= starts[None, :]) & (places[:, None] < req_ends[None, :])
    request_idx = jnp.arange(req_grp, dtype=jnp.int32)
    segment = jnp.sum(jnp.where(member, request_idx[None, :], 0), axis=1)
    offset = places - jnp.sum(jnp.where(member, starts[None, :], 0), axis=1)
    block_rows = cache_block.reshape(req_count, req_grp)
    my_blocks = lax.dynamic_index_in_dim(block_rows, group_idx, 0, keepdims=False)
    has_cache = my_blocks >= 0
    token_cached = jnp.sum(jnp.where(member & has_cache[None, :], 1, 0), axis=1) > 0
    position = (offset + jnp.where(token_cached, pre_len, 0)).astype(jnp.float32)
    need_blocks, need_requests = compact(block_rows, cache_dev)
    my_requests = lax.dynamic_index_in_dim(need_requests, group_idx, 0, keepdims=False)
    key_width = cache_keys.shape[2]
    both = jnp.concatenate([cache_keys, cache_values], axis=-1)
    both_t = both.transpose(1, 0, 2)
    gathered = exchange_cache(both_t, need_blocks.reshape(-1).astype(jnp.int32), req_count)
    gathered = gathered.transpose(1, 0, 2)
    far_keys = gathered[..., :key_width]
    far_values = gathered[..., key_width:]
    query_n = prepare(query_in.reshape(tok_grp, head_count, head_size), query_gain, position)
    key_n = prepare(key_in.reshape(tok_grp, head_count, head_size), key_gain, position)
    keyset = jnp.concatenate(
        [key_n, far_keys.reshape(cache_dev * pre_len, head_count, head_size)], axis=0
    )
    valueset = jnp.concatenate(
        [
            value_in.reshape(tok_grp, head_count, head_size),
            far_values.reshape(cache_dev * pre_len, head_count, head_size),
        ],
        axis=0,
    )
    key_request = jnp.concatenate([segment, jnp.repeat(my_requests, pre_len)])
    allowed = segment[:, None] == key_request[None, :]
    scores = jnp.einsum("qhd,khd->hqk", query_n, keyset, preferred_element_type=jnp.float32) * (
        1.0 / math.sqrt(head_size)
    )
    scores = jnp.where(allowed[None], scores, -1e30)
    peak = jnp.max(scores, axis=-1, keepdims=True)
    expos = jnp.exp(scores - peak)
    weights = (expos / jnp.sum(expos, axis=-1, keepdims=True)).astype(jnp.bfloat16)
    attended = jnp.einsum("hqk,khd->qhd", weights, valueset, preferred_element_type=jnp.float32)
    attended = attended.astype(jnp.bfloat16).reshape(tok_grp, width_q)
    attn_out = lax.psum_scatter(
        jnp.dot(attended, out_proj, preferred_element_type=jnp.float32),
        "exp",
        scatter_dimension=0,
        tiled=True,
    )
    residual = hidden_in.astype(jnp.float32) + attn_out
    normed = (
        residual
        * lax.rsqrt(jnp.mean(residual * residual, axis=-1, keepdims=True) + 1e-06)
        * norm_gain
    ).astype(jnp.bfloat16)
    topk_count = expert_ids.shape[1]
    slot_total = old_slots.shape[0]
    slots_here = slot_weights.shape[0]
    capacity = max(2, tok_dev * topk_count * 5 // (4 * slot_total))
    slot_range = jnp.arange(slot_total, dtype=jnp.int32)
    slot_of = jnp.sum(
        jnp.where(old_slots[None, :] == slot_range[:, None], slot_range[None, :], 0), axis=1
    )
    flat_ids = expert_ids.reshape(-1)
    onehot = flat_ids[:, None] == slot_range[None, :]
    row_slot = jnp.sum(jnp.where(onehot, slot_of[None, :], 0), axis=1)
    before = jnp.cumsum(onehot.astype(jnp.int32), axis=0) - onehot.astype(jnp.int32)
    row_rank = jnp.sum(jnp.where(onehot, before, 0), axis=1)
    target = row_slot * capacity + row_rank
    exp_idx = lax.axis_index("exp")
    pair_bit = exp_idx % 2
    pair_count = exp_count // 2
    own_part = lax.dynamic_index_in_dim(slot_weights, pair_bit, 0, keepdims=False)
    give_part = lax.dynamic_index_in_dim(slot_weights, 1 - pair_bit, 0, keepdims=False)
    swap = [(e, e ^ 1) for e in range(exp_count)]
    got_part = lax.ppermute(give_part, "exp", perm=swap)
    lanes = 128
    tile_rows = capacity * model_width // lanes

    def as_tiles(rows):
        return rows.reshape(req_count * exp_count, tile_rows, lanes)

    def as_rows(tiles):
        return tiles.reshape(req_count * exp_count * capacity, model_width)

    send_rows = jnp.repeat(normed, topk_count, axis=0)
    outbox = jnp.zeros((slot_total * capacity, model_width), jnp.bfloat16).at[target].set(send_rows)
    outbox = outbox.reshape(req_count, 1, slots_here * capacity * model_width)
    copies = jnp.broadcast_to(
        outbox, (req_count, pair_count, slots_here * capacity * model_width)
    )
    copies = as_tiles(copies)
    inbox = lax.all_to_all(copies, ("req", "exp"), split_axis=0, concat_axis=0, tiled=True)
    in_rows = as_rows(inbox)
    halves = []
    for part in (own_part, got_part):
        gate_act = jnp.dot(in_rows, part[0], preferred_element_type=jnp.float32)
        up_act = jnp.dot(in_rows, part[1], preferred_element_type=jnp.float32)
        hidden = (jax.nn.silu(gate_act) * up_act).astype(jnp.bfloat16)
        piece = lax.dot_general(
            hidden, part[2], (((1,), (1,)), ((), ())), preferred_element_type=jnp.float32
        )
        halves.append(piece.astype(jnp.bfloat16).astype(jnp.float32))
    partial_value = as_tiles((halves[0] + halves[1]).astype(jnp.bfloat16))
    returned = as_rows(
        lax.all_to_all(partial_value, ("req", "exp"), split_axis=0, concat_axis=0, tiled=True)
    )
    dest_req = row_slot // slots_here
    dest_pos = row_slot % slots_here
    result_rows = None
    for pair_num in range(pair_count):
        where_from = (dest_req * exp_count + pair_num * slots_here + dest_pos) * capacity + row_rank
        one = jnp.take(returned, where_from, axis=0).astype(jnp.float32)
        result_rows = one if result_rows is None else result_rows + one
    mixture = jnp.sum(
        result_rows.reshape(tok_dev, topk_count, model_width) * gate_values[:, :, None], axis=1
    )
    layer_out = (residual + mixture).astype(jnp.bfloat16)
    spread_slots = lax.all_to_all(slot_weights, "req", split_axis=2, concat_axis=0, tiled=True)
    replica_onehot = new_replicas[:, None] == slot_range[None, :]
    source_slot = jnp.sum(jnp.where(replica_onehot, slot_of[None, :], 0), axis=1)
    chosen_pieces = jnp.take(spread_slots, source_slot, axis=0)
    replica_weights = lax.all_to_all(chosen_pieces, "req", split_axis=0, concat_axis=2, tiled=True)
    return (layer_out, replica_weights)


def solution(mesh):
    in_specs = (
        P(("req", "exp"), None),
        P("req", "exp"),
        P("req", "exp"),
        P("req", "exp"),
        P(),
        P(),
        P("req", None, "exp"),
        P("req", None, "exp"),
        P(),
        P("req", None),
        P("exp", None),
        P(),
        P(("req", "exp"), None),
        P(("req", "exp"), None),
        P(),
        P(),
        P("req", None, None, "exp"),
    )
    out_specs = (P(("req", "exp"), None), P("req", None, None, "exp"))
    return jax.shard_map(body, mesh=mesh, in_specs=in_specs, out_specs=out_specs, check_vma=False)
```

```python
import functools
import math

import jax
import jax.numpy as jnp
from jax import lax
from jax.experimental import pallas as pl
from jax.experimental.pallas import tpu as pltpu
from jax.sharding import PartitionSpec as P

MESH = pl.DeviceIdType.MESH


def cache_kernel(n, need_ref, both_ref, out_ref, stage, send_buf, land, sems):
    me = lax.axis_index("req")
    ex = lax.axis_index("exp")
    barrier = pltpu.get_barrier_semaphore()

    def greet(k, carry):
        peer = lax.rem(me + k, n)
        pl.semaphore_signal(barrier, inc=1, device_id=(peer, ex), device_id_type=MESH)
        return carry

    lax.fori_loop(1, n, greet, 0)
    pl.semaphore_wait(barrier, n - 1)

    def first_copy(k, peer):
        return pltpu.make_async_remote_copy(
            src_ref=both_ref.at[peer],
            dst_ref=stage.at[me],
            send_sem=sems.at[0, k],
            recv_sem=sems.at[1, k],
            device_id=(peer, ex),
            device_id_type=MESH,
        )

    def second_copy(k, peer):
        return pltpu.make_async_remote_copy(
            src_ref=send_buf.at[k],
            dst_ref=land.at[me],
            send_sem=sems.at[2, k],
            recv_sem=sems.at[3, k],
            device_id=(peer, ex),
            device_id_type=MESH,
        )

    def send_first(k, carry):
        first_copy(k, lax.rem(me + k, n)).start()
        return carry

    lax.fori_loop(1, n, send_first, 0)
    stage[me] = both_ref[me]

    def wait_first(k, carry):
        source = lax.rem(me + n - k, n)
        pltpu.make_async_remote_copy(
            src_ref=both_ref.at[me],
            dst_ref=stage.at[source],
            send_sem=sems.at[0, k],
            recv_sem=sems.at[1, k],
            device_id=(source, ex),
            device_id_type=MESH,
        ).wait_recv()
        return carry

    lax.fori_loop(1, n, wait_first, 0)
    rows = lax.broadcasted_iota(jnp.int32, both_ref.shape[1:], 0)

    def pieces_for(dest):
        picked = []
        for c in range(2):
            block = need_ref[dest * 2 + c]
            slab = stage[block // 2].astype(jnp.float32)
            one = jnp.where(block % 2 == 0, slab[0:1], slab[1:2])
            picked.append(jnp.broadcast_to(one, slab.shape))
        return jnp.where(rows == 0, picked[0], picked[1]).astype(land.dtype)

    def send_second(k, carry):
        dest = lax.rem(me + k, n)
        send_buf[k] = pieces_for(dest)
        second_copy(k, dest).start()
        return carry

    lax.fori_loop(1, n, send_second, 0)
    land[me] = pieces_for(me)

    def wait_second(k, carry):
        source = lax.rem(me + n - k, n)
        pltpu.make_async_remote_copy(
            src_ref=send_buf.at[k],
            dst_ref=land.at[source],
            send_sem=sems.at[2, k],
            recv_sem=sems.at[3, k],
            device_id=(source, ex),
            device_id_type=MESH,
        ).wait_recv()
        first_copy(k, lax.rem(me + k, n)).wait_send()
        second_copy(k, lax.rem(me + k, n)).wait_send()
        return carry

    lax.fori_loop(1, n, wait_second, 0)
    out_ref[...] = land[...]


def exchange_cache(both_t, need_flat, n):
    shape = both_t.shape
    return pl.pallas_call(
        functools.partial(cache_kernel, n),
        out_shape=jax.ShapeDtypeStruct(shape, both_t.dtype),
        in_specs=[
            pl.BlockSpec(memory_space=pltpu.SMEM),
            pl.BlockSpec(memory_space=pltpu.VMEM),
        ],
        out_specs=pl.BlockSpec(memory_space=pltpu.VMEM),
        scratch_shapes=[
            pltpu.VMEM(shape, both_t.dtype),
            pltpu.VMEM(shape, both_t.dtype),
            pltpu.VMEM(shape, both_t.dtype),
            pltpu.SemaphoreType.DMA((4, n)),
        ],
        compiler_params=pltpu.CompilerParams(collective_id=0, has_side_effects=True),
    )(need_flat, both_t)


def prepare(values, gain, position):
    vector = values.astype(jnp.float32)
    scaled = vector * lax.rsqrt(jnp.mean(vector * vector, axis=-1, keepdims=True) + 1e-06) * gain
    half_size = scaled.shape[-1] // 2
    frequency = 10000.0 ** (-(jnp.arange(half_size, dtype=jnp.float32) * 2.0 / scaled.shape[-1]))
    angles = position[:, None] * frequency[None, :]
    cosine = jnp.cos(angles)[:, None, :]
    sine_part = jnp.sin(angles)[:, None, :]
    lower_half = scaled[..., :half_size]
    upper_half = scaled[..., half_size:]
    rotated = jnp.concatenate(
        [
            lower_half * cosine - upper_half * sine_part,
            upper_half * cosine + lower_half * sine_part,
        ],
        axis=-1,
    )
    return rotated.astype(jnp.bfloat16)


def compact(block_rows, slots_wanted):
    live = block_rows >= 0
    ranks = jnp.cumsum(live.astype(jnp.int32), axis=1) - 1
    request_idx = jnp.arange(block_rows.shape[1], dtype=jnp.int32)[None, :]
    chosen_blocks = []
    chosen_requests = []
    for slot_num in range(slots_wanted):
        picked = live & (ranks == slot_num)
        chosen_blocks.append(jnp.sum(jnp.where(picked, block_rows, 0), axis=1))
        chosen_requests.append(jnp.sum(jnp.where(picked, request_idx, 0), axis=1))
    return (jnp.stack(chosen_blocks, axis=1), jnp.stack(chosen_requests, axis=1))


def body(
    hidden_in,
    query_in,
    key_in,
    value_in,
    query_gain,
    key_gain,
    cache_keys,
    cache_values,
    cache_block,
    request_lengths,
    out_proj,
    norm_gain,
    expert_ids,
    gate_values,
    old_slots,
    new_replicas,
    slot_weights,
):
    req_count = lax.axis_size("req")
    exp_count = lax.axis_size("exp")
    group_idx = lax.axis_index("req")
    tok_grp, width_q = query_in.shape
    tok_dev, model_width = hidden_in.shape
    head_size = query_gain.shape[0]
    head_count = width_q // head_size
    cache_dev = cache_keys.shape[0]
    pre_len = cache_keys.shape[1]
    req_grp = request_lengths.shape[1]
    lengths = request_lengths[0]
    req_ends = jnp.cumsum(lengths)
    starts = req_ends - lengths
    places = jnp.arange(tok_grp, dtype=jnp.int32)
    member = (places[:, None] >= starts[None, :]) & (places[:, None] < req_ends[None, :])
    request_idx = jnp.arange(req_grp, dtype=jnp.int32)
    segment = jnp.sum(jnp.where(member, request_idx[None, :], 0), axis=1)
    offset = places - jnp.sum(jnp.where(member, starts[None, :], 0), axis=1)
    block_rows = cache_block.reshape(req_count, req_grp)
    my_blocks = lax.dynamic_index_in_dim(block_rows, group_idx, 0, keepdims=False)
    has_cache = my_blocks >= 0
    token_cached = jnp.sum(jnp.where(member & has_cache[None, :], 1, 0), axis=1) > 0
    position = (offset + jnp.where(token_cached, pre_len, 0)).astype(jnp.float32)
    need_blocks, need_requests = compact(block_rows, cache_dev)
    my_requests = lax.dynamic_index_in_dim(need_requests, group_idx, 0, keepdims=False)
    key_width = cache_keys.shape[2]
    both = jnp.concatenate([cache_keys, cache_values], axis=-1)
    both_t = both.transpose(1, 0, 2)
    gathered = exchange_cache(both_t, need_blocks.reshape(-1).astype(jnp.int32), req_count)
    gathered = gathered.transpose(1, 0, 2)
    slot_weights, gathered = lax.optimization_barrier((slot_weights, gathered))
    far_keys = gathered[..., :key_width]
    far_values = gathered[..., key_width:]
    query_n = prepare(query_in.reshape(tok_grp, head_count, head_size), query_gain, position)
    key_n = prepare(key_in.reshape(tok_grp, head_count, head_size), key_gain, position)
    keyset = jnp.concatenate(
        [key_n, far_keys.reshape(cache_dev * pre_len, head_count, head_size)], axis=0
    )
    valueset = jnp.concatenate(
        [
            value_in.reshape(tok_grp, head_count, head_size),
            far_values.reshape(cache_dev * pre_len, head_count, head_size),
        ],
        axis=0,
    )
    key_request = jnp.concatenate([segment, jnp.repeat(my_requests, pre_len)])
    allowed = segment[:, None] == key_request[None, :]
    scores = jnp.einsum("qhd,khd->hqk", query_n, keyset, preferred_element_type=jnp.float32) * (
        1.0 / math.sqrt(head_size)
    )
    scores = jnp.where(allowed[None], scores, -1e30)
    peak = jnp.max(scores, axis=-1, keepdims=True)
    expos = jnp.exp(scores - peak)
    weights = (expos / jnp.sum(expos, axis=-1, keepdims=True)).astype(jnp.bfloat16)
    attended = jnp.einsum("hqk,khd->qhd", weights, valueset, preferred_element_type=jnp.float32)
    attended = attended.astype(jnp.bfloat16).reshape(tok_grp, width_q)
    attn_out = lax.psum_scatter(
        jnp.dot(attended, out_proj, preferred_element_type=jnp.float32),
        "exp",
        scatter_dimension=0,
        tiled=True,
    )
    residual = hidden_in.astype(jnp.float32) + attn_out
    normed = (
        residual
        * lax.rsqrt(jnp.mean(residual * residual, axis=-1, keepdims=True) + 1e-06)
        * norm_gain
    ).astype(jnp.bfloat16)
    topk_count = expert_ids.shape[1]
    slot_total = old_slots.shape[0]
    slots_here = slot_weights.shape[0]
    capacity = max(2, tok_dev * topk_count * 5 // (4 * slot_total))
    slot_range = jnp.arange(slot_total, dtype=jnp.int32)
    slot_of = jnp.sum(
        jnp.where(old_slots[None, :] == slot_range[:, None], slot_range[None, :], 0), axis=1
    )
    flat_ids = expert_ids.reshape(-1)
    onehot = flat_ids[:, None] == slot_range[None, :]
    row_slot = jnp.sum(jnp.where(onehot, slot_of[None, :], 0), axis=1)
    before = jnp.cumsum(onehot.astype(jnp.int32), axis=0) - onehot.astype(jnp.int32)
    row_rank = jnp.sum(jnp.where(onehot, before, 0), axis=1)
    target = row_slot * capacity + row_rank
    exp_idx = lax.axis_index("exp")
    pair_bit = exp_idx % 2
    pair_count = exp_count // 2
    own_part = lax.dynamic_index_in_dim(slot_weights, pair_bit, 0, keepdims=False)
    give_part = lax.dynamic_index_in_dim(slot_weights, 1 - pair_bit, 0, keepdims=False)
    swap = [(e, e ^ 1) for e in range(exp_count)]
    got_part = lax.ppermute(give_part, "exp", perm=swap)
    lanes = 128
    tile_rows = capacity * model_width // lanes

    def as_tiles(rows):
        return rows.reshape(req_count * exp_count, tile_rows, lanes)

    def as_rows(tiles):
        return tiles.reshape(req_count * exp_count * capacity, model_width)

    send_rows = jnp.repeat(normed, topk_count, axis=0)
    outbox = jnp.zeros((slot_total * capacity, model_width), jnp.bfloat16).at[target].set(send_rows)
    outbox = outbox.reshape(req_count, 1, slots_here * capacity * model_width)
    copies = jnp.broadcast_to(
        outbox, (req_count, pair_count, slots_here * capacity * model_width)
    )
    copies = as_tiles(copies)
    inbox = lax.all_to_all(copies, ("req", "exp"), split_axis=0, concat_axis=0, tiled=True)
    in_rows = as_rows(inbox)
    halves = []
    for part in (own_part, got_part):
        gate_act = jnp.dot(in_rows, part[0], preferred_element_type=jnp.float32)
        up_act = jnp.dot(in_rows, part[1], preferred_element_type=jnp.float32)
        hidden = (jax.nn.silu(gate_act) * up_act).astype(jnp.bfloat16)
        piece = lax.dot_general(
            hidden, part[2], (((1,), (1,)), ((), ())), preferred_element_type=jnp.float32
        )
        halves.append(piece.astype(jnp.bfloat16).astype(jnp.float32))
    partial_value = as_tiles((halves[0] + halves[1]).astype(jnp.bfloat16))
    returned = as_rows(
        lax.all_to_all(partial_value, ("req", "exp"), split_axis=0, concat_axis=0, tiled=True)
    )
    dest_req = row_slot // slots_here
    dest_pos = row_slot % slots_here
    result_rows = None
    for pair_num in range(pair_count):
        where_from = (dest_req * exp_count + pair_num * slots_here + dest_pos) * capacity + row_rank
        one = jnp.take(returned, where_from, axis=0).astype(jnp.float32)
        result_rows = one if result_rows is None else result_rows + one
    mixture = jnp.sum(
        result_rows.reshape(tok_dev, topk_count, model_width) * gate_values[:, :, None], axis=1
    )
    layer_out = (residual + mixture).astype(jnp.bfloat16)
    spread_slots = lax.all_to_all(slot_weights, "req", split_axis=2, concat_axis=0, tiled=True)
    replica_onehot = new_replicas[:, None] == slot_range[None, :]
    source_slot = jnp.sum(jnp.where(replica_onehot, slot_of[None, :], 0), axis=1)
    chosen_pieces = jnp.take(spread_slots, source_slot, axis=0)
    replica_weights = lax.all_to_all(chosen_pieces, "req", split_axis=0, concat_axis=2, tiled=True)
    return (layer_out, replica_weights)


def solution(mesh):
    in_specs = (
        P(("req", "exp"), None),
        P("req", "exp"),
        P("req", "exp"),
        P("req", "exp"),
        P(),
        P(),
        P("req", None, "exp"),
        P("req", None, "exp"),
        P(),
        P("req", None),
        P("exp", None),
        P(),
        P(("req", "exp"), None),
        P(("req", "exp"), None),
        P(),
        P(),
        P("req", None, None, "exp"),
    )
    out_specs = (P(("req", "exp"), None), P("req", None, None, "exp"))
    return jax.shard_map(body, mesh=mesh, in_specs=in_specs, out_specs=out_specs, check_vma=False)
```

```python
import functools
import math

import jax
import jax.numpy as jnp
from jax import lax
from jax.experimental import pallas as pl
from jax.experimental.pallas import tpu as pltpu
from jax.sharding import PartitionSpec as P

MESH = pl.DeviceIdType.MESH


def cache_kernel(n, need_ref, both_ref, out_ref, stage, send_buf, land, sems):
    me = lax.axis_index("req")
    ex = lax.axis_index("exp")
    barrier = pltpu.get_barrier_semaphore()

    def greet(k, carry):
        peer = lax.rem(me + k, n)
        pl.semaphore_signal(barrier, inc=1, device_id=(peer, ex), device_id_type=MESH)
        return carry

    lax.fori_loop(1, n, greet, 0)
    pl.semaphore_wait(barrier, n - 1)

    def first_copy(k, peer):
        return pltpu.make_async_remote_copy(
            src_ref=both_ref.at[peer],
            dst_ref=stage.at[me],
            send_sem=sems.at[0, k],
            recv_sem=sems.at[1, k],
            device_id=(peer, ex),
            device_id_type=MESH,
        )

    def second_copy(k, peer):
        return pltpu.make_async_remote_copy(
            src_ref=send_buf.at[k],
            dst_ref=land.at[me],
            send_sem=sems.at[2, k],
            recv_sem=sems.at[3, k],
            device_id=(peer, ex),
            device_id_type=MESH,
        )

    def send_first(k, carry):
        first_copy(k, lax.rem(me + k, n)).start()
        return carry

    lax.fori_loop(1, n, send_first, 0)
    stage[me] = both_ref[me]

    def wait_first(k, carry):
        source = lax.rem(me + n - k, n)
        pltpu.make_async_remote_copy(
            src_ref=both_ref.at[me],
            dst_ref=stage.at[source],
            send_sem=sems.at[0, k],
            recv_sem=sems.at[1, k],
            device_id=(source, ex),
            device_id_type=MESH,
        ).wait_recv()
        return carry

    lax.fori_loop(1, n, wait_first, 0)
    rows = lax.broadcasted_iota(jnp.int32, both_ref.shape[1:], 0)

    def pieces_for(dest):
        picked = []
        for c in range(2):
            block = need_ref[dest * 2 + c]
            slab = stage[block // 2].astype(jnp.float32)
            one = jnp.where(block % 2 == 0, slab[0:1], slab[1:2])
            picked.append(jnp.broadcast_to(one, slab.shape))
        return jnp.where(rows == 0, picked[0], picked[1]).astype(land.dtype)

    def send_second(k, carry):
        dest = lax.rem(me + k, n)
        send_buf[k] = pieces_for(dest)
        second_copy(k, dest).start()
        return carry

    lax.fori_loop(1, n, send_second, 0)
    land[me] = pieces_for(me)

    def wait_second(k, carry):
        source = lax.rem(me + n - k, n)
        pltpu.make_async_remote_copy(
            src_ref=send_buf.at[k],
            dst_ref=land.at[source],
            send_sem=sems.at[2, k],
            recv_sem=sems.at[3, k],
            device_id=(source, ex),
            device_id_type=MESH,
        ).wait_recv()
        first_copy(k, lax.rem(me + k, n)).wait_send()
        second_copy(k, lax.rem(me + k, n)).wait_send()
        return carry

    lax.fori_loop(1, n, wait_second, 0)
    out_ref[...] = land[...]


def exchange_cache(both_t, need_flat, n):
    shape = both_t.shape
    return pl.pallas_call(
        functools.partial(cache_kernel, n),
        out_shape=jax.ShapeDtypeStruct(shape, both_t.dtype),
        in_specs=[
            pl.BlockSpec(memory_space=pltpu.SMEM),
            pl.BlockSpec(memory_space=pltpu.VMEM),
        ],
        out_specs=pl.BlockSpec(memory_space=pltpu.VMEM),
        scratch_shapes=[
            pltpu.VMEM(shape, both_t.dtype),
            pltpu.VMEM(shape, both_t.dtype),
            pltpu.VMEM(shape, both_t.dtype),
            pltpu.SemaphoreType.DMA((4, n)),
        ],
        compiler_params=pltpu.CompilerParams(collective_id=0, has_side_effects=True),
    )(need_flat, both_t)


def prepare(values, gain, position):
    vector = values.astype(jnp.float32)
    scaled = vector * lax.rsqrt(jnp.mean(vector * vector, axis=-1, keepdims=True) + 1e-06) * gain
    half_size = scaled.shape[-1] // 2
    frequency = 10000.0 ** (-(jnp.arange(half_size, dtype=jnp.float32) * 2.0 / scaled.shape[-1]))
    angles = position[:, None] * frequency[None, :]
    cosine = jnp.cos(angles)[:, None, :]
    sine_part = jnp.sin(angles)[:, None, :]
    lower_half = scaled[..., :half_size]
    upper_half = scaled[..., half_size:]
    rotated = jnp.concatenate(
        [
            lower_half * cosine - upper_half * sine_part,
            upper_half * cosine + lower_half * sine_part,
        ],
        axis=-1,
    )
    return rotated.astype(jnp.bfloat16)


def compact(block_rows, slots_wanted):
    live = block_rows >= 0
    ranks = jnp.cumsum(live.astype(jnp.int32), axis=1) - 1
    request_idx = jnp.arange(block_rows.shape[1], dtype=jnp.int32)[None, :]
    chosen_blocks = []
    chosen_requests = []
    for slot_num in range(slots_wanted):
        picked = live & (ranks == slot_num)
        chosen_blocks.append(jnp.sum(jnp.where(picked, block_rows, 0), axis=1))
        chosen_requests.append(jnp.sum(jnp.where(picked, request_idx, 0), axis=1))
    return (jnp.stack(chosen_blocks, axis=1), jnp.stack(chosen_requests, axis=1))


def body(
    hidden_in,
    query_in,
    key_in,
    value_in,
    query_gain,
    key_gain,
    cache_keys,
    cache_values,
    cache_block,
    request_lengths,
    out_proj,
    norm_gain,
    expert_ids,
    gate_values,
    old_slots,
    new_replicas,
    slot_weights,
):
    req_count = lax.axis_size("req")
    exp_count = lax.axis_size("exp")
    group_idx = lax.axis_index("req")
    tok_grp, width_q = query_in.shape
    tok_dev, model_width = hidden_in.shape
    head_size = query_gain.shape[0]
    head_count = width_q // head_size
    cache_dev = cache_keys.shape[0]
    pre_len = cache_keys.shape[1]
    req_grp = request_lengths.shape[1]
    lengths = request_lengths[0]
    req_ends = jnp.cumsum(lengths)
    starts = req_ends - lengths
    places = jnp.arange(tok_grp, dtype=jnp.int32)
    member = (places[:, None] >= starts[None, :]) & (places[:, None] < req_ends[None, :])
    request_idx = jnp.arange(req_grp, dtype=jnp.int32)
    segment = jnp.sum(jnp.where(member, request_idx[None, :], 0), axis=1)
    offset = places - jnp.sum(jnp.where(member, starts[None, :], 0), axis=1)
    block_rows = cache_block.reshape(req_count, req_grp)
    my_blocks = lax.dynamic_index_in_dim(block_rows, group_idx, 0, keepdims=False)
    has_cache = my_blocks >= 0
    token_cached = jnp.sum(jnp.where(member & has_cache[None, :], 1, 0), axis=1) > 0
    position = (offset + jnp.where(token_cached, pre_len, 0)).astype(jnp.float32)
    need_blocks, need_requests = compact(block_rows, cache_dev)
    my_requests = lax.dynamic_index_in_dim(need_requests, group_idx, 0, keepdims=False)
    key_width = cache_keys.shape[2]
    both = jnp.concatenate([cache_keys, cache_values], axis=-1)
    both_t = both.transpose(1, 0, 2)
    gathered = exchange_cache(both_t, need_blocks.reshape(-1).astype(jnp.int32), req_count)
    gathered = gathered.transpose(1, 0, 2)
    slot_weights, gathered = lax.optimization_barrier((slot_weights, gathered))
    far_keys = gathered[..., :key_width]
    far_values = gathered[..., key_width:]
    query_n = prepare(query_in.reshape(tok_grp, head_count, head_size), query_gain, position)
    key_n = prepare(key_in.reshape(tok_grp, head_count, head_size), key_gain, position)
    keyset = jnp.concatenate(
        [key_n, far_keys.reshape(cache_dev * pre_len, head_count, head_size)], axis=0
    )
    valueset = jnp.concatenate(
        [
            value_in.reshape(tok_grp, head_count, head_size),
            far_values.reshape(cache_dev * pre_len, head_count, head_size),
        ],
        axis=0,
    )
    key_request = jnp.concatenate([segment, jnp.repeat(my_requests, pre_len)])
    allowed = segment[:, None] == key_request[None, :]
    scores = jnp.einsum("qhd,khd->hqk", query_n, keyset, preferred_element_type=jnp.float32) * (
        1.0 / math.sqrt(head_size)
    )
    scores = jnp.where(allowed[None], scores, -1e30)
    peak = jnp.max(scores, axis=-1, keepdims=True)
    expos = jnp.exp(scores - peak)
    weights = (expos / jnp.sum(expos, axis=-1, keepdims=True)).astype(jnp.bfloat16)
    attended = jnp.einsum("hqk,khd->qhd", weights, valueset, preferred_element_type=jnp.float32)
    attended = attended.astype(jnp.bfloat16).reshape(tok_grp, width_q)
    attn_out = lax.psum_scatter(
        jnp.dot(attended, out_proj, preferred_element_type=jnp.float32),
        "exp",
        scatter_dimension=0,
        tiled=True,
    )
    residual = hidden_in.astype(jnp.float32) + attn_out
    normed = (
        residual
        * lax.rsqrt(jnp.mean(residual * residual, axis=-1, keepdims=True) + 1e-06)
        * norm_gain
    ).astype(jnp.bfloat16)
    topk_count = expert_ids.shape[1]
    slot_total = old_slots.shape[0]
    slots_here = slot_weights.shape[0]
    capacity = max(2, tok_dev * topk_count * 5 // (4 * slot_total))
    slot_range = jnp.arange(slot_total, dtype=jnp.int32)
    slot_of = jnp.sum(
        jnp.where(old_slots[None, :] == slot_range[:, None], slot_range[None, :], 0), axis=1
    )
    flat_ids = expert_ids.reshape(-1)
    onehot = flat_ids[:, None] == slot_range[None, :]
    row_slot = jnp.sum(jnp.where(onehot, slot_of[None, :], 0), axis=1)
    before = jnp.cumsum(onehot.astype(jnp.int32), axis=0) - onehot.astype(jnp.int32)
    row_rank = jnp.sum(jnp.where(onehot, before, 0), axis=1)
    target = row_slot * capacity + row_rank
    exp_idx = lax.axis_index("exp")
    pair_bit = exp_idx % 2
    pair_count = exp_count // 2
    own_part = lax.dynamic_index_in_dim(slot_weights, pair_bit, 0, keepdims=False)
    give_part = lax.dynamic_index_in_dim(slot_weights, 1 - pair_bit, 0, keepdims=False)
    swap = [(e, e ^ 1) for e in range(exp_count)]
    got_part = lax.ppermute(give_part, "exp", perm=swap)
    lanes = 128
    tile_rows = capacity * model_width // lanes

    def as_tiles(rows):
        return rows.reshape(req_count * exp_count, tile_rows, lanes)

    def as_rows(tiles):
        return tiles.reshape(req_count * exp_count * capacity, model_width)

    tile_high = model_width // lanes
    normed_tiles = normed.reshape(tok_dev, tile_high, lanes)
    row_token = jnp.arange(tok_dev * topk_count, dtype=jnp.int32) // topk_count
    source_token = jnp.zeros((slot_total * capacity,), jnp.int32).at[target].set(row_token)
    filled = jnp.zeros((slot_total * capacity,), jnp.bool_).at[target].set(True)
    outbox = jnp.where(filled[:, None, None], normed_tiles[source_token], jnp.bfloat16(0))
    outbox = outbox.reshape(req_count, 1, slots_here * tile_rows, lanes)
    copies = jnp.broadcast_to(outbox, (req_count, pair_count, slots_here * tile_rows, lanes))
    copies = copies.reshape(req_count * exp_count, tile_rows, lanes)
    inbox = lax.all_to_all(copies, ("req", "exp"), split_axis=0, concat_axis=0, tiled=True)
    in_rows = as_rows(inbox)
    halves = []
    for part in (own_part, got_part):
        gate_act = jnp.dot(in_rows, part[0], preferred_element_type=jnp.float32)
        up_act = jnp.dot(in_rows, part[1], preferred_element_type=jnp.float32)
        hidden = (jax.nn.silu(gate_act) * up_act).astype(jnp.bfloat16)
        piece = lax.dot_general(
            hidden, part[2], (((1,), (1,)), ((), ())), preferred_element_type=jnp.float32
        )
        halves.append(piece.astype(jnp.bfloat16).astype(jnp.float32))
    partial_value = as_tiles((halves[0] + halves[1]).astype(jnp.bfloat16))
    returned = lax.all_to_all(
        partial_value, ("req", "exp"), split_axis=0, concat_axis=0, tiled=True
    ).reshape(req_count * exp_count * capacity, tile_high, lanes)
    dest_req = row_slot // slots_here
    dest_pos = row_slot % slots_here
    result_rows = None
    for pair_num in range(pair_count):
        where_from = (dest_req * exp_count + pair_num * slots_here + dest_pos) * capacity + row_rank
        one = jnp.take(returned, where_from, axis=0).astype(jnp.float32)
        result_rows = one if result_rows is None else result_rows + one
    mixture = jnp.sum(
        result_rows.reshape(tok_dev, topk_count, tile_high, lanes)
        * gate_values[:, :, None, None],
        axis=1,
    )
    residual_tiles = residual.reshape(tok_dev, tile_high, lanes)
    layer_out = (residual_tiles + mixture).astype(jnp.bfloat16).reshape(tok_dev, model_width)
    spread_slots = lax.all_to_all(slot_weights, "req", split_axis=2, concat_axis=0, tiled=True)
    replica_onehot = new_replicas[:, None] == slot_range[None, :]
    source_slot = jnp.sum(jnp.where(replica_onehot, slot_of[None, :], 0), axis=1)
    chosen_pieces = jnp.take(spread_slots, source_slot, axis=0)
    replica_weights = lax.all_to_all(chosen_pieces, "req", split_axis=0, concat_axis=2, tiled=True)
    return (layer_out, replica_weights)


def solution(mesh):
    in_specs = (
        P(("req", "exp"), None),
        P("req", "exp"),
        P("req", "exp"),
        P("req", "exp"),
        P(),
        P(),
        P("req", None, "exp"),
        P("req", None, "exp"),
        P(),
        P("req", None),
        P("exp", None),
        P(),
        P(("req", "exp"), None),
        P(("req", "exp"), None),
        P(),
        P(),
        P("req", None, None, "exp"),
    )
    out_specs = (P(("req", "exp"), None), P("req", None, None, "exp"))
    return jax.shard_map(body, mesh=mesh, in_specs=in_specs, out_specs=out_specs, check_vma=False)
```

```python
import functools
import math

import jax
import jax.numpy as jnp
from jax import lax
from jax.experimental import pallas as pl
from jax.experimental.pallas import tpu as pltpu
from jax.sharding import PartitionSpec as P

MESH = pl.DeviceIdType.MESH


def cache_kernel(n, need_ref, both_ref, out_ref, stage, send_buf, land, sems):
    me = lax.axis_index("req")
    ex = lax.axis_index("exp")
    barrier = pltpu.get_barrier_semaphore()

    def greet(k, carry):
        peer = lax.rem(me + k, n)
        pl.semaphore_signal(barrier, inc=1, device_id=(peer, ex), device_id_type=MESH)
        return carry

    lax.fori_loop(1, n, greet, 0)
    pl.semaphore_wait(barrier, n - 1)

    def first_copy(k, peer):
        return pltpu.make_async_remote_copy(
            src_ref=both_ref.at[peer],
            dst_ref=stage.at[me],
            send_sem=sems.at[0, k],
            recv_sem=sems.at[1, k],
            device_id=(peer, ex),
            device_id_type=MESH,
        )

    def second_copy(k, peer):
        return pltpu.make_async_remote_copy(
            src_ref=send_buf.at[k],
            dst_ref=land.at[me],
            send_sem=sems.at[2, k],
            recv_sem=sems.at[3, k],
            device_id=(peer, ex),
            device_id_type=MESH,
        )

    def send_first(k, carry):
        first_copy(k, lax.rem(me + k, n)).start()
        return carry

    lax.fori_loop(1, n, send_first, 0)
    stage[me] = both_ref[me]

    def wait_first(k, carry):
        source = lax.rem(me + n - k, n)
        pltpu.make_async_remote_copy(
            src_ref=both_ref.at[me],
            dst_ref=stage.at[source],
            send_sem=sems.at[0, k],
            recv_sem=sems.at[1, k],
            device_id=(source, ex),
            device_id_type=MESH,
        ).wait_recv()
        return carry

    lax.fori_loop(1, n, wait_first, 0)
    rows = lax.broadcasted_iota(jnp.int32, both_ref.shape[1:], 0)

    def pieces_for(dest):
        picked = []
        for c in range(2):
            block = need_ref[dest * 2 + c]
            slab = stage[block // 2].astype(jnp.float32)
            one = jnp.where(block % 2 == 0, slab[0:1], slab[1:2])
            picked.append(jnp.broadcast_to(one, slab.shape))
        return jnp.where(rows == 0, picked[0], picked[1]).astype(land.dtype)

    def send_second(k, carry):
        dest = lax.rem(me + k, n)
        send_buf[k] = pieces_for(dest)
        second_copy(k, dest).start()
        return carry

    lax.fori_loop(1, n, send_second, 0)
    land[me] = pieces_for(me)

    def wait_second(k, carry):
        source = lax.rem(me + n - k, n)
        pltpu.make_async_remote_copy(
            src_ref=send_buf.at[k],
            dst_ref=land.at[source],
            send_sem=sems.at[2, k],
            recv_sem=sems.at[3, k],
            device_id=(source, ex),
            device_id_type=MESH,
        ).wait_recv()
        first_copy(k, lax.rem(me + k, n)).wait_send()
        second_copy(k, lax.rem(me + k, n)).wait_send()
        return carry

    lax.fori_loop(1, n, wait_second, 0)
    out_ref[...] = land[...]


def exchange_cache(both_t, need_flat, n):
    shape = both_t.shape
    return pl.pallas_call(
        functools.partial(cache_kernel, n),
        out_shape=jax.ShapeDtypeStruct(shape, both_t.dtype),
        in_specs=[
            pl.BlockSpec(memory_space=pltpu.SMEM),
            pl.BlockSpec(memory_space=pltpu.VMEM),
        ],
        out_specs=pl.BlockSpec(memory_space=pltpu.VMEM),
        scratch_shapes=[
            pltpu.VMEM(shape, both_t.dtype),
            pltpu.VMEM(shape, both_t.dtype),
            pltpu.VMEM(shape, both_t.dtype),
            pltpu.SemaphoreType.DMA((4, n)),
        ],
        compiler_params=pltpu.CompilerParams(collective_id=0, has_side_effects=True),
    )(need_flat, both_t)


def prepare(values, gain, position):
    vector = values.astype(jnp.float32)
    scaled = vector * lax.rsqrt(jnp.mean(vector * vector, axis=-1, keepdims=True) + 1e-06) * gain
    half_size = scaled.shape[-1] // 2
    frequency = 10000.0 ** (-(jnp.arange(half_size, dtype=jnp.float32) * 2.0 / scaled.shape[-1]))
    angles = position[:, None] * frequency[None, :]
    cosine = jnp.cos(angles)[:, None, :]
    sine_part = jnp.sin(angles)[:, None, :]
    lower_half = scaled[..., :half_size]
    upper_half = scaled[..., half_size:]
    rotated = jnp.concatenate(
        [
            lower_half * cosine - upper_half * sine_part,
            upper_half * cosine + lower_half * sine_part,
        ],
        axis=-1,
    )
    return rotated.astype(jnp.bfloat16)


def compact(block_rows, slots_wanted):
    live = block_rows >= 0
    ranks = jnp.cumsum(live.astype(jnp.int32), axis=1) - 1
    request_idx = jnp.arange(block_rows.shape[1], dtype=jnp.int32)[None, :]
    chosen_blocks = []
    chosen_requests = []
    for slot_num in range(slots_wanted):
        picked = live & (ranks == slot_num)
        chosen_blocks.append(jnp.sum(jnp.where(picked, block_rows, 0), axis=1))
        chosen_requests.append(jnp.sum(jnp.where(picked, request_idx, 0), axis=1))
    return (jnp.stack(chosen_blocks, axis=1), jnp.stack(chosen_requests, axis=1))


def body(
    hidden_in,
    query_in,
    key_in,
    value_in,
    query_gain,
    key_gain,
    cache_keys,
    cache_values,
    cache_block,
    request_lengths,
    out_proj,
    norm_gain,
    expert_ids,
    gate_values,
    old_slots,
    new_replicas,
    slot_weights,
):
    req_count = lax.axis_size("req")
    exp_count = lax.axis_size("exp")
    group_idx = lax.axis_index("req")
    tok_grp, width_q = query_in.shape
    tok_dev, model_width = hidden_in.shape
    head_size = query_gain.shape[0]
    head_count = width_q // head_size
    cache_dev = cache_keys.shape[0]
    pre_len = cache_keys.shape[1]
    req_grp = request_lengths.shape[1]
    lengths = request_lengths[0]
    req_ends = jnp.cumsum(lengths)
    starts = req_ends - lengths
    places = jnp.arange(tok_grp, dtype=jnp.int32)
    member = (places[:, None] >= starts[None, :]) & (places[:, None] < req_ends[None, :])
    request_idx = jnp.arange(req_grp, dtype=jnp.int32)
    segment = jnp.sum(jnp.where(member, request_idx[None, :], 0), axis=1)
    offset = places - jnp.sum(jnp.where(member, starts[None, :], 0), axis=1)
    block_rows = cache_block.reshape(req_count, req_grp)
    my_blocks = lax.dynamic_index_in_dim(block_rows, group_idx, 0, keepdims=False)
    has_cache = my_blocks >= 0
    token_cached = jnp.sum(jnp.where(member & has_cache[None, :], 1, 0), axis=1) > 0
    position = (offset + jnp.where(token_cached, pre_len, 0)).astype(jnp.float32)
    need_blocks, need_requests = compact(block_rows, cache_dev)
    my_requests = lax.dynamic_index_in_dim(need_requests, group_idx, 0, keepdims=False)
    key_width = cache_keys.shape[2]
    both = jnp.concatenate([cache_keys, cache_values], axis=-1)
    both_t = both.transpose(1, 0, 2)
    gathered = exchange_cache(both_t, need_blocks.reshape(-1).astype(jnp.int32), req_count)
    gathered = gathered.transpose(1, 0, 2)
    slot_weights, gathered = lax.optimization_barrier((slot_weights, gathered))
    far_keys = gathered[..., :key_width]
    far_values = gathered[..., key_width:]
    query_n = prepare(query_in.reshape(tok_grp, head_count, head_size), query_gain, position)
    key_n = prepare(key_in.reshape(tok_grp, head_count, head_size), key_gain, position)
    keyset = jnp.concatenate(
        [key_n, far_keys.reshape(cache_dev * pre_len, head_count, head_size)], axis=0
    )
    valueset = jnp.concatenate(
        [
            value_in.reshape(tok_grp, head_count, head_size),
            far_values.reshape(cache_dev * pre_len, head_count, head_size),
        ],
        axis=0,
    )
    key_request = jnp.concatenate([segment, jnp.repeat(my_requests, pre_len)])
    allowed = segment[:, None] == key_request[None, :]
    scores = jnp.einsum("qhd,khd->hqk", query_n, keyset, preferred_element_type=jnp.float32) * (
        1.0 / math.sqrt(head_size)
    )
    scores = jnp.where(allowed[None], scores, -1e30)
    peak = jnp.max(scores, axis=-1, keepdims=True)
    expos = jnp.exp(scores - peak)
    weights = (expos / jnp.sum(expos, axis=-1, keepdims=True)).astype(jnp.bfloat16)
    attended = jnp.einsum("hqk,khd->qhd", weights, valueset, preferred_element_type=jnp.float32)
    attended = attended.astype(jnp.bfloat16).reshape(tok_grp, width_q)
    attn_out = lax.psum_scatter(
        jnp.dot(attended, out_proj, preferred_element_type=jnp.float32),
        "exp",
        scatter_dimension=0,
        tiled=True,
    )
    residual = hidden_in.astype(jnp.float32) + attn_out
    normed = (
        residual
        * lax.rsqrt(jnp.mean(residual * residual, axis=-1, keepdims=True) + 1e-06)
        * norm_gain
    ).astype(jnp.bfloat16)
    topk_count = expert_ids.shape[1]
    slot_total = old_slots.shape[0]
    slots_here = slot_weights.shape[0]
    capacity = max(2, tok_dev * topk_count * 5 // (4 * slot_total))
    slot_range = jnp.arange(slot_total, dtype=jnp.int32)
    slot_of = jnp.sum(
        jnp.where(old_slots[None, :] == slot_range[:, None], slot_range[None, :], 0), axis=1
    )
    flat_ids = expert_ids.reshape(-1)
    onehot = flat_ids[:, None] == slot_range[None, :]
    row_slot = jnp.sum(jnp.where(onehot, slot_of[None, :], 0), axis=1)
    before = jnp.cumsum(onehot.astype(jnp.int32), axis=0) - onehot.astype(jnp.int32)
    row_rank = jnp.sum(jnp.where(onehot, before, 0), axis=1)
    target = row_slot * capacity + row_rank
    exp_idx = lax.axis_index("exp")
    pair_bit = exp_idx % 2
    pair_count = exp_count // 2
    own_part = lax.dynamic_index_in_dim(slot_weights, pair_bit, 0, keepdims=False)
    give_part = lax.dynamic_index_in_dim(slot_weights, 1 - pair_bit, 0, keepdims=False)
    swap = [(e, e ^ 1) for e in range(exp_count)]
    got_part = lax.ppermute(give_part, "exp", perm=swap)
    lanes = 128
    tile_rows = capacity * model_width // lanes

    def as_tiles(rows):
        return rows.reshape(req_count * exp_count, tile_rows, lanes)

    def as_rows(tiles):
        return tiles.reshape(req_count * exp_count * capacity, model_width)

    tile_high = model_width // lanes
    normed_tiles = normed.reshape(tok_dev, tile_high, lanes)
    row_token = jnp.arange(tok_dev * topk_count, dtype=jnp.int32) // topk_count
    source_token = jnp.zeros((slot_total * capacity,), jnp.int32).at[target].set(row_token)
    filled = jnp.zeros((slot_total * capacity,), jnp.bool_).at[target].set(True)
    outbox = jnp.where(filled[:, None, None], normed_tiles[source_token], jnp.bfloat16(0))
    outbox = outbox.reshape(req_count, 1, slots_here * tile_rows, lanes)
    copies = jnp.broadcast_to(outbox, (req_count, pair_count, slots_here * tile_rows, lanes))
    copies = copies.reshape(req_count * exp_count, tile_rows, lanes)
    half_rows = slot_weights.shape[2] // 2
    slot_range_r = jnp.arange(slot_total, dtype=jnp.int32)
    replica_onehot = new_replicas[:, None] == slot_range_r[None, :]
    source_slot = jnp.sum(jnp.where(replica_onehot, slot_of[None, :], 0), axis=1)
    spread_first = lax.all_to_all(
        slot_weights[:, :, :half_rows], "req", split_axis=2, concat_axis=0, tiled=True
    )
    copies, spread_first = lax.optimization_barrier((copies, spread_first))
    inbox = lax.all_to_all(copies, ("req", "exp"), split_axis=0, concat_axis=0, tiled=True)
    chosen_first = jnp.take(spread_first, source_slot, axis=0)
    later_weights, chosen_first, inbox = lax.optimization_barrier(
        (slot_weights, chosen_first, inbox)
    )
    replica_first = lax.all_to_all(chosen_first, "req", split_axis=0, concat_axis=2, tiled=True)
    spread_second = lax.all_to_all(
        later_weights[:, :, half_rows:], "req", split_axis=2, concat_axis=0, tiled=True
    )
    chosen_second = jnp.take(spread_second, source_slot, axis=0)
    in_rows = as_rows(inbox)
    halves = []
    for part in (own_part, got_part):
        gate_act = jnp.dot(in_rows, part[0], preferred_element_type=jnp.float32)
        up_act = jnp.dot(in_rows, part[1], preferred_element_type=jnp.float32)
        hidden = (jax.nn.silu(gate_act) * up_act).astype(jnp.bfloat16)
        piece = lax.dot_general(
            hidden, part[2], (((1,), (1,)), ((), ())), preferred_element_type=jnp.float32
        )
        halves.append(piece.astype(jnp.bfloat16).astype(jnp.float32))
    partial_value = as_tiles((halves[0] + halves[1]).astype(jnp.bfloat16))
    replica_first, partial_value = lax.optimization_barrier((replica_first, partial_value))
    returned = lax.all_to_all(
        partial_value, ("req", "exp"), split_axis=0, concat_axis=0, tiled=True
    ).reshape(req_count * exp_count * capacity, tile_high, lanes)
    chosen_second, returned = lax.optimization_barrier((chosen_second, returned))
    replica_second = lax.all_to_all(
        chosen_second, "req", split_axis=0, concat_axis=2, tiled=True
    )
    dest_req = row_slot // slots_here
    dest_pos = row_slot % slots_here
    result_rows = None
    for pair_num in range(pair_count):
        where_from = (dest_req * exp_count + pair_num * slots_here + dest_pos) * capacity + row_rank
        one = jnp.take(returned, where_from, axis=0).astype(jnp.float32)
        result_rows = one if result_rows is None else result_rows + one
    mixture = jnp.sum(
        result_rows.reshape(tok_dev, topk_count, tile_high, lanes)
        * gate_values[:, :, None, None],
        axis=1,
    )
    residual_tiles = residual.reshape(tok_dev, tile_high, lanes)
    layer_out = (residual_tiles + mixture).astype(jnp.bfloat16).reshape(tok_dev, model_width)
    replica_weights = jnp.concatenate([replica_first, replica_second], axis=2)
    return (layer_out, replica_weights)


def solution(mesh):
    in_specs = (
        P(("req", "exp"), None),
        P("req", "exp"),
        P("req", "exp"),
        P("req", "exp"),
        P(),
        P(),
        P("req", None, "exp"),
        P("req", None, "exp"),
        P(),
        P("req", None),
        P("exp", None),
        P(),
        P(("req", "exp"), None),
        P(("req", "exp"), None),
        P(),
        P(),
        P("req", None, None, "exp"),
    )
    out_specs = (P(("req", "exp"), None), P("req", None, None, "exp"))
    return jax.shard_map(body, mesh=mesh, in_specs=in_specs, out_specs=out_specs, check_vma=False)
```

```python
import functools
import math

import jax
import jax.numpy as jnp
from jax import lax
from jax.experimental import pallas as pl
from jax.experimental.pallas import tpu as pltpu
from jax.sharding import PartitionSpec as P

MESH = pl.DeviceIdType.MESH


def cache_kernel(n, need_ref, both_ref, out_ref, stage, send_buf, land, sems):
    me = lax.axis_index("req")
    ex = lax.axis_index("exp")
    barrier = pltpu.get_barrier_semaphore()

    def greet(k, carry):
        peer = lax.rem(me + k, n)
        pl.semaphore_signal(barrier, inc=1, device_id=(peer, ex), device_id_type=MESH)
        return carry

    lax.fori_loop(1, n, greet, 0)
    pl.semaphore_wait(barrier, n - 1)

    def first_copy(k, peer):
        return pltpu.make_async_remote_copy(
            src_ref=both_ref.at[peer],
            dst_ref=stage.at[me],
            send_sem=sems.at[0, k],
            recv_sem=sems.at[1, k],
            device_id=(peer, ex),
            device_id_type=MESH,
        )

    def second_copy(k, peer):
        return pltpu.make_async_remote_copy(
            src_ref=send_buf.at[k],
            dst_ref=land.at[me],
            send_sem=sems.at[2, k],
            recv_sem=sems.at[3, k],
            device_id=(peer, ex),
            device_id_type=MESH,
        )

    def send_first(k, carry):
        first_copy(k, lax.rem(me + k, n)).start()
        return carry

    lax.fori_loop(1, n, send_first, 0)
    stage[me] = both_ref[me]

    def wait_first(k, carry):
        source = lax.rem(me + n - k, n)
        pltpu.make_async_remote_copy(
            src_ref=both_ref.at[me],
            dst_ref=stage.at[source],
            send_sem=sems.at[0, k],
            recv_sem=sems.at[1, k],
            device_id=(source, ex),
            device_id_type=MESH,
        ).wait_recv()
        return carry

    lax.fori_loop(1, n, wait_first, 0)
    rows = lax.broadcasted_iota(jnp.int32, both_ref.shape[1:], 0)

    def pieces_for(dest):
        picked = []
        for c in range(2):
            block = need_ref[dest * 2 + c]
            slab = stage[block // 2].astype(jnp.float32)
            one = jnp.where(block % 2 == 0, slab[0:1], slab[1:2])
            picked.append(jnp.broadcast_to(one, slab.shape))
        return jnp.where(rows == 0, picked[0], picked[1]).astype(land.dtype)

    def send_second(k, carry):
        dest = lax.rem(me + k, n)
        send_buf[k] = pieces_for(dest)
        second_copy(k, dest).start()
        return carry

    lax.fori_loop(1, n, send_second, 0)
    land[me] = pieces_for(me)

    def wait_second(k, carry):
        source = lax.rem(me + n - k, n)
        pltpu.make_async_remote_copy(
            src_ref=send_buf.at[k],
            dst_ref=land.at[source],
            send_sem=sems.at[2, k],
            recv_sem=sems.at[3, k],
            device_id=(source, ex),
            device_id_type=MESH,
        ).wait_recv()
        first_copy(k, lax.rem(me + k, n)).wait_send()
        second_copy(k, lax.rem(me + k, n)).wait_send()
        return carry

    lax.fori_loop(1, n, wait_second, 0)
    out_ref[...] = land[...]


def exchange_cache(both_t, need_flat, n):
    shape = both_t.shape
    return pl.pallas_call(
        functools.partial(cache_kernel, n),
        out_shape=jax.ShapeDtypeStruct(shape, both_t.dtype),
        in_specs=[
            pl.BlockSpec(memory_space=pltpu.SMEM),
            pl.BlockSpec(memory_space=pltpu.VMEM),
        ],
        out_specs=pl.BlockSpec(memory_space=pltpu.VMEM),
        scratch_shapes=[
            pltpu.VMEM(shape, both_t.dtype),
            pltpu.VMEM(shape, both_t.dtype),
            pltpu.VMEM(shape, both_t.dtype),
            pltpu.SemaphoreType.DMA((4, n)),
        ],
        compiler_params=pltpu.CompilerParams(collective_id=0, has_side_effects=True),
    )(need_flat, both_t)


def prepare(values, gain, position):
    vector = values.astype(jnp.float32)
    scaled = vector * lax.rsqrt(jnp.mean(vector * vector, axis=-1, keepdims=True) + 1e-06) * gain
    half_size = scaled.shape[-1] // 2
    frequency = 10000.0 ** (-(jnp.arange(half_size, dtype=jnp.float32) * 2.0 / scaled.shape[-1]))
    angles = position[:, None] * frequency[None, :]
    cosine = jnp.cos(angles)[:, None, :]
    sine_part = jnp.sin(angles)[:, None, :]
    lower_half = scaled[..., :half_size]
    upper_half = scaled[..., half_size:]
    rotated = jnp.concatenate(
        [
            lower_half * cosine - upper_half * sine_part,
            upper_half * cosine + lower_half * sine_part,
        ],
        axis=-1,
    )
    return rotated.astype(jnp.bfloat16)


def compact(block_rows, slots_wanted):
    live = block_rows >= 0
    ranks = jnp.cumsum(live.astype(jnp.int32), axis=1) - 1
    request_idx = jnp.arange(block_rows.shape[1], dtype=jnp.int32)[None, :]
    chosen_blocks = []
    chosen_requests = []
    for slot_num in range(slots_wanted):
        picked = live & (ranks == slot_num)
        chosen_blocks.append(jnp.sum(jnp.where(picked, block_rows, 0), axis=1))
        chosen_requests.append(jnp.sum(jnp.where(picked, request_idx, 0), axis=1))
    return (jnp.stack(chosen_blocks, axis=1), jnp.stack(chosen_requests, axis=1))


def body(
    hidden_in,
    query_in,
    key_in,
    value_in,
    query_gain,
    key_gain,
    cache_keys,
    cache_values,
    cache_block,
    request_lengths,
    out_proj,
    norm_gain,
    expert_ids,
    gate_values,
    old_slots,
    new_replicas,
    slot_weights,
):
    req_count = lax.axis_size("req")
    exp_count = lax.axis_size("exp")
    group_idx = lax.axis_index("req")
    tok_grp, width_q = query_in.shape
    tok_dev, model_width = hidden_in.shape
    head_size = query_gain.shape[0]
    head_count = width_q // head_size
    cache_dev = cache_keys.shape[0]
    pre_len = cache_keys.shape[1]
    req_grp = request_lengths.shape[1]
    lengths = request_lengths[0]
    req_ends = jnp.cumsum(lengths)
    starts = req_ends - lengths
    places = jnp.arange(tok_grp, dtype=jnp.int32)
    member = (places[:, None] >= starts[None, :]) & (places[:, None] < req_ends[None, :])
    request_idx = jnp.arange(req_grp, dtype=jnp.int32)
    segment = jnp.sum(jnp.where(member, request_idx[None, :], 0), axis=1)
    offset = places - jnp.sum(jnp.where(member, starts[None, :], 0), axis=1)
    block_rows = cache_block.reshape(req_count, req_grp)
    my_blocks = lax.dynamic_index_in_dim(block_rows, group_idx, 0, keepdims=False)
    has_cache = my_blocks >= 0
    token_cached = jnp.sum(jnp.where(member & has_cache[None, :], 1, 0), axis=1) > 0
    position = (offset + jnp.where(token_cached, pre_len, 0)).astype(jnp.float32)
    need_blocks, need_requests = compact(block_rows, cache_dev)
    my_requests = lax.dynamic_index_in_dim(need_requests, group_idx, 0, keepdims=False)
    key_width = cache_keys.shape[2]
    both = jnp.concatenate([cache_keys, cache_values], axis=-1)
    both_t = both.transpose(1, 0, 2)
    gathered = exchange_cache(both_t, need_blocks.reshape(-1).astype(jnp.int32), req_count)
    gathered = gathered.transpose(1, 0, 2)
    slot_weights, gathered = lax.optimization_barrier((slot_weights, gathered))
    far_keys = gathered[..., :key_width]
    far_values = gathered[..., key_width:]
    query_n = prepare(query_in.reshape(tok_grp, head_count, head_size), query_gain, position)
    key_n = prepare(key_in.reshape(tok_grp, head_count, head_size), key_gain, position)
    keyset = jnp.concatenate(
        [key_n, far_keys.reshape(cache_dev * pre_len, head_count, head_size)], axis=0
    )
    valueset = jnp.concatenate(
        [
            value_in.reshape(tok_grp, head_count, head_size),
            far_values.reshape(cache_dev * pre_len, head_count, head_size),
        ],
        axis=0,
    )
    key_request = jnp.concatenate([segment, jnp.repeat(my_requests, pre_len)])
    allowed = segment[:, None] == key_request[None, :]
    scores = jnp.einsum("qhd,khd->hqk", query_n, keyset, preferred_element_type=jnp.float32) * (
        1.0 / math.sqrt(head_size)
    )
    scores = jnp.where(allowed[None], scores, -1e30)
    peak = jnp.max(scores, axis=-1, keepdims=True)
    expos = jnp.exp(scores - peak)
    weights = (expos / jnp.sum(expos, axis=-1, keepdims=True)).astype(jnp.bfloat16)
    attended = jnp.einsum("hqk,khd->qhd", weights, valueset, preferred_element_type=jnp.float32)
    attended = attended.astype(jnp.bfloat16).reshape(tok_grp, width_q)
    attn_out = lax.psum_scatter(
        jnp.dot(attended, out_proj, preferred_element_type=jnp.float32),
        "exp",
        scatter_dimension=0,
        tiled=True,
    )
    residual = hidden_in.astype(jnp.float32) + attn_out
    normed = (
        residual
        * lax.rsqrt(jnp.mean(residual * residual, axis=-1, keepdims=True) + 1e-06)
        * norm_gain
    ).astype(jnp.bfloat16)
    topk_count = expert_ids.shape[1]
    slot_total = old_slots.shape[0]
    slots_here = slot_weights.shape[0]
    capacity = max(2, tok_dev * topk_count * 5 // (4 * slot_total))
    slot_range = jnp.arange(slot_total, dtype=jnp.int32)
    slot_of = jnp.sum(
        jnp.where(old_slots[None, :] == slot_range[:, None], slot_range[None, :], 0), axis=1
    )
    flat_ids = expert_ids.reshape(-1)
    onehot = flat_ids[:, None] == slot_range[None, :]
    row_slot = jnp.sum(jnp.where(onehot, slot_of[None, :], 0), axis=1)
    before = jnp.cumsum(onehot.astype(jnp.int32), axis=0) - onehot.astype(jnp.int32)
    row_rank = jnp.sum(jnp.where(onehot, before, 0), axis=1)
    target = row_slot * capacity + row_rank
    exp_idx = lax.axis_index("exp")
    pair_bit = exp_idx % 2
    pair_count = exp_count // 2
    own_part = lax.dynamic_index_in_dim(slot_weights, pair_bit, 0, keepdims=False)
    give_part = lax.dynamic_index_in_dim(slot_weights, 1 - pair_bit, 0, keepdims=False)
    swap = [(e, e ^ 1) for e in range(exp_count)]
    got_part = lax.ppermute(give_part, "exp", perm=swap)
    lanes = 128
    tile_rows = capacity * model_width // lanes

    def as_tiles(rows):
        return rows.reshape(req_count * exp_count, tile_rows, lanes)

    def as_rows(tiles):
        return tiles.reshape(req_count * exp_count * capacity, model_width)

    tile_high = model_width // lanes
    normed_tiles = normed.reshape(tok_dev, tile_high, lanes)
    row_token = jnp.arange(tok_dev * topk_count, dtype=jnp.int32) // topk_count
    source_token = jnp.zeros((slot_total * capacity,), jnp.int32).at[target].set(row_token)
    filled = jnp.zeros((slot_total * capacity,), jnp.bool_).at[target].set(True)
    outbox = jnp.where(filled[:, None, None], normed_tiles[source_token], jnp.bfloat16(0))
    outbox = outbox.reshape(req_count, 1, slots_here * tile_rows, lanes)
    copies = jnp.broadcast_to(outbox, (req_count, pair_count, slots_here * tile_rows, lanes))
    copies = copies.reshape(req_count * exp_count, tile_rows, lanes)
    inbox = lax.all_to_all(copies, ("req", "exp"), split_axis=0, concat_axis=0, tiled=True)
    in_rows = as_rows(inbox)
    halves = []
    for part in (own_part, got_part):
        gate_act = jnp.dot(in_rows, part[0], preferred_element_type=jnp.float32)
        up_act = jnp.dot(in_rows, part[1], preferred_element_type=jnp.float32)
        hidden = (jax.nn.silu(gate_act) * up_act).astype(jnp.bfloat16)
        piece = lax.dot_general(
            hidden, part[2], (((1,), (1,)), ((), ())), preferred_element_type=jnp.float32
        )
        halves.append(piece.astype(jnp.bfloat16).astype(jnp.float32))
    partial_value = as_tiles((halves[0] + halves[1]).astype(jnp.bfloat16))
    returned = lax.all_to_all(
        partial_value, ("req", "exp"), split_axis=0, concat_axis=0, tiled=True
    ).reshape(req_count * exp_count * capacity, tile_high, lanes)
    dest_req = row_slot // slots_here
    dest_pos = row_slot % slots_here
    result_rows = None
    for pair_num in range(pair_count):
        where_from = (dest_req * exp_count + pair_num * slots_here + dest_pos) * capacity + row_rank
        one = jnp.take(returned, where_from, axis=0).astype(jnp.float32)
        result_rows = one if result_rows is None else result_rows + one
    mixture = jnp.sum(
        result_rows.reshape(tok_dev, topk_count, tile_high, lanes)
        * gate_values[:, :, None, None],
        axis=1,
    )
    residual_tiles = residual.reshape(tok_dev, tile_high, lanes)
    layer_out = (residual_tiles + mixture).astype(jnp.bfloat16).reshape(tok_dev, model_width)
    stacked_rows = slot_weights.shape[1] * slot_weights.shape[2]
    piece_rows = stacked_rows // req_count
    spread = [
        lax.all_to_all(
            slot_weights[c].reshape(req_count, piece_rows, slot_weights.shape[3]),
            "req",
            split_axis=0,
            concat_axis=0,
            tiled=True,
        )
        for c in range(slots_here)
    ]
    spread_slots = jnp.stack(spread, axis=1).reshape(
        slot_total, piece_rows, slot_weights.shape[3]
    )
    replica_onehot = new_replicas[:, None] == slot_range[None, :]
    source_slot = jnp.sum(jnp.where(replica_onehot, slot_of[None, :], 0), axis=1)
    chosen_pieces = jnp.take(spread_slots, source_slot, axis=0)
    replica_weights = lax.all_to_all(chosen_pieces, "req", split_axis=0, concat_axis=0, tiled=True)
    replica_weights = replica_weights.reshape((1,) + slot_weights.shape[1:])
    return (layer_out, replica_weights)


def solution(mesh):
    in_specs = (
        P(("req", "exp"), None),
        P("req", "exp"),
        P("req", "exp"),
        P("req", "exp"),
        P(),
        P(),
        P("req", None, "exp"),
        P("req", None, "exp"),
        P(),
        P("req", None),
        P("exp", None),
        P(),
        P(("req", "exp"), None),
        P(("req", "exp"), None),
        P(),
        P(),
        P("req", None, None, "exp"),
    )
    out_specs = (P(("req", "exp"), None), P("req", None, None, "exp"))
    return jax.shard_map(body, mesh=mesh, in_specs=in_specs, out_specs=out_specs, check_vma=False)
```

```python
import functools
import math

import jax
import jax.numpy as jnp
from jax import lax
from jax.experimental import pallas as pl
from jax.experimental.pallas import tpu as pltpu
from jax.sharding import PartitionSpec as P

MESH = pl.DeviceIdType.MESH


def cache_kernel(n, need_ref, both_ref, out_ref, stage, send_buf, land, sems):
    me = lax.axis_index("req")
    ex = lax.axis_index("exp")
    barrier = pltpu.get_barrier_semaphore()

    def greet(k, carry):
        peer = lax.rem(me + k, n)
        pl.semaphore_signal(barrier, inc=1, device_id=(peer, ex), device_id_type=MESH)
        return carry

    lax.fori_loop(1, n, greet, 0)
    pl.semaphore_wait(barrier, n - 1)

    def first_copy(k, peer):
        return pltpu.make_async_remote_copy(
            src_ref=both_ref.at[peer],
            dst_ref=stage.at[me],
            send_sem=sems.at[0, k],
            recv_sem=sems.at[1, k],
            device_id=(peer, ex),
            device_id_type=MESH,
        )

    def second_copy(k, peer):
        return pltpu.make_async_remote_copy(
            src_ref=send_buf.at[k],
            dst_ref=land.at[me],
            send_sem=sems.at[2, k],
            recv_sem=sems.at[3, k],
            device_id=(peer, ex),
            device_id_type=MESH,
        )

    def send_first(k, carry):
        first_copy(k, lax.rem(me + k, n)).start()
        return carry

    lax.fori_loop(1, n, send_first, 0)
    stage[me] = both_ref[me]

    def wait_first(k, carry):
        source = lax.rem(me + n - k, n)
        pltpu.make_async_remote_copy(
            src_ref=both_ref.at[me],
            dst_ref=stage.at[source],
            send_sem=sems.at[0, k],
            recv_sem=sems.at[1, k],
            device_id=(source, ex),
            device_id_type=MESH,
        ).wait_recv()
        return carry

    lax.fori_loop(1, n, wait_first, 0)
    rows = lax.broadcasted_iota(jnp.int32, both_ref.shape[1:], 0)

    def pieces_for(dest):
        picked = []
        for c in range(2):
            block = need_ref[dest * 2 + c]
            slab = stage[block // 2].astype(jnp.float32)
            one = jnp.where(block % 2 == 0, slab[0:1], slab[1:2])
            picked.append(jnp.broadcast_to(one, slab.shape))
        return jnp.where(rows == 0, picked[0], picked[1]).astype(land.dtype)

    def send_second(k, carry):
        dest = lax.rem(me + k, n)
        send_buf[k] = pieces_for(dest)
        second_copy(k, dest).start()
        return carry

    lax.fori_loop(1, n, send_second, 0)
    land[me] = pieces_for(me)

    def wait_second(k, carry):
        source = lax.rem(me + n - k, n)
        pltpu.make_async_remote_copy(
            src_ref=send_buf.at[k],
            dst_ref=land.at[source],
            send_sem=sems.at[2, k],
            recv_sem=sems.at[3, k],
            device_id=(source, ex),
            device_id_type=MESH,
        ).wait_recv()
        first_copy(k, lax.rem(me + k, n)).wait_send()
        second_copy(k, lax.rem(me + k, n)).wait_send()
        return carry

    lax.fori_loop(1, n, wait_second, 0)
    out_ref[...] = land[...]


def exchange_cache(both_t, need_flat, n):
    shape = both_t.shape
    return pl.pallas_call(
        functools.partial(cache_kernel, n),
        out_shape=jax.ShapeDtypeStruct(shape, both_t.dtype),
        in_specs=[
            pl.BlockSpec(memory_space=pltpu.SMEM),
            pl.BlockSpec(memory_space=pltpu.VMEM),
        ],
        out_specs=pl.BlockSpec(memory_space=pltpu.VMEM),
        scratch_shapes=[
            pltpu.VMEM(shape, both_t.dtype),
            pltpu.VMEM(shape, both_t.dtype),
            pltpu.VMEM(shape, both_t.dtype),
            pltpu.SemaphoreType.DMA((4, n)),
        ],
        compiler_params=pltpu.CompilerParams(collective_id=0, has_side_effects=True),
    )(need_flat, both_t)


def prepare(values, gain, position):
    vector = values.astype(jnp.float32)
    scaled = vector * lax.rsqrt(jnp.mean(vector * vector, axis=-1, keepdims=True) + 1e-06) * gain
    half_size = scaled.shape[-1] // 2
    frequency = 10000.0 ** (-(jnp.arange(half_size, dtype=jnp.float32) * 2.0 / scaled.shape[-1]))
    angles = position[:, None] * frequency[None, :]
    cosine = jnp.cos(angles)[:, None, :]
    sine_part = jnp.sin(angles)[:, None, :]
    lower_half = scaled[..., :half_size]
    upper_half = scaled[..., half_size:]
    rotated = jnp.concatenate(
        [
            lower_half * cosine - upper_half * sine_part,
            upper_half * cosine + lower_half * sine_part,
        ],
        axis=-1,
    )
    return rotated.astype(jnp.bfloat16)


def compact(block_rows, slots_wanted):
    live = block_rows >= 0
    ranks = jnp.cumsum(live.astype(jnp.int32), axis=1) - 1
    request_idx = jnp.arange(block_rows.shape[1], dtype=jnp.int32)[None, :]
    chosen_blocks = []
    chosen_requests = []
    for slot_num in range(slots_wanted):
        picked = live & (ranks == slot_num)
        chosen_blocks.append(jnp.sum(jnp.where(picked, block_rows, 0), axis=1))
        chosen_requests.append(jnp.sum(jnp.where(picked, request_idx, 0), axis=1))
    return (jnp.stack(chosen_blocks, axis=1), jnp.stack(chosen_requests, axis=1))


def body(
    hidden_in,
    query_in,
    key_in,
    value_in,
    query_gain,
    key_gain,
    cache_keys,
    cache_values,
    cache_block,
    request_lengths,
    out_proj,
    norm_gain,
    expert_ids,
    gate_values,
    old_slots,
    new_replicas,
    slot_weights,
):
    req_count = lax.axis_size("req")
    exp_count = lax.axis_size("exp")
    group_idx = lax.axis_index("req")
    tok_grp, width_q = query_in.shape
    tok_dev, model_width = hidden_in.shape
    head_size = query_gain.shape[0]
    head_count = width_q // head_size
    cache_dev = cache_keys.shape[0]
    pre_len = cache_keys.shape[1]
    req_grp = request_lengths.shape[1]
    lengths = request_lengths[0]
    req_ends = jnp.cumsum(lengths)
    starts = req_ends - lengths
    places = jnp.arange(tok_grp, dtype=jnp.int32)
    member = (places[:, None] >= starts[None, :]) & (places[:, None] < req_ends[None, :])
    request_idx = jnp.arange(req_grp, dtype=jnp.int32)
    segment = jnp.sum(jnp.where(member, request_idx[None, :], 0), axis=1)
    offset = places - jnp.sum(jnp.where(member, starts[None, :], 0), axis=1)
    block_rows = cache_block.reshape(req_count, req_grp)
    my_blocks = lax.dynamic_index_in_dim(block_rows, group_idx, 0, keepdims=False)
    has_cache = my_blocks >= 0
    token_cached = jnp.sum(jnp.where(member & has_cache[None, :], 1, 0), axis=1) > 0
    position = (offset + jnp.where(token_cached, pre_len, 0)).astype(jnp.float32)
    need_blocks, need_requests = compact(block_rows, cache_dev)
    my_requests = lax.dynamic_index_in_dim(need_requests, group_idx, 0, keepdims=False)
    key_width = cache_keys.shape[2]
    both = jnp.concatenate([cache_keys, cache_values], axis=-1)
    both_t = both.transpose(1, 0, 2)
    gathered = exchange_cache(both_t, need_blocks.reshape(-1).astype(jnp.int32), req_count)
    gathered = gathered.transpose(1, 0, 2)
    slot_weights, gathered = lax.optimization_barrier((slot_weights, gathered))
    far_keys = gathered[..., :key_width]
    far_values = gathered[..., key_width:]
    query_n = prepare(query_in.reshape(tok_grp, head_count, head_size), query_gain, position)
    key_n = prepare(key_in.reshape(tok_grp, head_count, head_size), key_gain, position)
    keyset = jnp.concatenate(
        [key_n, far_keys.reshape(cache_dev * pre_len, head_count, head_size)], axis=0
    )
    valueset = jnp.concatenate(
        [
            value_in.reshape(tok_grp, head_count, head_size),
            far_values.reshape(cache_dev * pre_len, head_count, head_size),
        ],
        axis=0,
    )
    key_request = jnp.concatenate([segment, jnp.repeat(my_requests, pre_len)])
    allowed = segment[:, None] == key_request[None, :]
    scores = jnp.einsum("qhd,khd->hqk", query_n, keyset, preferred_element_type=jnp.float32) * (
        1.0 / math.sqrt(head_size)
    )
    scores = jnp.where(allowed[None], scores, -1e30)
    peak = jnp.max(scores, axis=-1, keepdims=True)
    expos = jnp.exp(scores - peak)
    weights = (expos / jnp.sum(expos, axis=-1, keepdims=True)).astype(jnp.bfloat16)
    attended = jnp.einsum("hqk,khd->qhd", weights, valueset, preferred_element_type=jnp.float32)
    attended = attended.astype(jnp.bfloat16).reshape(tok_grp, width_q)
    attn_out = lax.psum_scatter(
        jnp.dot(attended, out_proj, preferred_element_type=jnp.float32),
        "exp",
        scatter_dimension=0,
        tiled=True,
    )
    residual = hidden_in.astype(jnp.float32) + attn_out
    normed = (
        residual
        * lax.rsqrt(jnp.mean(residual * residual, axis=-1, keepdims=True) + 1e-06)
        * norm_gain
    ).astype(jnp.bfloat16)
    topk_count = expert_ids.shape[1]
    slot_total = old_slots.shape[0]
    slots_here = slot_weights.shape[0]
    capacity = max(2, tok_dev * topk_count * 5 // (4 * slot_total))
    slot_range = jnp.arange(slot_total, dtype=jnp.int32)
    slot_of = jnp.sum(
        jnp.where(old_slots[None, :] == slot_range[:, None], slot_range[None, :], 0), axis=1
    )
    flat_ids = expert_ids.reshape(-1)
    onehot = flat_ids[:, None] == slot_range[None, :]
    row_slot = jnp.sum(jnp.where(onehot, slot_of[None, :], 0), axis=1)
    before = jnp.cumsum(onehot.astype(jnp.int32), axis=0) - onehot.astype(jnp.int32)
    row_rank = jnp.sum(jnp.where(onehot, before, 0), axis=1)
    target = row_slot * capacity + row_rank
    exp_idx = lax.axis_index("exp")
    pair_bit = exp_idx % 2
    pair_count = exp_count // 2
    own_part = lax.dynamic_index_in_dim(slot_weights, pair_bit, 0, keepdims=False)
    give_part = lax.dynamic_index_in_dim(slot_weights, 1 - pair_bit, 0, keepdims=False)
    swap = [(e, e ^ 1) for e in range(exp_count)]
    got_part = lax.ppermute(give_part, "exp", perm=swap)
    lanes = 128
    tile_rows = capacity * model_width // lanes

    def as_tiles(rows):
        return rows.reshape(req_count * exp_count, tile_rows, lanes)

    def as_rows(tiles):
        return tiles.reshape(req_count * exp_count * capacity, model_width)

    tile_high = model_width // lanes
    normed_tiles = normed.reshape(tok_dev, tile_high, lanes)
    row_token = jnp.arange(tok_dev * topk_count, dtype=jnp.int32) // topk_count
    source_token = jnp.zeros((slot_total * capacity,), jnp.int32).at[target].set(row_token)
    filled = jnp.zeros((slot_total * capacity,), jnp.bool_).at[target].set(True)
    per_req = slots_here * capacity
    copy_token = jnp.broadcast_to(
        source_token.reshape(req_count, 1, per_req), (req_count, pair_count, per_req)
    )
    copy_filled = jnp.broadcast_to(
        filled.reshape(req_count, 1, per_req), (req_count, pair_count, per_req)
    )
    copies = jnp.where(
        copy_filled[..., None, None], normed_tiles[copy_token], jnp.bfloat16(0)
    )
    copies = copies.reshape(req_count * exp_count, tile_rows, lanes)
    inbox = lax.all_to_all(copies, ("req", "exp"), split_axis=0, concat_axis=0, tiled=True)
    in_rows = as_rows(inbox)
    halves = []
    for part in (own_part, got_part):
        gate_act = jnp.dot(in_rows, part[0], preferred_element_type=jnp.float32)
        up_act = jnp.dot(in_rows, part[1], preferred_element_type=jnp.float32)
        hidden = (jax.nn.silu(gate_act) * up_act).astype(jnp.bfloat16)
        piece = lax.dot_general(
            hidden, part[2], (((1,), (1,)), ((), ())), preferred_element_type=jnp.float32
        )
        halves.append(piece.astype(jnp.bfloat16).astype(jnp.float32))
    partial_value = as_tiles((halves[0] + halves[1]).astype(jnp.bfloat16))
    returned = lax.all_to_all(
        partial_value, ("req", "exp"), split_axis=0, concat_axis=0, tiled=True
    ).reshape(req_count * exp_count * capacity, tile_high, lanes)
    dest_req = row_slot // slots_here
    dest_pos = row_slot % slots_here
    result_rows = None
    for pair_num in range(pair_count):
        where_from = (dest_req * exp_count + pair_num * slots_here + dest_pos) * capacity + row_rank
        one = jnp.take(returned, where_from, axis=0).astype(jnp.float32)
        result_rows = one if result_rows is None else result_rows + one
    mixture = jnp.sum(
        result_rows.reshape(tok_dev, topk_count, tile_high, lanes)
        * gate_values[:, :, None, None],
        axis=1,
    )
    residual_tiles = residual.reshape(tok_dev, tile_high, lanes)
    layer_out = (residual_tiles + mixture).astype(jnp.bfloat16).reshape(tok_dev, model_width)
    stacked_rows = slot_weights.shape[1] * slot_weights.shape[2]
    piece_rows = stacked_rows // req_count
    spread = [
        lax.all_to_all(
            slot_weights[c].reshape(req_count, piece_rows, slot_weights.shape[3]),
            "req",
            split_axis=0,
            concat_axis=0,
            tiled=True,
        )
        for c in range(slots_here)
    ]
    spread_slots = jnp.stack(spread, axis=1).reshape(
        slot_total, piece_rows, slot_weights.shape[3]
    )
    replica_onehot = new_replicas[:, None] == slot_range[None, :]
    source_slot = jnp.sum(jnp.where(replica_onehot, slot_of[None, :], 0), axis=1)
    chosen_pieces = jnp.take(spread_slots, source_slot, axis=0)
    replica_weights = lax.all_to_all(chosen_pieces, "req", split_axis=0, concat_axis=0, tiled=True)
    replica_weights = replica_weights.reshape((1,) + slot_weights.shape[1:])
    return (layer_out, replica_weights)


def solution(mesh):
    in_specs = (
        P(("req", "exp"), None),
        P("req", "exp"),
        P("req", "exp"),
        P("req", "exp"),
        P(),
        P(),
        P("req", None, "exp"),
        P("req", None, "exp"),
        P(),
        P("req", None),
        P("exp", None),
        P(),
        P(("req", "exp"), None),
        P(("req", "exp"), None),
        P(),
        P(),
        P("req", None, None, "exp"),
    )
    out_specs = (P(("req", "exp"), None), P("req", None, None, "exp"))
    return jax.shard_map(body, mesh=mesh, in_specs=in_specs, out_specs=out_specs, check_vma=False)
```

```python
import functools
import math

import jax
import jax.numpy as jnp
from jax import lax
from jax.experimental import pallas as pl
from jax.experimental.pallas import tpu as pltpu
from jax.sharding import PartitionSpec as P

MESH = pl.DeviceIdType.MESH


def cache_kernel(n, need_ref, both_ref, out_ref, stage, send_buf, land, sems):
    me = lax.axis_index("req")
    ex = lax.axis_index("exp")
    barrier = pltpu.get_barrier_semaphore()

    def greet(k, carry):
        peer = lax.rem(me + k, n)
        pl.semaphore_signal(barrier, inc=1, device_id=(peer, ex), device_id_type=MESH)
        return carry

    lax.fori_loop(1, n, greet, 0)
    pl.semaphore_wait(barrier, n - 1)

    def first_copy(k, peer):
        return pltpu.make_async_remote_copy(
            src_ref=both_ref.at[peer],
            dst_ref=stage.at[me],
            send_sem=sems.at[0, k],
            recv_sem=sems.at[1, k],
            device_id=(peer, ex),
            device_id_type=MESH,
        )

    def second_copy(k, peer):
        return pltpu.make_async_remote_copy(
            src_ref=send_buf.at[k],
            dst_ref=land.at[me],
            send_sem=sems.at[2, k],
            recv_sem=sems.at[3, k],
            device_id=(peer, ex),
            device_id_type=MESH,
        )

    def send_first(k, carry):
        first_copy(k, lax.rem(me + k, n)).start()
        return carry

    lax.fori_loop(1, n, send_first, 0)
    stage[me] = both_ref[me]

    def wait_first(k, carry):
        source = lax.rem(me + n - k, n)
        pltpu.make_async_remote_copy(
            src_ref=both_ref.at[me],
            dst_ref=stage.at[source],
            send_sem=sems.at[0, k],
            recv_sem=sems.at[1, k],
            device_id=(source, ex),
            device_id_type=MESH,
        ).wait_recv()
        return carry

    lax.fori_loop(1, n, wait_first, 0)
    rows = lax.broadcasted_iota(jnp.int32, both_ref.shape[1:], 0)

    def pieces_for(dest):
        picked = []
        for c in range(2):
            block = need_ref[dest * 2 + c]
            slab = stage[block // 2].astype(jnp.float32)
            one = jnp.where(block % 2 == 0, slab[0:1], slab[1:2])
            picked.append(jnp.broadcast_to(one, slab.shape))
        return jnp.where(rows == 0, picked[0], picked[1]).astype(land.dtype)

    def send_second(k, carry):
        dest = lax.rem(me + k, n)
        send_buf[k] = pieces_for(dest)
        second_copy(k, dest).start()
        return carry

    lax.fori_loop(1, n, send_second, 0)
    land[me] = pieces_for(me)

    def wait_second(k, carry):
        source = lax.rem(me + n - k, n)
        pltpu.make_async_remote_copy(
            src_ref=send_buf.at[k],
            dst_ref=land.at[source],
            send_sem=sems.at[2, k],
            recv_sem=sems.at[3, k],
            device_id=(source, ex),
            device_id_type=MESH,
        ).wait_recv()
        first_copy(k, lax.rem(me + k, n)).wait_send()
        second_copy(k, lax.rem(me + k, n)).wait_send()
        return carry

    lax.fori_loop(1, n, wait_second, 0)
    out_ref[...] = land[...]


def exchange_cache(both_t, need_flat, n):
    shape = both_t.shape
    return pl.pallas_call(
        functools.partial(cache_kernel, n),
        out_shape=jax.ShapeDtypeStruct(shape, both_t.dtype),
        in_specs=[
            pl.BlockSpec(memory_space=pltpu.SMEM),
            pl.BlockSpec(memory_space=pltpu.VMEM),
        ],
        out_specs=pl.BlockSpec(memory_space=pltpu.VMEM),
        scratch_shapes=[
            pltpu.VMEM(shape, both_t.dtype),
            pltpu.VMEM(shape, both_t.dtype),
            pltpu.VMEM(shape, both_t.dtype),
            pltpu.SemaphoreType.DMA((4, n)),
        ],
        compiler_params=pltpu.CompilerParams(collective_id=0, has_side_effects=True),
    )(need_flat, both_t)


def prepare(values, gain, position):
    vector = values.astype(jnp.float32)
    scaled = vector * lax.rsqrt(jnp.mean(vector * vector, axis=-1, keepdims=True) + 1e-06) * gain
    half_size = scaled.shape[-1] // 2
    frequency = 10000.0 ** (-(jnp.arange(half_size, dtype=jnp.float32) * 2.0 / scaled.shape[-1]))
    angles = position[:, None] * frequency[None, :]
    cosine = jnp.cos(angles)[:, None, :]
    sine_part = jnp.sin(angles)[:, None, :]
    lower_half = scaled[..., :half_size]
    upper_half = scaled[..., half_size:]
    rotated = jnp.concatenate(
        [
            lower_half * cosine - upper_half * sine_part,
            upper_half * cosine + lower_half * sine_part,
        ],
        axis=-1,
    )
    return rotated.astype(jnp.bfloat16)


def compact(block_rows, slots_wanted):
    live = block_rows >= 0
    ranks = jnp.cumsum(live.astype(jnp.int32), axis=1) - 1
    request_idx = jnp.arange(block_rows.shape[1], dtype=jnp.int32)[None, :]
    chosen_blocks = []
    chosen_requests = []
    for slot_num in range(slots_wanted):
        picked = live & (ranks == slot_num)
        chosen_blocks.append(jnp.sum(jnp.where(picked, block_rows, 0), axis=1))
        chosen_requests.append(jnp.sum(jnp.where(picked, request_idx, 0), axis=1))
    return (jnp.stack(chosen_blocks, axis=1), jnp.stack(chosen_requests, axis=1))


def body(
    hidden_in,
    query_in,
    key_in,
    value_in,
    query_gain,
    key_gain,
    cache_keys,
    cache_values,
    cache_block,
    request_lengths,
    out_proj,
    norm_gain,
    expert_ids,
    gate_values,
    old_slots,
    new_replicas,
    slot_weights,
):
    req_count = lax.axis_size("req")
    exp_count = lax.axis_size("exp")
    group_idx = lax.axis_index("req")
    tok_grp, width_q = query_in.shape
    tok_dev, model_width = hidden_in.shape
    head_size = query_gain.shape[0]
    head_count = width_q // head_size
    cache_dev = cache_keys.shape[0]
    pre_len = cache_keys.shape[1]
    req_grp = request_lengths.shape[1]
    lengths = request_lengths[0]
    req_ends = jnp.cumsum(lengths)
    starts = req_ends - lengths
    places = jnp.arange(tok_grp, dtype=jnp.int32)
    member = (places[:, None] >= starts[None, :]) & (places[:, None] < req_ends[None, :])
    request_idx = jnp.arange(req_grp, dtype=jnp.int32)
    segment = jnp.sum(jnp.where(member, request_idx[None, :], 0), axis=1)
    offset = places - jnp.sum(jnp.where(member, starts[None, :], 0), axis=1)
    block_rows = cache_block.reshape(req_count, req_grp)
    my_blocks = lax.dynamic_index_in_dim(block_rows, group_idx, 0, keepdims=False)
    has_cache = my_blocks >= 0
    token_cached = jnp.sum(jnp.where(member & has_cache[None, :], 1, 0), axis=1) > 0
    position = (offset + jnp.where(token_cached, pre_len, 0)).astype(jnp.float32)
    need_blocks, need_requests = compact(block_rows, cache_dev)
    my_requests = lax.dynamic_index_in_dim(need_requests, group_idx, 0, keepdims=False)
    key_width = cache_keys.shape[2]
    both = jnp.concatenate([cache_keys, cache_values], axis=-1)
    both_t = both.transpose(1, 0, 2)
    gathered = exchange_cache(both_t, need_blocks.reshape(-1).astype(jnp.int32), req_count)
    gathered = gathered.transpose(1, 0, 2)
    slot_weights, gathered = lax.optimization_barrier((slot_weights, gathered))
    far_keys = gathered[..., :key_width]
    far_values = gathered[..., key_width:]
    query_n = prepare(query_in.reshape(tok_grp, head_count, head_size), query_gain, position)
    key_n = prepare(key_in.reshape(tok_grp, head_count, head_size), key_gain, position)
    keyset = jnp.concatenate(
        [key_n, far_keys.reshape(cache_dev * pre_len, head_count, head_size)], axis=0
    )
    valueset = jnp.concatenate(
        [
            value_in.reshape(tok_grp, head_count, head_size),
            far_values.reshape(cache_dev * pre_len, head_count, head_size),
        ],
        axis=0,
    )
    key_request = jnp.concatenate([segment, jnp.repeat(my_requests, pre_len)])
    allowed = segment[:, None] == key_request[None, :]
    scores = jnp.einsum("qhd,khd->hqk", query_n, keyset, preferred_element_type=jnp.float32) * (
        1.0 / math.sqrt(head_size)
    )
    scores = jnp.where(allowed[None], scores, -1e30)
    peak = jnp.max(scores, axis=-1, keepdims=True)
    expos = jnp.exp(scores - peak)
    weights = (expos / jnp.sum(expos, axis=-1, keepdims=True)).astype(jnp.bfloat16)
    attended = jnp.einsum("hqk,khd->qhd", weights, valueset, preferred_element_type=jnp.float32)
    attended = attended.astype(jnp.bfloat16).reshape(tok_grp, width_q)
    attn_out = lax.psum_scatter(
        jnp.dot(attended, out_proj, preferred_element_type=jnp.float32),
        "exp",
        scatter_dimension=0,
        tiled=True,
    )
    residual = hidden_in.astype(jnp.float32) + attn_out
    normed = (
        residual
        * lax.rsqrt(jnp.mean(residual * residual, axis=-1, keepdims=True) + 1e-06)
        * norm_gain
    ).astype(jnp.bfloat16)
    topk_count = expert_ids.shape[1]
    slot_total = old_slots.shape[0]
    slots_here = slot_weights.shape[0]
    capacity = max(2, tok_dev * topk_count * 5 // (4 * slot_total))
    slot_range = jnp.arange(slot_total, dtype=jnp.int32)
    slot_of = jnp.sum(
        jnp.where(old_slots[None, :] == slot_range[:, None], slot_range[None, :], 0), axis=1
    )
    flat_ids = expert_ids.reshape(-1)
    onehot = flat_ids[:, None] == slot_range[None, :]
    row_slot = jnp.sum(jnp.where(onehot, slot_of[None, :], 0), axis=1)
    before = jnp.cumsum(onehot.astype(jnp.int32), axis=0) - onehot.astype(jnp.int32)
    row_rank = jnp.sum(jnp.where(onehot, before, 0), axis=1)
    target = row_slot * capacity + row_rank
    exp_idx = lax.axis_index("exp")
    pair_bit = exp_idx % 2
    pair_count = exp_count // 2
    own_part = lax.dynamic_index_in_dim(slot_weights, pair_bit, 0, keepdims=False)
    give_part = lax.dynamic_index_in_dim(slot_weights, 1 - pair_bit, 0, keepdims=False)
    swap = [(e, e ^ 1) for e in range(exp_count)]
    got_part = lax.ppermute(give_part, "exp", perm=swap)
    lanes = 128
    tile_rows = capacity * model_width // lanes

    def as_tiles(rows):
        return rows.reshape(req_count * exp_count, tile_rows, lanes)

    def as_rows(tiles):
        return tiles.reshape(req_count * exp_count * capacity, model_width)

    tile_high = model_width // lanes
    normed_tiles = normed.reshape(tok_dev, tile_high, lanes)
    row_token = jnp.arange(tok_dev * topk_count, dtype=jnp.int32) // topk_count
    source_token = jnp.zeros((slot_total * capacity,), jnp.int32).at[target].set(row_token)
    filled = jnp.zeros((slot_total * capacity,), jnp.bool_).at[target].set(True)
    per_req = slots_here * capacity
    copy_token = jnp.broadcast_to(
        source_token.reshape(req_count, 1, per_req), (req_count, pair_count, per_req)
    )
    copy_filled = jnp.broadcast_to(
        filled.reshape(req_count, 1, per_req), (req_count, pair_count, per_req)
    )
    copies = jnp.where(
        copy_filled[..., None, None], normed_tiles[copy_token], jnp.bfloat16(0)
    )
    copies = copies.reshape(req_count * exp_count, tile_rows, lanes)
    got_part, copies = lax.optimization_barrier((got_part, copies))
    inbox = lax.all_to_all(copies, ("req", "exp"), split_axis=0, concat_axis=0, tiled=True)
    in_rows = as_rows(inbox)
    halves = []
    for part in (own_part, got_part):
        gate_act = jnp.dot(in_rows, part[0], preferred_element_type=jnp.float32)
        up_act = jnp.dot(in_rows, part[1], preferred_element_type=jnp.float32)
        hidden = (jax.nn.silu(gate_act) * up_act).astype(jnp.bfloat16)
        piece = lax.dot_general(
            hidden, part[2], (((1,), (1,)), ((), ())), preferred_element_type=jnp.float32
        )
        halves.append(piece.astype(jnp.bfloat16).astype(jnp.float32))
    partial_value = as_tiles((halves[0] + halves[1]).astype(jnp.bfloat16))
    returned = lax.all_to_all(
        partial_value, ("req", "exp"), split_axis=0, concat_axis=0, tiled=True
    ).reshape(req_count * exp_count * capacity, tile_high, lanes)
    dest_req = row_slot // slots_here
    dest_pos = row_slot % slots_here
    result_rows = None
    for pair_num in range(pair_count):
        where_from = (dest_req * exp_count + pair_num * slots_here + dest_pos) * capacity + row_rank
        one = jnp.take(returned, where_from, axis=0).astype(jnp.float32)
        result_rows = one if result_rows is None else result_rows + one
    mixture = jnp.sum(
        result_rows.reshape(tok_dev, topk_count, tile_high, lanes)
        * gate_values[:, :, None, None],
        axis=1,
    )
    residual_tiles = residual.reshape(tok_dev, tile_high, lanes)
    layer_out = (residual_tiles + mixture).astype(jnp.bfloat16).reshape(tok_dev, model_width)
    stacked_rows = slot_weights.shape[1] * slot_weights.shape[2]
    piece_rows = stacked_rows // req_count
    spread = [
        lax.all_to_all(
            slot_weights[c].reshape(req_count, piece_rows, slot_weights.shape[3]),
            "req",
            split_axis=0,
            concat_axis=0,
            tiled=True,
        )
        for c in range(slots_here)
    ]
    spread_slots = jnp.stack(spread, axis=1).reshape(
        slot_total, piece_rows, slot_weights.shape[3]
    )
    replica_onehot = new_replicas[:, None] == slot_range[None, :]
    source_slot = jnp.sum(jnp.where(replica_onehot, slot_of[None, :], 0), axis=1)
    chosen_pieces = jnp.take(spread_slots, source_slot, axis=0)
    replica_weights = lax.all_to_all(chosen_pieces, "req", split_axis=0, concat_axis=0, tiled=True)
    replica_weights = replica_weights.reshape((1,) + slot_weights.shape[1:])
    return (layer_out, replica_weights)


def solution(mesh):
    in_specs = (
        P(("req", "exp"), None),
        P("req", "exp"),
        P("req", "exp"),
        P("req", "exp"),
        P(),
        P(),
        P("req", None, "exp"),
        P("req", None, "exp"),
        P(),
        P("req", None),
        P("exp", None),
        P(),
        P(("req", "exp"), None),
        P(("req", "exp"), None),
        P(),
        P(),
        P("req", None, None, "exp"),
    )
    out_specs = (P(("req", "exp"), None), P("req", None, None, "exp"))
    return jax.shard_map(body, mesh=mesh, in_specs=in_specs, out_specs=out_specs, check_vma=False)
```

```python
import functools
import math

import jax
import jax.numpy as jnp
from jax import lax
from jax.experimental import pallas as pl
from jax.experimental.pallas import tpu as pltpu
from jax.sharding import PartitionSpec as P

MESH = pl.DeviceIdType.MESH


def cache_kernel(n, need_ref, both_ref, out_ref, stage, send_buf, land, sems):
    me = lax.axis_index("req")
    ex = lax.axis_index("exp")
    barrier = pltpu.get_barrier_semaphore()

    def greet(k, carry):
        peer = lax.rem(me + k, n)
        pl.semaphore_signal(barrier, inc=1, device_id=(peer, ex), device_id_type=MESH)
        return carry

    lax.fori_loop(1, n, greet, 0)
    pl.semaphore_wait(barrier, n - 1)

    def first_copy(k, peer):
        return pltpu.make_async_remote_copy(
            src_ref=both_ref.at[peer],
            dst_ref=stage.at[me],
            send_sem=sems.at[0, k],
            recv_sem=sems.at[1, k],
            device_id=(peer, ex),
            device_id_type=MESH,
        )

    def second_copy(k, peer):
        return pltpu.make_async_remote_copy(
            src_ref=send_buf.at[k],
            dst_ref=land.at[me],
            send_sem=sems.at[2, k],
            recv_sem=sems.at[3, k],
            device_id=(peer, ex),
            device_id_type=MESH,
        )

    def send_first(k, carry):
        first_copy(k, lax.rem(me + k, n)).start()
        return carry

    lax.fori_loop(1, n, send_first, 0)
    stage[me] = both_ref[me]

    def wait_first(k, carry):
        source = lax.rem(me + n - k, n)
        pltpu.make_async_remote_copy(
            src_ref=both_ref.at[me],
            dst_ref=stage.at[source],
            send_sem=sems.at[0, k],
            recv_sem=sems.at[1, k],
            device_id=(source, ex),
            device_id_type=MESH,
        ).wait_recv()
        return carry

    lax.fori_loop(1, n, wait_first, 0)
    rows = lax.broadcasted_iota(jnp.int32, both_ref.shape[1:], 0)

    def pieces_for(dest):
        picked = []
        for c in range(2):
            block = need_ref[dest * 2 + c]
            slab = stage[block // 2].astype(jnp.float32)
            one = jnp.where(block % 2 == 0, slab[0:1], slab[1:2])
            picked.append(jnp.broadcast_to(one, slab.shape))
        return jnp.where(rows == 0, picked[0], picked[1]).astype(land.dtype)

    def send_second(k, carry):
        dest = lax.rem(me + k, n)
        send_buf[k] = pieces_for(dest)
        second_copy(k, dest).start()
        return carry

    lax.fori_loop(1, n, send_second, 0)
    land[me] = pieces_for(me)

    def wait_second(k, carry):
        source = lax.rem(me + n - k, n)
        pltpu.make_async_remote_copy(
            src_ref=send_buf.at[k],
            dst_ref=land.at[source],
            send_sem=sems.at[2, k],
            recv_sem=sems.at[3, k],
            device_id=(source, ex),
            device_id_type=MESH,
        ).wait_recv()
        first_copy(k, lax.rem(me + k, n)).wait_send()
        second_copy(k, lax.rem(me + k, n)).wait_send()
        return carry

    lax.fori_loop(1, n, wait_second, 0)
    out_ref[...] = land[...]


def exchange_cache(both_t, need_flat, n):
    shape = both_t.shape
    return pl.pallas_call(
        functools.partial(cache_kernel, n),
        out_shape=jax.ShapeDtypeStruct(shape, both_t.dtype),
        in_specs=[
            pl.BlockSpec(memory_space=pltpu.SMEM),
            pl.BlockSpec(memory_space=pltpu.VMEM),
        ],
        out_specs=pl.BlockSpec(memory_space=pltpu.VMEM),
        scratch_shapes=[
            pltpu.VMEM(shape, both_t.dtype),
            pltpu.VMEM(shape, both_t.dtype),
            pltpu.VMEM(shape, both_t.dtype),
            pltpu.SemaphoreType.DMA((4, n)),
        ],
        compiler_params=pltpu.CompilerParams(collective_id=0, has_side_effects=True),
    )(need_flat, both_t)


def prepare(values, gain, position):
    vector = values.astype(jnp.float32)
    scaled = vector * lax.rsqrt(jnp.mean(vector * vector, axis=-1, keepdims=True) + 1e-06) * gain
    half_size = scaled.shape[-1] // 2
    frequency = 10000.0 ** (-(jnp.arange(half_size, dtype=jnp.float32) * 2.0 / scaled.shape[-1]))
    angles = position[:, None] * frequency[None, :]
    cosine = jnp.cos(angles)[:, None, :]
    sine_part = jnp.sin(angles)[:, None, :]
    lower_half = scaled[..., :half_size]
    upper_half = scaled[..., half_size:]
    rotated = jnp.concatenate(
        [
            lower_half * cosine - upper_half * sine_part,
            upper_half * cosine + lower_half * sine_part,
        ],
        axis=-1,
    )
    return rotated.astype(jnp.bfloat16)


def compact(block_rows, slots_wanted):
    live = block_rows >= 0
    ranks = jnp.cumsum(live.astype(jnp.int32), axis=1) - 1
    request_idx = jnp.arange(block_rows.shape[1], dtype=jnp.int32)[None, :]
    chosen_blocks = []
    chosen_requests = []
    for slot_num in range(slots_wanted):
        picked = live & (ranks == slot_num)
        chosen_blocks.append(jnp.sum(jnp.where(picked, block_rows, 0), axis=1))
        chosen_requests.append(jnp.sum(jnp.where(picked, request_idx, 0), axis=1))
    return (jnp.stack(chosen_blocks, axis=1), jnp.stack(chosen_requests, axis=1))


def body(
    hidden_in,
    query_in,
    key_in,
    value_in,
    query_gain,
    key_gain,
    cache_keys,
    cache_values,
    cache_block,
    request_lengths,
    out_proj,
    norm_gain,
    expert_ids,
    gate_values,
    old_slots,
    new_replicas,
    slot_weights,
):
    req_count = lax.axis_size("req")
    exp_count = lax.axis_size("exp")
    group_idx = lax.axis_index("req")
    tok_grp, width_q = query_in.shape
    tok_dev, model_width = hidden_in.shape
    head_size = query_gain.shape[0]
    head_count = width_q // head_size
    cache_dev = cache_keys.shape[0]
    pre_len = cache_keys.shape[1]
    req_grp = request_lengths.shape[1]
    lengths = request_lengths[0]
    req_ends = jnp.cumsum(lengths)
    starts = req_ends - lengths
    places = jnp.arange(tok_grp, dtype=jnp.int32)
    member = (places[:, None] >= starts[None, :]) & (places[:, None] < req_ends[None, :])
    request_idx = jnp.arange(req_grp, dtype=jnp.int32)
    segment = jnp.sum(jnp.where(member, request_idx[None, :], 0), axis=1)
    offset = places - jnp.sum(jnp.where(member, starts[None, :], 0), axis=1)
    block_rows = cache_block.reshape(req_count, req_grp)
    my_blocks = lax.dynamic_index_in_dim(block_rows, group_idx, 0, keepdims=False)
    has_cache = my_blocks >= 0
    token_cached = jnp.sum(jnp.where(member & has_cache[None, :], 1, 0), axis=1) > 0
    position = (offset + jnp.where(token_cached, pre_len, 0)).astype(jnp.float32)
    need_blocks, need_requests = compact(block_rows, cache_dev)
    my_requests = lax.dynamic_index_in_dim(need_requests, group_idx, 0, keepdims=False)
    key_width = cache_keys.shape[2]
    both = jnp.concatenate([cache_keys, cache_values], axis=-1)
    both_t = both.transpose(1, 0, 2)
    gathered = exchange_cache(both_t, need_blocks.reshape(-1).astype(jnp.int32), req_count)
    gathered = gathered.transpose(1, 0, 2)
    slot_weights, gathered = lax.optimization_barrier((slot_weights, gathered))
    far_keys = gathered[..., :key_width]
    far_values = gathered[..., key_width:]
    query_n = prepare(query_in.reshape(tok_grp, head_count, head_size), query_gain, position)
    key_n = prepare(key_in.reshape(tok_grp, head_count, head_size), key_gain, position)
    keyset = jnp.concatenate(
        [key_n, far_keys.reshape(cache_dev * pre_len, head_count, head_size)], axis=0
    )
    valueset = jnp.concatenate(
        [
            value_in.reshape(tok_grp, head_count, head_size),
            far_values.reshape(cache_dev * pre_len, head_count, head_size),
        ],
        axis=0,
    )
    key_request = jnp.concatenate([segment, jnp.repeat(my_requests, pre_len)])
    allowed = segment[:, None] == key_request[None, :]
    scores = jnp.einsum("qhd,khd->hqk", query_n, keyset, preferred_element_type=jnp.float32) * (
        1.0 / math.sqrt(head_size)
    )
    scores = jnp.where(allowed[None], scores, -1e30)
    peak = jnp.max(scores, axis=-1, keepdims=True)
    expos = jnp.exp(scores - peak)
    weights = (expos / jnp.sum(expos, axis=-1, keepdims=True)).astype(jnp.bfloat16)
    attended = jnp.einsum("hqk,khd->qhd", weights, valueset, preferred_element_type=jnp.float32)
    attended = attended.astype(jnp.bfloat16).reshape(tok_grp, width_q)
    attn_out = lax.psum_scatter(
        jnp.dot(attended, out_proj, preferred_element_type=jnp.float32),
        "exp",
        scatter_dimension=0,
        tiled=True,
    )
    residual = hidden_in.astype(jnp.float32) + attn_out
    normed = (
        residual
        * lax.rsqrt(jnp.mean(residual * residual, axis=-1, keepdims=True) + 1e-06)
        * norm_gain
    ).astype(jnp.bfloat16)
    topk_count = expert_ids.shape[1]
    slot_total = old_slots.shape[0]
    slots_here = slot_weights.shape[0]
    capacity = max(2, tok_dev * topk_count * 5 // (4 * slot_total))
    slot_range = jnp.arange(slot_total, dtype=jnp.int32)
    slot_of = jnp.sum(
        jnp.where(old_slots[None, :] == slot_range[:, None], slot_range[None, :], 0), axis=1
    )
    flat_ids = expert_ids.reshape(-1)
    onehot = flat_ids[:, None] == slot_range[None, :]
    row_slot = jnp.sum(jnp.where(onehot, slot_of[None, :], 0), axis=1)
    before = jnp.cumsum(onehot.astype(jnp.int32), axis=0) - onehot.astype(jnp.int32)
    row_rank = jnp.sum(jnp.where(onehot, before, 0), axis=1)
    target = row_slot * capacity + row_rank
    exp_idx = lax.axis_index("exp")
    pair_bit = exp_idx % 2
    pair_count = exp_count // 2
    own_part = lax.dynamic_index_in_dim(slot_weights, pair_bit, 0, keepdims=False)
    stacked_rows = slot_weights.shape[1] * slot_weights.shape[2]
    piece_rows = stacked_rows // req_count

    def spread_slot(weights, c):
        return lax.all_to_all(
            weights[c].reshape(req_count, piece_rows, slot_weights.shape[3]),
            "req",
            split_axis=0,
            concat_axis=0,
            tiled=True,
        )

    first_spread = spread_slot(slot_weights, 0)
    late_weights, first_spread = lax.optimization_barrier((slot_weights, first_spread))
    spread = [first_spread] + [spread_slot(late_weights, c) for c in range(1, slots_here)]
    swap_weights, spread = lax.optimization_barrier((slot_weights, spread))
    give_part = lax.dynamic_index_in_dim(swap_weights, 1 - pair_bit, 0, keepdims=False)
    swap = [(e, e ^ 1) for e in range(exp_count)]
    got_part = lax.ppermute(give_part, "exp", perm=swap)
    lanes = 128
    tile_rows = capacity * model_width // lanes

    def as_tiles(rows):
        return rows.reshape(req_count * exp_count, tile_rows, lanes)

    def as_rows(tiles):
        return tiles.reshape(req_count * exp_count * capacity, model_width)

    tile_high = model_width // lanes
    normed_tiles = normed.reshape(tok_dev, tile_high, lanes)
    row_token = jnp.arange(tok_dev * topk_count, dtype=jnp.int32) // topk_count
    source_token = jnp.zeros((slot_total * capacity,), jnp.int32).at[target].set(row_token)
    filled = jnp.zeros((slot_total * capacity,), jnp.bool_).at[target].set(True)
    per_req = slots_here * capacity
    copy_token = jnp.broadcast_to(
        source_token.reshape(req_count, 1, per_req), (req_count, pair_count, per_req)
    )
    copy_filled = jnp.broadcast_to(
        filled.reshape(req_count, 1, per_req), (req_count, pair_count, per_req)
    )
    copies = jnp.where(
        copy_filled[..., None, None], normed_tiles[copy_token], jnp.bfloat16(0)
    )
    copies = copies.reshape(req_count * exp_count, tile_rows, lanes)
    inbox = lax.all_to_all(copies, ("req", "exp"), split_axis=0, concat_axis=0, tiled=True)
    in_rows = as_rows(inbox)
    halves = []
    for part in (own_part, got_part):
        gate_act = jnp.dot(in_rows, part[0], preferred_element_type=jnp.float32)
        up_act = jnp.dot(in_rows, part[1], preferred_element_type=jnp.float32)
        hidden = (jax.nn.silu(gate_act) * up_act).astype(jnp.bfloat16)
        piece = lax.dot_general(
            hidden, part[2], (((1,), (1,)), ((), ())), preferred_element_type=jnp.float32
        )
        halves.append(piece.astype(jnp.bfloat16).astype(jnp.float32))
    partial_value = as_tiles((halves[0] + halves[1]).astype(jnp.bfloat16))
    returned = lax.all_to_all(
        partial_value, ("req", "exp"), split_axis=0, concat_axis=0, tiled=True
    ).reshape(req_count * exp_count * capacity, tile_high, lanes)
    dest_req = row_slot // slots_here
    dest_pos = row_slot % slots_here
    result_rows = None
    for pair_num in range(pair_count):
        where_from = (dest_req * exp_count + pair_num * slots_here + dest_pos) * capacity + row_rank
        one = jnp.take(returned, where_from, axis=0).astype(jnp.float32)
        result_rows = one if result_rows is None else result_rows + one
    mixture = jnp.sum(
        result_rows.reshape(tok_dev, topk_count, tile_high, lanes)
        * gate_values[:, :, None, None],
        axis=1,
    )
    residual_tiles = residual.reshape(tok_dev, tile_high, lanes)
    layer_out = (residual_tiles + mixture).astype(jnp.bfloat16).reshape(tok_dev, model_width)
    spread_slots = jnp.stack(spread, axis=1).reshape(
        slot_total, piece_rows, slot_weights.shape[3]
    )
    replica_onehot = new_replicas[:, None] == slot_range[None, :]
    source_slot = jnp.sum(jnp.where(replica_onehot, slot_of[None, :], 0), axis=1)
    chosen_pieces = jnp.take(spread_slots, source_slot, axis=0)
    replica_weights = lax.all_to_all(chosen_pieces, "req", split_axis=0, concat_axis=0, tiled=True)
    replica_weights = replica_weights.reshape((1,) + slot_weights.shape[1:])
    return (layer_out, replica_weights)


def solution(mesh):
    in_specs = (
        P(("req", "exp"), None),
        P("req", "exp"),
        P("req", "exp"),
        P("req", "exp"),
        P(),
        P(),
        P("req", None, "exp"),
        P("req", None, "exp"),
        P(),
        P("req", None),
        P("exp", None),
        P(),
        P(("req", "exp"), None),
        P(("req", "exp"), None),
        P(),
        P(),
        P("req", None, None, "exp"),
    )
    out_specs = (P(("req", "exp"), None), P("req", None, None, "exp"))
    return jax.shard_map(body, mesh=mesh, in_specs=in_specs, out_specs=out_specs, check_vma=False)
```

```python
import functools
import math

import jax
import jax.numpy as jnp
from jax import lax
from jax.experimental import pallas as pl
from jax.experimental.pallas import tpu as pltpu
from jax.sharding import PartitionSpec as P

MESH = pl.DeviceIdType.MESH


def cache_kernel(n, need_ref, both_ref, out_ref, stage, send_buf, land, sems):
    me = lax.axis_index("req")
    ex = lax.axis_index("exp")

    def first_copy(k, peer):
        return pltpu.make_async_remote_copy(
            src_ref=both_ref.at[peer],
            dst_ref=stage.at[me],
            send_sem=sems.at[0, k],
            recv_sem=sems.at[1, k],
            device_id=(peer, ex),
            device_id_type=MESH,
        )

    def second_copy(k, peer):
        return pltpu.make_async_remote_copy(
            src_ref=send_buf.at[k],
            dst_ref=land.at[me],
            send_sem=sems.at[2, k],
            recv_sem=sems.at[3, k],
            device_id=(peer, ex),
            device_id_type=MESH,
        )

    def send_first(k, carry):
        first_copy(k, lax.rem(me + k, n)).start()
        return carry

    lax.fori_loop(1, n, send_first, 0)
    stage[me] = both_ref[me]

    def wait_first(k, carry):
        source = lax.rem(me + n - k, n)
        pltpu.make_async_remote_copy(
            src_ref=both_ref.at[me],
            dst_ref=stage.at[source],
            send_sem=sems.at[0, k],
            recv_sem=sems.at[1, k],
            device_id=(source, ex),
            device_id_type=MESH,
        ).wait_recv()
        return carry

    lax.fori_loop(1, n, wait_first, 0)
    rows = lax.broadcasted_iota(jnp.int32, both_ref.shape[1:], 0)

    def pieces_for(dest):
        picked = []
        for c in range(2):
            block = need_ref[dest * 2 + c]
            slab = stage[block // 2].astype(jnp.float32)
            one = jnp.where(block % 2 == 0, slab[0:1], slab[1:2])
            picked.append(jnp.broadcast_to(one, slab.shape))
        return jnp.where(rows == 0, picked[0], picked[1]).astype(land.dtype)

    def send_second(k, carry):
        dest = lax.rem(me + k, n)
        send_buf[k] = pieces_for(dest)
        second_copy(k, dest).start()
        return carry

    lax.fori_loop(1, n, send_second, 0)
    land[me] = pieces_for(me)

    def wait_second(k, carry):
        source = lax.rem(me + n - k, n)
        pltpu.make_async_remote_copy(
            src_ref=send_buf.at[k],
            dst_ref=land.at[source],
            send_sem=sems.at[2, k],
            recv_sem=sems.at[3, k],
            device_id=(source, ex),
            device_id_type=MESH,
        ).wait_recv()
        first_copy(k, lax.rem(me + k, n)).wait_send()
        second_copy(k, lax.rem(me + k, n)).wait_send()
        return carry

    lax.fori_loop(1, n, wait_second, 0)
    out_ref[...] = land[...]


def exchange_cache(both_t, need_flat, n):
    shape = both_t.shape
    return pl.pallas_call(
        functools.partial(cache_kernel, n),
        out_shape=jax.ShapeDtypeStruct(shape, both_t.dtype),
        in_specs=[
            pl.BlockSpec(memory_space=pltpu.SMEM),
            pl.BlockSpec(memory_space=pltpu.VMEM),
        ],
        out_specs=pl.BlockSpec(memory_space=pltpu.VMEM),
        scratch_shapes=[
            pltpu.VMEM(shape, both_t.dtype),
            pltpu.VMEM(shape, both_t.dtype),
            pltpu.VMEM(shape, both_t.dtype),
            pltpu.SemaphoreType.DMA((4, n)),
        ],
        compiler_params=pltpu.CompilerParams(has_side_effects=True),
    )(need_flat, both_t)


def prepare(values, gain, position):
    vector = values.astype(jnp.float32)
    scaled = vector * lax.rsqrt(jnp.mean(vector * vector, axis=-1, keepdims=True) + 1e-06) * gain
    half_size = scaled.shape[-1] // 2
    frequency = 10000.0 ** (-(jnp.arange(half_size, dtype=jnp.float32) * 2.0 / scaled.shape[-1]))
    angles = position[:, None] * frequency[None, :]
    cosine = jnp.cos(angles)[:, None, :]
    sine_part = jnp.sin(angles)[:, None, :]
    lower_half = scaled[..., :half_size]
    upper_half = scaled[..., half_size:]
    rotated = jnp.concatenate(
        [
            lower_half * cosine - upper_half * sine_part,
            upper_half * cosine + lower_half * sine_part,
        ],
        axis=-1,
    )
    return rotated.astype(jnp.bfloat16)


def compact(block_rows, slots_wanted):
    live = block_rows >= 0
    ranks = jnp.cumsum(live.astype(jnp.int32), axis=1) - 1
    request_idx = jnp.arange(block_rows.shape[1], dtype=jnp.int32)[None, :]
    chosen_blocks = []
    chosen_requests = []
    for slot_num in range(slots_wanted):
        picked = live & (ranks == slot_num)
        chosen_blocks.append(jnp.sum(jnp.where(picked, block_rows, 0), axis=1))
        chosen_requests.append(jnp.sum(jnp.where(picked, request_idx, 0), axis=1))
    return (jnp.stack(chosen_blocks, axis=1), jnp.stack(chosen_requests, axis=1))


def body(
    hidden_in,
    query_in,
    key_in,
    value_in,
    query_gain,
    key_gain,
    cache_keys,
    cache_values,
    cache_block,
    request_lengths,
    out_proj,
    norm_gain,
    expert_ids,
    gate_values,
    old_slots,
    new_replicas,
    slot_weights,
):
    req_count = lax.axis_size("req")
    exp_count = lax.axis_size("exp")
    group_idx = lax.axis_index("req")
    tok_grp, width_q = query_in.shape
    tok_dev, model_width = hidden_in.shape
    head_size = query_gain.shape[0]
    head_count = width_q // head_size
    cache_dev = cache_keys.shape[0]
    pre_len = cache_keys.shape[1]
    req_grp = request_lengths.shape[1]
    lengths = request_lengths[0]
    req_ends = jnp.cumsum(lengths)
    starts = req_ends - lengths
    places = jnp.arange(tok_grp, dtype=jnp.int32)
    member = (places[:, None] >= starts[None, :]) & (places[:, None] < req_ends[None, :])
    request_idx = jnp.arange(req_grp, dtype=jnp.int32)
    segment = jnp.sum(jnp.where(member, request_idx[None, :], 0), axis=1)
    offset = places - jnp.sum(jnp.where(member, starts[None, :], 0), axis=1)
    block_rows = cache_block.reshape(req_count, req_grp)
    my_blocks = lax.dynamic_index_in_dim(block_rows, group_idx, 0, keepdims=False)
    has_cache = my_blocks >= 0
    token_cached = jnp.sum(jnp.where(member & has_cache[None, :], 1, 0), axis=1) > 0
    position = (offset + jnp.where(token_cached, pre_len, 0)).astype(jnp.float32)
    need_blocks, need_requests = compact(block_rows, cache_dev)
    my_requests = lax.dynamic_index_in_dim(need_requests, group_idx, 0, keepdims=False)
    key_width = cache_keys.shape[2]
    both = jnp.concatenate([cache_keys, cache_values], axis=-1)
    both_t = both.transpose(1, 0, 2)
    gathered = exchange_cache(both_t, need_blocks.reshape(-1).astype(jnp.int32), req_count)
    gathered = gathered.transpose(1, 0, 2)
    slot_weights, gathered = lax.optimization_barrier((slot_weights, gathered))
    far_keys = gathered[..., :key_width]
    far_values = gathered[..., key_width:]
    query_n = prepare(query_in.reshape(tok_grp, head_count, head_size), query_gain, position)
    key_n = prepare(key_in.reshape(tok_grp, head_count, head_size), key_gain, position)
    keyset = jnp.concatenate(
        [key_n, far_keys.reshape(cache_dev * pre_len, head_count, head_size)], axis=0
    )
    valueset = jnp.concatenate(
        [
            value_in.reshape(tok_grp, head_count, head_size),
            far_values.reshape(cache_dev * pre_len, head_count, head_size),
        ],
        axis=0,
    )
    key_request = jnp.concatenate([segment, jnp.repeat(my_requests, pre_len)])
    allowed = segment[:, None] == key_request[None, :]
    scores = jnp.einsum("qhd,khd->hqk", query_n, keyset, preferred_element_type=jnp.float32) * (
        1.0 / math.sqrt(head_size)
    )
    scores = jnp.where(allowed[None], scores, -1e30)
    peak = jnp.max(scores, axis=-1, keepdims=True)
    expos = jnp.exp(scores - peak)
    weights = (expos / jnp.sum(expos, axis=-1, keepdims=True)).astype(jnp.bfloat16)
    attended = jnp.einsum("hqk,khd->qhd", weights, valueset, preferred_element_type=jnp.float32)
    attended = attended.astype(jnp.bfloat16).reshape(tok_grp, width_q)
    attn_out = lax.psum_scatter(
        jnp.dot(attended, out_proj, preferred_element_type=jnp.float32),
        "exp",
        scatter_dimension=0,
        tiled=True,
    )
    residual = hidden_in.astype(jnp.float32) + attn_out
    normed = (
        residual
        * lax.rsqrt(jnp.mean(residual * residual, axis=-1, keepdims=True) + 1e-06)
        * norm_gain
    ).astype(jnp.bfloat16)
    topk_count = expert_ids.shape[1]
    slot_total = old_slots.shape[0]
    slots_here = slot_weights.shape[0]
    capacity = max(2, tok_dev * topk_count * 5 // (4 * slot_total))
    slot_range = jnp.arange(slot_total, dtype=jnp.int32)
    slot_of = jnp.sum(
        jnp.where(old_slots[None, :] == slot_range[:, None], slot_range[None, :], 0), axis=1
    )
    flat_ids = expert_ids.reshape(-1)
    onehot = flat_ids[:, None] == slot_range[None, :]
    row_slot = jnp.sum(jnp.where(onehot, slot_of[None, :], 0), axis=1)
    before = jnp.cumsum(onehot.astype(jnp.int32), axis=0) - onehot.astype(jnp.int32)
    row_rank = jnp.sum(jnp.where(onehot, before, 0), axis=1)
    target = row_slot * capacity + row_rank
    exp_idx = lax.axis_index("exp")
    pair_bit = exp_idx % 2
    pair_count = exp_count // 2
    own_part = lax.dynamic_index_in_dim(slot_weights, pair_bit, 0, keepdims=False)
    give_part = lax.dynamic_index_in_dim(slot_weights, 1 - pair_bit, 0, keepdims=False)
    swap = [(e, e ^ 1) for e in range(exp_count)]
    got_part = lax.ppermute(give_part, "exp", perm=swap)
    lanes = 128
    tile_rows = capacity * model_width // lanes

    def as_tiles(rows):
        return rows.reshape(req_count * exp_count, tile_rows, lanes)

    def as_rows(tiles):
        return tiles.reshape(req_count * exp_count * capacity, model_width)

    tile_high = model_width // lanes
    normed_tiles = normed.reshape(tok_dev, tile_high, lanes)
    row_token = jnp.arange(tok_dev * topk_count, dtype=jnp.int32) // topk_count
    source_token = jnp.zeros((slot_total * capacity,), jnp.int32).at[target].set(row_token)
    filled = jnp.zeros((slot_total * capacity,), jnp.bool_).at[target].set(True)
    per_req = slots_here * capacity
    copy_token = jnp.broadcast_to(
        source_token.reshape(req_count, 1, per_req), (req_count, pair_count, per_req)
    )
    copy_filled = jnp.broadcast_to(
        filled.reshape(req_count, 1, per_req), (req_count, pair_count, per_req)
    )
    copies = jnp.where(
        copy_filled[..., None, None], normed_tiles[copy_token], jnp.bfloat16(0)
    )
    copies = copies.reshape(req_count * exp_count, tile_rows, lanes)
    inbox = lax.all_to_all(copies, ("req", "exp"), split_axis=0, concat_axis=0, tiled=True)
    in_rows = as_rows(inbox)
    halves = []
    for part in (own_part, got_part):
        gate_act = jnp.dot(in_rows, part[0], preferred_element_type=jnp.float32)
        up_act = jnp.dot(in_rows, part[1], preferred_element_type=jnp.float32)
        hidden = (jax.nn.silu(gate_act) * up_act).astype(jnp.bfloat16)
        piece = lax.dot_general(
            hidden, part[2], (((1,), (1,)), ((), ())), preferred_element_type=jnp.float32
        )
        halves.append(piece.astype(jnp.bfloat16).astype(jnp.float32))
    partial_value = as_tiles((halves[0] + halves[1]).astype(jnp.bfloat16))
    returned = lax.all_to_all(
        partial_value, ("req", "exp"), split_axis=0, concat_axis=0, tiled=True
    ).reshape(req_count * exp_count * capacity, tile_high, lanes)
    dest_req = row_slot // slots_here
    dest_pos = row_slot % slots_here
    result_rows = None
    for pair_num in range(pair_count):
        where_from = (dest_req * exp_count + pair_num * slots_here + dest_pos) * capacity + row_rank
        one = jnp.take(returned, where_from, axis=0).astype(jnp.float32)
        result_rows = one if result_rows is None else result_rows + one
    mixture = jnp.sum(
        result_rows.reshape(tok_dev, topk_count, tile_high, lanes)
        * gate_values[:, :, None, None],
        axis=1,
    )
    residual_tiles = residual.reshape(tok_dev, tile_high, lanes)
    layer_out = (residual_tiles + mixture).astype(jnp.bfloat16).reshape(tok_dev, model_width)
    stacked_rows = slot_weights.shape[1] * slot_weights.shape[2]
    piece_rows = stacked_rows // req_count
    spread = [
        lax.all_to_all(
            slot_weights[c].reshape(req_count, piece_rows, slot_weights.shape[3]),
            "req",
            split_axis=0,
            concat_axis=0,
            tiled=True,
        )
        for c in range(slots_here)
    ]
    spread_slots = jnp.stack(spread, axis=1).reshape(
        slot_total, piece_rows, slot_weights.shape[3]
    )
    replica_onehot = new_replicas[:, None] == slot_range[None, :]
    source_slot = jnp.sum(jnp.where(replica_onehot, slot_of[None, :], 0), axis=1)
    chosen_pieces = jnp.take(spread_slots, source_slot, axis=0)
    replica_weights = lax.all_to_all(chosen_pieces, "req", split_axis=0, concat_axis=0, tiled=True)
    replica_weights = replica_weights.reshape((1,) + slot_weights.shape[1:])
    return (layer_out, replica_weights)


def solution(mesh):
    in_specs = (
        P(("req", "exp"), None),
        P("req", "exp"),
        P("req", "exp"),
        P("req", "exp"),
        P(),
        P(),
        P("req", None, "exp"),
        P("req", None, "exp"),
        P(),
        P("req", None),
        P("exp", None),
        P(),
        P(("req", "exp"), None),
        P(("req", "exp"), None),
        P(),
        P(),
        P("req", None, None, "exp"),
    )
    out_specs = (P(("req", "exp"), None), P("req", None, None, "exp"))
    return jax.shard_map(body, mesh=mesh, in_specs=in_specs, out_specs=out_specs, check_vma=False)
```

```python
import functools
import math

import jax
import jax.numpy as jnp
from jax import lax
from jax.experimental import pallas as pl
from jax.experimental.pallas import tpu as pltpu
from jax.sharding import PartitionSpec as P

MESH = pl.DeviceIdType.MESH


def cache_kernel(n, need_ref, both_ref, out_ref, stage, send_buf, land, sems):
    me = lax.axis_index("req")
    ex = lax.axis_index("exp")
    barrier = pltpu.get_barrier_semaphore()

    def greet(k, carry):
        peer = lax.rem(me + k, n)
        pl.semaphore_signal(barrier, inc=1, device_id=(peer, ex), device_id_type=MESH)
        return carry

    lax.fori_loop(1, n, greet, 0)
    pl.semaphore_wait(barrier, n - 1)

    def first_copy(k, peer):
        return pltpu.make_async_remote_copy(
            src_ref=both_ref.at[peer],
            dst_ref=stage.at[me],
            send_sem=sems.at[0, k],
            recv_sem=sems.at[1, k],
            device_id=(peer, ex),
            device_id_type=MESH,
        )

    def second_copy(k, peer):
        return pltpu.make_async_remote_copy(
            src_ref=send_buf.at[k],
            dst_ref=land.at[me],
            send_sem=sems.at[2, k],
            recv_sem=sems.at[3, k],
            device_id=(peer, ex),
            device_id_type=MESH,
        )

    def send_first(k, carry):
        first_copy(k, lax.rem(me + k, n)).start()
        return carry

    lax.fori_loop(1, n, send_first, 0)
    stage[me] = both_ref[me]

    def wait_first(k, carry):
        source = lax.rem(me + n - k, n)
        pltpu.make_async_remote_copy(
            src_ref=both_ref.at[me],
            dst_ref=stage.at[source],
            send_sem=sems.at[0, k],
            recv_sem=sems.at[1, k],
            device_id=(source, ex),
            device_id_type=MESH,
        ).wait_recv()
        return carry

    lax.fori_loop(1, n, wait_first, 0)
    rows = lax.broadcasted_iota(jnp.int32, both_ref.shape[1:], 0)

    def pieces_for(dest):
        picked = []
        for c in range(2):
            block = need_ref[dest * 2 + c]
            slab = stage[block // 2].astype(jnp.float32)
            one = jnp.where(block % 2 == 0, slab[0:1], slab[1:2])
            picked.append(jnp.broadcast_to(one, slab.shape))
        return jnp.where(rows == 0, picked[0], picked[1]).astype(land.dtype)

    def send_second(k, carry):
        dest = lax.rem(me + k, n)
        send_buf[k] = pieces_for(dest)
        second_copy(k, dest).start()
        return carry

    lax.fori_loop(1, n, send_second, 0)
    land[me] = pieces_for(me)

    def wait_second(k, carry):
        source = lax.rem(me + n - k, n)
        pltpu.make_async_remote_copy(
            src_ref=send_buf.at[k],
            dst_ref=land.at[source],
            send_sem=sems.at[2, k],
            recv_sem=sems.at[3, k],
            device_id=(source, ex),
            device_id_type=MESH,
        ).wait_recv()
        first_copy(k, lax.rem(me + k, n)).wait_send()
        second_copy(k, lax.rem(me + k, n)).wait_send()
        return carry

    lax.fori_loop(1, n, wait_second, 0)
    out_ref[...] = land[...]


def exchange_cache(both_t, need_flat, n):
    shape = both_t.shape
    return pl.pallas_call(
        functools.partial(cache_kernel, n),
        out_shape=jax.ShapeDtypeStruct(shape, both_t.dtype),
        in_specs=[
            pl.BlockSpec(memory_space=pltpu.SMEM),
            pl.BlockSpec(memory_space=pltpu.VMEM),
        ],
        out_specs=pl.BlockSpec(memory_space=pltpu.VMEM),
        scratch_shapes=[
            pltpu.VMEM(shape, both_t.dtype),
            pltpu.VMEM(shape, both_t.dtype),
            pltpu.VMEM(shape, both_t.dtype),
            pltpu.SemaphoreType.DMA((4, n)),
        ],
        compiler_params=pltpu.CompilerParams(collective_id=0, has_side_effects=True),
    )(need_flat, both_t)


def prepare(values, gain, position):
    vector = values.astype(jnp.float32)
    scaled = vector * lax.rsqrt(jnp.mean(vector * vector, axis=-1, keepdims=True) + 1e-06) * gain
    half_size = scaled.shape[-1] // 2
    frequency = 10000.0 ** (-(jnp.arange(half_size, dtype=jnp.float32) * 2.0 / scaled.shape[-1]))
    angles = position[:, None] * frequency[None, :]
    cosine = jnp.cos(angles)[:, None, :]
    sine_part = jnp.sin(angles)[:, None, :]
    lower_half = scaled[..., :half_size]
    upper_half = scaled[..., half_size:]
    rotated = jnp.concatenate(
        [
            lower_half * cosine - upper_half * sine_part,
            upper_half * cosine + lower_half * sine_part,
        ],
        axis=-1,
    )
    return rotated.astype(jnp.bfloat16)


def compact(block_rows, slots_wanted):
    live = block_rows >= 0
    ranks = jnp.cumsum(live.astype(jnp.int32), axis=1) - 1
    request_idx = jnp.arange(block_rows.shape[1], dtype=jnp.int32)[None, :]
    chosen_blocks = []
    chosen_requests = []
    for slot_num in range(slots_wanted):
        picked = live & (ranks == slot_num)
        chosen_blocks.append(jnp.sum(jnp.where(picked, block_rows, 0), axis=1))
        chosen_requests.append(jnp.sum(jnp.where(picked, request_idx, 0), axis=1))
    return (jnp.stack(chosen_blocks, axis=1), jnp.stack(chosen_requests, axis=1))


def body(
    hidden_in,
    query_in,
    key_in,
    value_in,
    query_gain,
    key_gain,
    cache_keys,
    cache_values,
    cache_block,
    request_lengths,
    out_proj,
    norm_gain,
    expert_ids,
    gate_values,
    old_slots,
    new_replicas,
    slot_weights,
):
    req_count = lax.axis_size("req")
    exp_count = lax.axis_size("exp")
    group_idx = lax.axis_index("req")
    tok_grp, width_q = query_in.shape
    tok_dev, model_width = hidden_in.shape
    head_size = query_gain.shape[0]
    head_count = width_q // head_size
    cache_dev = cache_keys.shape[0]
    pre_len = cache_keys.shape[1]
    req_grp = request_lengths.shape[1]
    lengths = request_lengths[0]
    req_ends = jnp.cumsum(lengths)
    starts = req_ends - lengths
    places = jnp.arange(tok_grp, dtype=jnp.int32)
    member = (places[:, None] >= starts[None, :]) & (places[:, None] < req_ends[None, :])
    request_idx = jnp.arange(req_grp, dtype=jnp.int32)
    segment = jnp.sum(jnp.where(member, request_idx[None, :], 0), axis=1)
    offset = places - jnp.sum(jnp.where(member, starts[None, :], 0), axis=1)
    block_rows = cache_block.reshape(req_count, req_grp)
    my_blocks = lax.dynamic_index_in_dim(block_rows, group_idx, 0, keepdims=False)
    has_cache = my_blocks >= 0
    token_cached = jnp.sum(jnp.where(member & has_cache[None, :], 1, 0), axis=1) > 0
    position = (offset + jnp.where(token_cached, pre_len, 0)).astype(jnp.float32)
    need_blocks, need_requests = compact(block_rows, cache_dev)
    my_requests = lax.dynamic_index_in_dim(need_requests, group_idx, 0, keepdims=False)
    key_width = cache_keys.shape[2]
    both = jnp.concatenate([cache_keys, cache_values], axis=-1)
    both_t = both.transpose(1, 0, 2)
    gathered = exchange_cache(both_t, need_blocks.reshape(-1).astype(jnp.int32), req_count)
    gathered = gathered.transpose(1, 0, 2)
    slot_weights, gathered = lax.optimization_barrier((slot_weights, gathered))
    far_keys = gathered[..., :key_width]
    far_values = gathered[..., key_width:]
    query_n = prepare(query_in.reshape(tok_grp, head_count, head_size), query_gain, position)
    key_n = prepare(key_in.reshape(tok_grp, head_count, head_size), key_gain, position)
    keyset = jnp.concatenate(
        [key_n, far_keys.reshape(cache_dev * pre_len, head_count, head_size)], axis=0
    )
    valueset = jnp.concatenate(
        [
            value_in.reshape(tok_grp, head_count, head_size),
            far_values.reshape(cache_dev * pre_len, head_count, head_size),
        ],
        axis=0,
    )
    key_request = jnp.concatenate([segment, jnp.repeat(my_requests, pre_len)])
    allowed = segment[:, None] == key_request[None, :]
    scores = jnp.einsum("qhd,khd->hqk", query_n, keyset, preferred_element_type=jnp.float32) * (
        1.0 / math.sqrt(head_size)
    )
    scores = jnp.where(allowed[None], scores, -1e30)
    peak = jnp.max(scores, axis=-1, keepdims=True)
    expos = jnp.exp(scores - peak)
    weights = (expos / jnp.sum(expos, axis=-1, keepdims=True)).astype(jnp.bfloat16)
    attended = jnp.einsum("hqk,khd->qhd", weights, valueset, preferred_element_type=jnp.float32)
    attended = attended.astype(jnp.bfloat16).reshape(tok_grp, width_q)
    attn_out = lax.psum_scatter(
        jnp.dot(attended, out_proj, preferred_element_type=jnp.float32),
        "exp",
        scatter_dimension=0,
        tiled=True,
    )
    residual = hidden_in.astype(jnp.float32) + attn_out
    normed = (
        residual
        * lax.rsqrt(jnp.mean(residual * residual, axis=-1, keepdims=True) + 1e-06)
        * norm_gain
    ).astype(jnp.bfloat16)
    topk_count = expert_ids.shape[1]
    slot_total = old_slots.shape[0]
    slots_here = slot_weights.shape[0]
    capacity = max(2, tok_dev * topk_count * 5 // (4 * slot_total))
    slot_range = jnp.arange(slot_total, dtype=jnp.int32)
    slot_of = jnp.sum(
        jnp.where(old_slots[None, :] == slot_range[:, None], slot_range[None, :], 0), axis=1
    )
    flat_ids = expert_ids.reshape(-1)
    onehot = flat_ids[:, None] == slot_range[None, :]
    row_slot = jnp.sum(jnp.where(onehot, slot_of[None, :], 0), axis=1)
    before = jnp.cumsum(onehot.astype(jnp.int32), axis=0) - onehot.astype(jnp.int32)
    row_rank = jnp.sum(jnp.where(onehot, before, 0), axis=1)
    target = row_slot * capacity + row_rank
    exp_idx = lax.axis_index("exp")
    pair_bit = exp_idx % 2
    pair_count = exp_count // 2
    own_part = lax.dynamic_index_in_dim(slot_weights, pair_bit, 0, keepdims=False)
    give_part = lax.dynamic_index_in_dim(slot_weights, 1 - pair_bit, 0, keepdims=False)
    swap = [(e, e ^ 1) for e in range(exp_count)]
    got_part = lax.ppermute(give_part, "exp", perm=swap)
    lanes = 128
    tile_rows = capacity * model_width // lanes

    def as_tiles(rows):
        return rows.reshape(req_count * exp_count, tile_rows, lanes)

    def as_rows(tiles):
        return tiles.reshape(req_count * exp_count * capacity, model_width)

    tile_high = model_width // lanes
    normed_tiles = normed.reshape(tok_dev, tile_high, lanes)
    row_token = jnp.arange(tok_dev * topk_count, dtype=jnp.int32) // topk_count
    source_token = jnp.zeros((slot_total * capacity,), jnp.int32).at[target].set(row_token)
    filled = jnp.zeros((slot_total * capacity,), jnp.bool_).at[target].set(True)
    per_req = slots_here * capacity
    copy_token = jnp.broadcast_to(
        source_token.reshape(req_count, 1, per_req), (req_count, pair_count, per_req)
    )
    copy_filled = jnp.broadcast_to(
        filled.reshape(req_count, 1, per_req), (req_count, pair_count, per_req)
    )
    copies = jnp.where(
        copy_filled[..., None, None], normed_tiles[copy_token], jnp.bfloat16(0)
    )
    copies = copies.reshape(req_count * exp_count, tile_rows, lanes)
    inbox = lax.all_to_all(copies, ("req", "exp"), split_axis=0, concat_axis=0, tiled=True)
    in_rows = inbox.reshape(req_count * exp_count * capacity, tile_high, lanes)
    tiled_dims = (((1, 2), (0, 1)), ((), ()))
    halves = []
    for part in (own_part, got_part):
        gate_act = lax.dot_general(
            in_rows, part[0].reshape(tile_high, lanes, -1), tiled_dims,
            preferred_element_type=jnp.float32,
        )
        up_act = lax.dot_general(
            in_rows, part[1].reshape(tile_high, lanes, -1), tiled_dims,
            preferred_element_type=jnp.float32,
        )
        hidden = (jax.nn.silu(gate_act) * up_act).astype(jnp.bfloat16)
        piece = lax.dot_general(
            hidden, part[2], (((1,), (1,)), ((), ())), preferred_element_type=jnp.float32
        )
        halves.append(piece.astype(jnp.bfloat16).astype(jnp.float32))
    partial_value = as_tiles((halves[0] + halves[1]).astype(jnp.bfloat16))
    returned = lax.all_to_all(
        partial_value, ("req", "exp"), split_axis=0, concat_axis=0, tiled=True
    ).reshape(req_count * exp_count * capacity, tile_high, lanes)
    dest_req = row_slot // slots_here
    dest_pos = row_slot % slots_here
    result_rows = None
    for pair_num in range(pair_count):
        where_from = (dest_req * exp_count + pair_num * slots_here + dest_pos) * capacity + row_rank
        one = jnp.take(returned, where_from, axis=0).astype(jnp.float32)
        result_rows = one if result_rows is None else result_rows + one
    mixture = jnp.sum(
        result_rows.reshape(tok_dev, topk_count, tile_high, lanes)
        * gate_values[:, :, None, None],
        axis=1,
    )
    residual_tiles = residual.reshape(tok_dev, tile_high, lanes)
    layer_out = (residual_tiles + mixture).astype(jnp.bfloat16).reshape(tok_dev, model_width)
    stacked_rows = slot_weights.shape[1] * slot_weights.shape[2]
    piece_rows = stacked_rows // req_count
    spread = [
        lax.all_to_all(
            slot_weights[c].reshape(req_count, piece_rows, slot_weights.shape[3]),
            "req",
            split_axis=0,
            concat_axis=0,
            tiled=True,
        )
        for c in range(slots_here)
    ]
    spread_slots = jnp.stack(spread, axis=1).reshape(
        slot_total, piece_rows, slot_weights.shape[3]
    )
    replica_onehot = new_replicas[:, None] == slot_range[None, :]
    source_slot = jnp.sum(jnp.where(replica_onehot, slot_of[None, :], 0), axis=1)
    chosen_pieces = jnp.take(spread_slots, source_slot, axis=0)
    replica_weights = lax.all_to_all(chosen_pieces, "req", split_axis=0, concat_axis=0, tiled=True)
    replica_weights = replica_weights.reshape((1,) + slot_weights.shape[1:])
    return (layer_out, replica_weights)


def solution(mesh):
    in_specs = (
        P(("req", "exp"), None),
        P("req", "exp"),
        P("req", "exp"),
        P("req", "exp"),
        P(),
        P(),
        P("req", None, "exp"),
        P("req", None, "exp"),
        P(),
        P("req", None),
        P("exp", None),
        P(),
        P(("req", "exp"), None),
        P(("req", "exp"), None),
        P(),
        P(),
        P("req", None, None, "exp"),
    )
    out_specs = (P(("req", "exp"), None), P("req", None, None, "exp"))
    return jax.shard_map(body, mesh=mesh, in_specs=in_specs, out_specs=out_specs, check_vma=False)
```
